32 devices in a mesh: fsdp: 8 (over y, x, core), sp: 4 (over z).
Axes of the slice: x: 2, y: 2, z: 4, core: 2. Of those that a mesh axis runs over, the one named last changes fastest.
Arguments:
- inputs: bfloat16 [32, 1024, 768], P('fsdp', 'sp'), may hold values from -6 to 6
- global_pos: int32 [32, 4], P('fsdp'), may hold values from 0 to 1023, as said below
- w_local: bfloat16 [3, 768, 768], P(None, 'fsdp'), may hold values from -0.21875 to 0.21875
- w_global: bfloat16 [3, 768, 768], P(None, 'fsdp'), may hold values from -0.3125 to 0.3125
- w_out: bfloat16 [768, 768], P('fsdp'), may hold values from -2.5 to 2.5
- b_proj: bfloat16 [6, 768], P(None, 'fsdp'), may hold values from -3 to 3
- gains: bfloat16 [2, 768], P(None, 'fsdp'), may hold values from 0.5 to 1.5
- shifts: bfloat16 [2, 768], P(None, 'fsdp'), may hold values from -3 to 3
- w_in: bfloat16 [768, 3072], P('fsdp'), may hold values from -0.21875 to 0.21875
- c_in: bfloat16 [3072], P('fsdp'), may hold values from -3 to 3
- w_back: bfloat16 [3072, 768], P('fsdp'), may hold values from -0.109375 to 0.109375
- cotangent: bfloat16 [32, 1024, 768], P('fsdp', 'sp'), may hold values from -6 to 6
Outputs:
- output: bfloat16 [32, 1024, 768], P('fsdp', 'sp')
- grad_inputs: bfloat16 [32, 1024, 768], P('fsdp', 'sp')
- grad_w_local: float32 [3, 768, 768], P(None, 'fsdp')
- grad_w_global: float32 [3, 768, 768], P(None, 'fsdp')
- grad_w_out: float32 [768, 768], P('fsdp')
- grad_b_proj: float32 [6, 768], P(None, 'fsdp')
- grad_gains: float32 [2, 768], P(None, 'fsdp')
- grad_shifts: float32 [2, 768], P(None, 'fsdp')
- grad_w_in: float32 [768, 3072], P('fsdp')
- grad_c_in: float32 [3072], P('fsdp')
- grad_w_back: float32 [3072, 768], P('fsdp')
The draws below stay inside these ranges and needn't reach their ends.
Inputs may be any that keep to these rules, and one draw needn't show every extreme that they name: `global_pos`: in each sequence the 4 global positions are different; the first is 0 and the second is 1023.
All inputs are finite; a program needn't handle non-finite values.
Results may differ from the reference program's by a relative error of at most 0.017.
Values may be sent and summed in bfloat16 or wider, within the bound.
No kernel may reach another device: no remote copies, remote signals or barrier semaphores. Data moves between devices by JAX's collectives and lax.ppermute only.
A program may use at most 256 MiB of HBM per device.

```python
import jax
import jax.numpy as jnp
from jax import lax

D = 768
HEADS = 12
HEAD_DIM = 64
FF = 3072
WIN = 256
LEN = 1024
NG = 4
SEQS = 32


def draw_global_pos(key, part):
    seq_keys = jax.random.split(key, SEQS)

    def one_row(row_key):
        picked = jax.random.permutation(row_key, LEN - 2)[:NG - 2] + 1
        ends = jnp.array([0, LEN - 1], jnp.int32)
        return jnp.concatenate([ends, picked.astype(jnp.int32)])
    return jax.vmap(one_row)(seq_keys)


def raised(entries, key, source, target, blocks, factor):
    owner, partner = [(jnp.arange(entries.shape[position]) // (entries.shape[position] // blocks)).reshape([-1 if axis == position else 1 for axis in range(entries.ndim)]) for position in (source, target)]
    chosen = jax.random.permutation(key, blocks)[partner]
    strong = (owner == chosen) | (owner == (partner + blocks // 2) % blocks)
    return jnp.where(strong, factor * entries, entries)


def steps_of(key, extent, cuts, least, largest):
    level, own = 1.0, jax.random.fold_in(key, 6)
    for dim, blocks in cuts:
        steps = jnp.exp(jax.random.uniform(jax.random.fold_in(own, dim), (blocks,), jnp.float32, least / len(cuts), largest / len(cuts)))
        level = level * jnp.repeat(steps, extent[dim] // blocks).reshape([-1 if axis == dim else 1 for axis in range(len(extent))])
    return level


def bell_draw(own_key, extent, spread, most, shards=(), kind=jnp.bfloat16):
    entries = jax.random.normal(own_key, extent, jnp.float32) * spread
    if len(shards) > 0:
        entries = steps_of(own_key, extent, shards, -0.22, 0.18) * entries
    return jnp.clip(entries, min=-most, max=most).astype(kind)


def bell_draw_with(own_key, dims, width, reach, shards, heavy, kind=jnp.bfloat16):
    values = width * jax.random.normal(own_key, dims, jnp.float32)
    if shards:
        values = values * steps_of(own_key, dims, shards, -0.22, 0.18)
    return jnp.clip(raised(values, jax.random.fold_in(own_key, 3), *heavy), -reach, reach).astype(kind)


def setup_inputs(seed: int = 0) -> dict:
    key_of = jax.random.split(jax.random.key(seed), 13)
    inputs = bell_draw(key_of[0], (SEQS, LEN, D), 1.0, 6.0, ((0, 8), (1, 4)))
    global_pos = draw_global_pos(jax.random.fold_in(key_of[12], 71), 0)
    w_local = bell_draw(key_of[2], (3, D, D), D ** -0.5, 0.21875, ((1, 8),))
    w_global = bell_draw(key_of[3], (3, D, D), (D // 2) ** -0.5, 0.3125, ((1, 8),))
    w_out = bell_draw(key_of[4], (D, D), (max(D // 128, 1)) ** -0.5, 2.5, ((0, 8),))
    b_proj = bell_draw(key_of[5], (6, D), 0.5, 3.0, ((1, 8),))
    gains = jnp.clip(1.0 + 0.1 * jax.random.normal(key_of[6], (2, D), jnp.float32), 0.5, 1.5).astype(jnp.bfloat16)
    shifts = bell_draw(key_of[7], (2, D), 0.5, 3.0, ((1, 8),))
    w_in = bell_draw(key_of[8], (D, FF), D ** -0.5, 0.21875, ((0, 8),))
    c_in = bell_draw(key_of[9], (FF,), 0.5, 3.0, ((0, 8),))
    w_back = bell_draw(key_of[10], (FF, D), FF ** -0.5, 0.109375, ((0, 8),))
    cotangent = bell_draw_with(key_of[11], (SEQS, LEN, D), 1.0, 6.0, ((0, 8), (1, 4)), (0, 2, 8, 2.0))
    return dict(inputs=inputs, global_pos=global_pos, w_local=w_local, w_global=w_global, w_out=w_out, b_proj=b_proj, gains=gains, shifts=shifts, w_in=w_in, c_in=c_in, w_back=w_back, cotangent=cotangent)


HIGHEST = lax.Precision.HIGHEST
MASKED_SCORE = -1000000000.0
NORM_EPS = 1e-05

@jax.custom_vjp
def low(v):
    return lax.optimization_barrier(v.astype(jnp.bfloat16)).astype(jnp.float32)

@jax.custom_vjp
def low_back(v):
    return v

def low_keep(v):
    return (low(v), None)

def low_pass(kept, grad):
    return (grad,)

def back_keep(v):
    return (v, None)

def back_low(kept, grad):
    return (low(grad),)
low.defvjp(low_keep, low_pass)
low_back.defvjp(back_keep, back_low)

def matmul_high(left_side, right_side):
    return jnp.matmul(left_side, right_side, precision=HIGHEST)

def layer_norm(summed, gain_row, shift_row):
    center = summed - lax.optimization_barrier(jnp.mean(summed, axis=-1, keepdims=True))
    inverse = lax.rsqrt(lax.optimization_barrier(jnp.mean(center * center, axis=-1, keepdims=True)) + NORM_EPS)
    return center * inverse * gain_row + shift_row

def split_heads(matrix):
    return matrix.reshape(matrix.shape[0], HEADS, HEAD_DIM)

def one_sequence(sequence, positions, params):
    w_local, w_global, w_out, b_proj, gains, shifts, w_in, c_in, w_back = params
    length = sequence.shape[0]
    score_scale = HEAD_DIM ** (-0.5)
    queries = split_heads(low_back(low((matmul_high(sequence, w_local[0]) + b_proj[0]) * score_scale)))
    key_loc = split_heads(low_back(low(matmul_high(sequence, w_local[1]))))
    value_loc = split_heads(low_back(low(matmul_high(sequence, w_local[2]) + b_proj[1])))
    key_glob = split_heads(low_back(low(matmul_high(sequence, w_global[1]))))
    value_glob = split_heads(low_back(low(matmul_high(sequence, w_global[2]) + b_proj[3])))
    places = jnp.arange(length, dtype=jnp.int32)
    select = (positions[:, None] == places[None, :]).astype(jnp.float32)
    rows_glob = matmul_high(select, sequence)
    query_glob = split_heads(low_back(low((matmul_high(rows_glob, w_global[0]) + b_proj[2]) * score_scale)))
    is_glob = lax.optimization_barrier(jnp.sum(select, axis=0))
    in_band = jnp.abs(places[:, None] - places[None, :]) <= WIN
    allowed = in_band | (is_glob[None, :] > 0.5)
    scores = low_back(jnp.einsum('ihe,jhe->hij', queries, key_loc, precision=HIGHEST))
    probs = jax.nn.softmax(jnp.where(allowed[None], scores, MASKED_SCORE), axis=-1)
    context = jnp.einsum('hij,jhe->ihe', low(probs), value_loc, precision=HIGHEST)
    scores_glob = low_back(jnp.einsum('ghe,jhe->hgj', query_glob, key_glob, precision=HIGHEST))
    probs_glob = jax.nn.softmax(scores_glob, axis=-1)
    context_glob = jnp.einsum('hgj,jhe->ghe', low(probs_glob), value_glob, precision=HIGHEST)
    context = context * (1.0 - is_glob)[:, None, None] + jnp.einsum('gi,ghe->ihe', select, context_glob, precision=HIGHEST)
    merged = low_back(low(context.reshape(length, HEADS * HEAD_DIM)))
    attended = low_back(matmul_high(merged, w_out) + b_proj[4])
    first_norm = layer_norm(sequence + attended, gains[0], shifts[0])
    ffn_inner = low_back(matmul_high(low(first_norm), w_in) + c_in)
    active = low(jax.nn.gelu(ffn_inner, approximate=False))
    branch = low_back(matmul_high(active, w_back) + b_proj[5])
    return layer_norm(first_norm + branch, gains[1], shifts[1])

def reference(inputs, global_pos, w_local, w_global, w_out, b_proj, gains, shifts, w_in, c_in, w_back, cotangent):
    params = tuple((argument.astype(jnp.float32) for argument in (w_local, w_global, w_out, b_proj, gains, shifts, w_in, c_in, w_back)))

    def forward(tokens, weights):

        def per_sequence(seq_pair):
            return one_sequence(seq_pair[0], seq_pair[1], weights)
        return lax.map(jax.checkpoint(per_sequence), (tokens, global_pos))
    output, pull_back = jax.vjp(forward, inputs.astype(jnp.float32), params)
    grad_inputs, grad_params = pull_back(cotangent.astype(jnp.float32))
    return (output.astype(jnp.bfloat16), grad_inputs.astype(jnp.bfloat16), grad_params[0], grad_params[1], grad_params[2], grad_params[3], grad_params[4], grad_params[5], grad_params[6], grad_params[7], grad_params[8])
```

```python
import jax
import jax.numpy as jnp
from jax import lax
from jax.sharding import PartitionSpec as P

HEADS = 12
HEAD_DIM = 64
WIN = 256

HIGHEST = lax.Precision.HIGHEST
MASKED_SCORE = -1000000000.0
NORM_EPS = 1e-05
BF = jnp.bfloat16
F32 = jnp.float32


def normalize(summed):
    center = summed - jnp.mean(summed, axis=-1, keepdims=True)
    inverse = lax.rsqrt(jnp.mean(center * center, axis=-1, keepdims=True) + NORM_EPS)
    return (center * inverse, inverse)


def norm_back(scaled, normed, inverse):
    return inverse * (
        scaled
        - jnp.mean(scaled, axis=-1, keepdims=True)
        - normed * jnp.mean(scaled * normed, axis=-1, keepdims=True)
    )


def mm(a, b):
    return jnp.dot(a, b, preferred_element_type=F32)


def mm_nt(a, b):
    return lax.dot_general(a, b, (((1,), (1,)), ((), ())), preferred_element_type=F32)


def mm_tn(a, b):
    return lax.dot_general(a, b, (((0,), (0,)), ((), ())), preferred_element_type=F32)


def gelu_pair(inner):
    cdf = 0.5 * (1.0 + lax.erf(inner * (0.5**0.5)))
    pdf = jnp.exp(-0.5 * inner * inner) * 0.3989422804014327
    return (inner * cdf, cdf + inner * pdf)


def sequence_step(x, positions, upstream_low, weights):
    w_local, w_global, w_out, b_proj, gains, shifts, w_in, c_in, w_back = weights
    length, width = x.shape
    scale = HEAD_DIM ** (-0.5)
    bias = b_proj.astype(F32)
    gain = gains.astype(F32)
    shift = shifts.astype(F32)

    def heads(value):
        return value.reshape(value.shape[0], HEADS, HEAD_DIM)

    q = heads(((mm(x, w_local[0]) + bias[0]) * scale).astype(BF))
    k = heads(mm(x, w_local[1]).astype(BF))
    v = heads((mm(x, w_local[2]) + bias[1]).astype(BF))
    kg = heads(mm(x, w_global[1]).astype(BF))
    vg = heads((mm(x, w_global[2]) + bias[3]).astype(BF))
    places = jnp.arange(length, dtype=jnp.int32)
    select = positions[:, None] == places[None, :]
    select_low = select.astype(BF)
    select_full = select.astype(F32)
    is_glob = jnp.sum(select_full, axis=0)
    keep_local = 1.0 - is_glob
    rows_glob = mm(select_low, x).astype(BF)
    qg = heads(((mm(rows_glob, w_global[0]) + bias[2]) * scale).astype(BF))
    block = 256
    offsets = list(range(0, length, block))

    def block_scores(offset):
        qb = q[offset : offset + block]
        row_places = offset + jnp.arange(block, dtype=jnp.int32)
        in_band = jnp.abs(row_places[:, None] - places[None, :]) <= WIN
        allowed = in_band | (is_glob[None, :] > 0.5)
        raw = jnp.einsum("ihe,jhe->hij", qb, k, preferred_element_type=F32)
        return (qb, jnp.where(allowed[None], raw, MASKED_SCORE))

    kept = []
    contexts = []
    for offset in offsets:
        qb, masked = block_scores(offset)
        top = jnp.max(masked, axis=-1, keepdims=True)
        powers = jnp.exp(masked - top)
        total = jnp.sum(powers, axis=-1, keepdims=True)
        low = (powers / total).astype(BF)
        contexts.append(jnp.einsum("hij,jhe->ihe", low, v, preferred_element_type=F32))
        kept.append((top, total))
    context_loc = jnp.concatenate(contexts, axis=0)
    glob_scores = jnp.einsum("ghe,jhe->hgj", qg, kg, preferred_element_type=F32)
    glob_probs = jax.nn.softmax(glob_scores, axis=-1)
    glob_low = glob_probs.astype(BF)
    context_glob = jnp.einsum("hgj,jhe->ghe", glob_low, vg, preferred_element_type=F32)
    context = context_loc * keep_local[:, None, None] + jnp.einsum(
        "gl,ghe->lhe", select_full, context_glob, precision=HIGHEST
    )
    merged = context.astype(BF).reshape(length, width)
    attended = mm(merged, w_out) + bias[4]
    normed_one, inverse_one = normalize(x.astype(F32) + attended)
    first_norm = normed_one * gain[0] + shift[0]
    first_low = first_norm.astype(BF)
    inner = mm(first_low, w_in) + c_in.astype(F32)
    act, slope = gelu_pair(inner)
    active = act.astype(BF)
    normed_two, inverse_two = normalize(first_norm + (mm(active, w_back) + bias[5]))
    result = normed_two * gain[1] + shift[1]
    upstream = upstream_low.astype(F32)
    grad_gain_two = jnp.sum(upstream * normed_two, axis=0)
    grad_shift_two = jnp.sum(upstream, axis=0)
    grad_second = norm_back(upstream * gain[1], normed_two, inverse_two)
    branch_grad = grad_second.astype(BF)
    grad_back_w = mm_tn(active, branch_grad)
    grad_out_bias = jnp.sum(branch_grad.astype(F32), axis=0)
    inner_grad = (mm_nt(branch_grad, w_back) * slope).astype(BF)
    grad_in_w = mm_tn(first_low, inner_grad)
    grad_in_bias = jnp.sum(inner_grad.astype(F32), axis=0)
    grad_first = grad_second + mm_nt(inner_grad, w_in)
    grad_gain_one = jnp.sum(grad_first * normed_one, axis=0)
    grad_shift_one = jnp.sum(grad_first, axis=0)
    grad_sum_one = norm_back(grad_first * gain[0], normed_one, inverse_one)
    attn_grad = grad_sum_one.astype(BF)
    grad_out_w = mm_tn(merged, attn_grad)
    grad_att_bias = jnp.sum(attn_grad.astype(F32), axis=0)
    ctx_grad = heads(mm_nt(attn_grad, w_out).astype(BF))
    local_grad = (ctx_grad.astype(F32) * keep_local[:, None, None]).astype(BF)
    glob_ctx_grad = jnp.einsum(
        "gl,lhe->ghe", select_low, ctx_grad, preferred_element_type=F32
    ).astype(BF)
    key_grad = jnp.zeros(k.shape, F32)
    value_grad = jnp.zeros(v.shape, F32)
    query_parts = []
    for index, offset in enumerate(offsets):
        qb, masked = block_scores(offset)
        probs = jnp.exp(masked - kept[index][0]) / kept[index][1]
        low = probs.astype(BF)
        gb = local_grad[offset : offset + block]
        grad_probs = jnp.einsum("ihe,jhe->hij", gb, v, preferred_element_type=F32)
        dot = jnp.sum(probs * grad_probs, axis=-1, keepdims=True)
        score_grad = (probs * (grad_probs - dot)).astype(BF)
        query_parts.append(jnp.einsum("hij,jhe->ihe", score_grad, k, preferred_element_type=F32))
        key_grad = key_grad + jnp.einsum(
            "hij,ihe->jhe", score_grad, qb, preferred_element_type=F32
        )
        value_grad = value_grad + jnp.einsum("hij,ihe->jhe", low, gb, preferred_element_type=F32)
    dq = jnp.concatenate(query_parts, axis=0).astype(BF)
    glob_grad_probs = jnp.einsum("ghe,jhe->hgj", glob_ctx_grad, vg, preferred_element_type=F32)
    glob_dot = jnp.sum(glob_probs * glob_grad_probs, axis=-1, keepdims=True)
    glob_score_grad = (glob_probs * (glob_grad_probs - glob_dot)).astype(BF)
    dqg = jnp.einsum("hgj,jhe->ghe", glob_score_grad, kg, preferred_element_type=F32).astype(BF)
    dkg = jnp.einsum("hgj,ghe->jhe", glob_score_grad, qg, preferred_element_type=F32).astype(BF)
    dvg = jnp.einsum("hgj,ghe->jhe", glob_low, glob_ctx_grad, preferred_element_type=F32).astype(BF)

    def flat(value):
        return value.astype(BF).reshape(value.shape[0], width)

    dq, dk, dv, dkg, dvg = (flat(value) for value in (dq, key_grad, value_grad, dkg, dvg))
    pre_query = dq * scale
    glob_pre = flat(dqg) * scale
    token_grad = (
        grad_sum_one
        + mm_nt(pre_query, w_local[0])
        + mm_nt(dk, w_local[1])
        + mm_nt(dv, w_local[2])
        + mm_nt(dkg, w_global[1])
        + mm_nt(dvg, w_global[2])
    )
    token_grad = token_grad + jnp.einsum(
        "gr,gd->rd", select_full, mm_nt(glob_pre, w_global[0]), precision=HIGHEST
    )
    grad_local = jnp.stack([mm_tn(x, pre_query), mm_tn(x, dk), mm_tn(x, dv)])
    grad_global = jnp.stack([mm_tn(rows_glob, glob_pre), mm_tn(x, dkg), mm_tn(x, dvg)])

    def total_of(value):
        return jnp.sum(value.astype(F32), axis=0)

    grad_bias = jnp.stack(
        [
            total_of(pre_query),
            total_of(dv),
            total_of(glob_pre),
            total_of(dvg),
            grad_att_bias,
            grad_out_bias,
        ]
    )
    grad_gain = jnp.stack([grad_gain_one, grad_gain_two])
    grad_shift = jnp.stack([grad_shift_one, grad_shift_two])
    return (
        result.astype(BF),
        token_grad.astype(BF),
        (
            grad_local,
            grad_global,
            grad_out_w,
            grad_bias,
            grad_gain,
            grad_shift,
            grad_in_w,
            grad_in_bias,
            grad_back_w,
        ),
    )


def per_device(
    inputs,
    global_pos,
    w_local,
    w_global,
    w_out,
    b_proj,
    gains,
    shifts,
    w_in,
    c_in,
    w_back,
    cotangent,
):
    sp_count = lax.axis_size("sp")
    fsdp_count = lax.axis_size("fsdp")
    sp_index = lax.axis_index("sp")
    own_seqs = inputs.shape[0] // sp_count
    shard = w_out.shape[0]
    width = w_out.shape[1]
    ff_shard = w_back.shape[0]
    pieces = w_in.shape[1] // width

    def to_sequence(value):
        return lax.all_to_all(value, "sp", split_axis=0, concat_axis=1, tiled=True)

    def to_tokens(value):
        return lax.all_to_all(value, "sp", split_axis=1, concat_axis=0, tiled=True)

    x_all = to_sequence(inputs)
    up_all = to_sequence(cotangent)
    own_pos = lax.dynamic_slice_in_dim(global_pos, sp_index * own_seqs, own_seqs, 0)

    small = jnp.concatenate(
        [b_proj.reshape(-1), gains.reshape(-1), shifts.reshape(-1), c_in.reshape(-1)]
    )
    small_rows = -(-small.shape[0] // width)
    small = jnp.pad(small, (0, small_rows * width - small.shape[0])).reshape(small_rows, width)
    pack_one = jnp.concatenate(
        [w_local.reshape(-1, width), w_global.reshape(-1, width), w_out, small], axis=0
    )
    pack_two = jnp.concatenate(
        [w_in.reshape(shard, pieces, width).transpose(1, 0, 2).reshape(-1, width), w_back], axis=0
    )
    all_one = lax.all_gather(pack_one, "fsdp")
    all_two = lax.all_gather(pack_two, "fsdp")

    def part(packed, start):
        return packed[:, start : start + shard].reshape(fsdp_count * shard, width)

    full_local = [part(all_one, index * shard) for index in range(3)]
    full_global = [part(all_one, (3 + index) * shard) for index in range(3)]
    full_out = part(all_one, 6 * shard)
    small_all = all_one[:, 7 * shard :].reshape(fsdp_count, -1)

    def vectors(start, count):
        taken = small_all[:, start : start + count * shard].reshape(fsdp_count, count, shard)
        return taken.transpose(1, 0, 2).reshape(count, fsdp_count * shard)

    full_bias = vectors(0, 6)
    full_gain = vectors(6 * shard, 2)
    full_shift = vectors(8 * shard, 2)
    full_c = small_all[:, 10 * shard : 10 * shard + ff_shard].reshape(-1)
    full_in = jnp.concatenate([part(all_two, index * shard) for index in range(pieces)], axis=1)
    full_back = all_two[:, pieces * shard :].reshape(-1, width)
    weights = (
        full_local,
        full_global,
        full_out,
        full_bias,
        full_gain,
        full_shift,
        full_in,
        full_c,
        full_back,
    )
    results = []
    token_grads = []
    totals = None
    for index in range(own_seqs):
        result, token_grad, grads = sequence_step(
            x_all[index], own_pos[index], up_all[index], weights
        )
        results.append(result)
        token_grads.append(token_grad)
        totals = grads if totals is None else tuple(a + b for a, b in zip(totals, grads))
    out = to_tokens(jnp.stack(results))
    grad_inputs = to_tokens(jnp.stack(token_grads))
    g_local, g_global, g_out, g_bias, g_gain, g_shift, g_in, g_c, g_back = totals

    def rows(value):
        return value.astype(BF).reshape(-1, fsdp_count, shard, width).transpose(1, 0, 2, 3)

    def cols(value):
        return value.reshape(-1, fsdp_count, shard).transpose(1, 0, 2).reshape(fsdp_count, -1)

    g_small = jnp.concatenate(
        [cols(g_bias), cols(g_gain), cols(g_shift), g_c.reshape(fsdp_count, ff_shard)], axis=1
    ).astype(BF)
    g_small = jnp.pad(g_small, ((0, 0), (0, small_rows * width - g_small.shape[1])))
    first = jnp.concatenate(
        [
            rows(g_in.reshape(width, pieces, width).transpose(1, 0, 2)).reshape(
                fsdp_count, -1, width
            ),
            g_back.astype(BF).reshape(fsdp_count, ff_shard, width),
        ],
        axis=1,
    )
    second = jnp.concatenate(
        [
            rows(g_local).reshape(fsdp_count, -1, width),
            rows(g_global).reshape(fsdp_count, -1, width),
            rows(g_out).reshape(fsdp_count, -1, width),
            g_small.reshape(fsdp_count, small_rows, width),
        ],
        axis=1,
    )

    def reduce(value):
        mine = lax.psum_scatter(value, "fsdp", scatter_dimension=0, tiled=False)
        return lax.psum(mine, "sp").astype(F32)

    first = reduce(first)
    second = reduce(second)
    small_sum = second[7 * shard :].reshape(-1)
    return (
        out,
        grad_inputs,
        second[: 3 * shard].reshape(3, shard, width),
        second[3 * shard : 6 * shard].reshape(3, shard, width),
        second[6 * shard : 7 * shard],
        small_sum[: 6 * shard].reshape(6, shard),
        small_sum[6 * shard : 8 * shard].reshape(2, shard),
        small_sum[8 * shard : 10 * shard].reshape(2, shard),
        first[: pieces * shard]
        .reshape(pieces, shard, width)
        .transpose(1, 0, 2)
        .reshape(shard, pieces * width),
        small_sum[10 * shard : 10 * shard + ff_shard],
        first[pieces * shard :],
    )


def solution(mesh):
    rows = P("fsdp", None)
    tokens = P("fsdp", "sp", None)
    columns = P(None, "fsdp")
    stacked = P(None, "fsdp", None)
    return jax.shard_map(
        per_device,
        mesh=mesh,
        in_specs=(
            tokens,
            rows,
            stacked,
            stacked,
            rows,
            columns,
            columns,
            columns,
            rows,
            P("fsdp"),
            rows,
            tokens,
        ),
        out_specs=(
            tokens,
            tokens,
            stacked,
            stacked,
            rows,
            columns,
            columns,
            columns,
            rows,
            P("fsdp"),
            rows,
        ),
        check_vma=False,
    )
```

```python
import jax
import jax.numpy as jnp
from jax import lax
from jax.experimental import pallas as pl
from jax.experimental.pallas import tpu as pltpu
from jax.sharding import PartitionSpec as P

HEADS = 12
HEAD_DIM = 64
WIN = 256
QB = 128
NEG = -1e9

HIGHEST = lax.Precision.HIGHEST
NORM_EPS = 1e-05
BF = jnp.bfloat16
F32 = jnp.float32


def normalize(summed):
    center = summed - jnp.mean(summed, axis=-1, keepdims=True)
    inverse = lax.rsqrt(jnp.mean(center * center, axis=-1, keepdims=True) + NORM_EPS)
    return (center * inverse, inverse)


def norm_back(scaled, normed, inverse):
    return inverse * (
        scaled
        - jnp.mean(scaled, axis=-1, keepdims=True)
        - normed * jnp.mean(scaled * normed, axis=-1, keepdims=True)
    )


def mm(a, b):
    return jnp.dot(a, b, preferred_element_type=F32)


def mm_nt(a, b):
    return lax.dot_general(a, b, (((1,), (1,)), ((), ())), preferred_element_type=F32)


def mm_tn(a, b):
    return lax.dot_general(a, b, (((0,), (0,)), ((), ())), preferred_element_type=F32)


def gelu_pair(inner):
    cdf = 0.5 * (1.0 + lax.erf(inner * (0.5**0.5)))
    pdf = jnp.exp(-0.5 * inner * inner) * 0.3989422804014327
    return (inner * cdf, cdf + inner * pdf)


def dot_nn(a,b): return jnp.dot(a,b,preferred_element_type=F32)
def dot_nt(a,b): return lax.dot_general(a,b,(((1,),(1,)),((),())),preferred_element_type=F32)
def dot_tn(a,b): return lax.dot_general(a,b,(((0,),(0,)),((),())),preferred_element_type=F32)

def split_pair(block):
    lane=lax.broadcasted_iota(jnp.int32,block.shape,1)
    zero=jnp.zeros_like(block)
    return jnp.concatenate([jnp.where(lane<HEAD_DIM,block,zero),jnp.where(lane<HEAD_DIM,zero,block)],axis=0)

def far_mask(pos, start):
    place=start+lax.broadcasted_iota(jnp.int32,(16,2*QB),1)%QB
    return (pos>=0)&(jnp.abs(place-pos)>WIN)

def edge_masks():
    row=lax.broadcasted_iota(jnp.int32,(QB,2*QB),0)
    col=lax.broadcasted_iota(jnp.int32,(QB,2*QB),1)%QB
    return row>=col, row<=col

def key_range(start,length):
    return max(0,start-WIN), min(length,start+QB+WIN)

def pick_head(both):
    row=lax.broadcasted_iota(jnp.int32,(2*HEAD_DIM,QB),0)
    return jnp.where(row<HEAD_DIM,both[:,:QB],both[:,QB:])

def masked_scores(raw,start,length,low_ok,high_ok):
    lo,hi=key_range(start,length)
    parts=[]
    for first in range(lo,hi,QB):
        chunk=raw[first-lo:first-lo+QB]
        if first==start-WIN: chunk=jnp.where(low_ok,chunk,NEG)
        elif first==start+WIN: chunk=jnp.where(high_ok,chunk,NEG)
        parts.append(chunk)
    return parts

def fwd_kernel(pos_ref,q_ref,k_ref,v_ref,ctx_ref,lse_ref):
    length=q_ref.shape[0]
    pos=pos_ref[...]
    token=lax.broadcasted_iota(jnp.int32,(16,length),1)
    sel=jnp.where(token==pos,1.0,0.0).astype(BF)
    key_far=dot_nn(sel,k_ref[...]).astype(BF)
    val_far_t=dot_nn(sel,v_ref[...]).astype(BF).T
    val_t=v_ref[...].T
    low_ok,high_ok=edge_masks()
    for start in range(0,length,QB):
        lo,hi=key_range(start,length)
        qq=split_pair(q_ref[start:start+QB,:])
        raw=dot_nt(k_ref[lo:hi,:],qq)
        parts=masked_scores(raw,start,length,low_ok,high_ok)
        far=jnp.where(far_mask(pos,start),dot_nt(key_far,qq),NEG)
        top=jnp.max(far,axis=0,keepdims=True)
        for part in parts: top=jnp.maximum(top,jnp.max(part,axis=0,keepdims=True))
        far_p=jnp.exp(far-top)
        total=jnp.sum(far_p,axis=0,keepdims=True)
        probs=[]
        for part in parts:
            p=jnp.exp(part-top)
            total=total+jnp.sum(p,axis=0,keepdims=True)
            probs.append(p.astype(BF))
        both=dot_nn(val_t[:,lo:hi],jnp.concatenate(probs,axis=0))+dot_nn(val_far_t,far_p.astype(BF))
        both=both*(1.0/total)
        ctx_ref[start:start+QB,:]=pick_head(both).T.astype(BF)
        lse=top+jnp.log(total)
        lse_ref[0,0:1,start:start+QB]=lse[:,:QB]
        lse_ref[0,1:2,start:start+QB]=lse[:,QB:]

def attn_fwd(pos,q,k,v):
    length,width=q.shape
    pairs=width//128
    col=pl.BlockSpec((length,128),lambda i:(0,i))
    return pl.pallas_call(fwd_kernel,grid=(pairs,),
        in_specs=[pl.BlockSpec((16,1),lambda i:(0,0)),col,col,col],
        out_specs=[col,pl.BlockSpec((1,8,length),lambda i:(i,0,0))],
        out_shape=[jax.ShapeDtypeStruct((length,width),BF),jax.ShapeDtypeStruct((pairs,8,length),F32)],
        compiler_params=pltpu.CompilerParams(vmem_limit_bytes=32<<20),
        cost_estimate=pl.CostEstimate(flops=int(20e9),bytes_accessed=8<<20,transcendentals=8<<20),
        name="attend")(pos,q,k,v)

def bwd_kernel(pos_ref,q_ref,k_ref,v_ref,g_ref,ctx_ref,lse_ref,dq_ref,dk_ref,dv_ref,dk_acc,dv_acc,grad_scr):
    length=q_ref.shape[0]
    pos=pos_ref[...]
    token=lax.broadcasted_iota(jnp.int32,(16,length),1)
    sel_bool=token==pos
    sel=jnp.where(sel_bool,1.0,0.0).astype(BF)
    sel_full=jnp.where(sel_bool,1.0,0.0)
    key_far=dot_nn(sel,k_ref[...]).astype(BF)
    val_far=dot_nn(sel,v_ref[...]).astype(BF)
    key_far_t=key_far.T
    key_t=k_ref[...].T
    ones=jnp.ones((16,128),F32)
    is_glob=lax.dot_general(sel_full,ones,(((0,),(0,)),((),())),preferred_element_type=F32)
    grad_scr[...]=jnp.where(is_glob>0.5,0.0,g_ref[...].astype(F32)).astype(BF)
    prod=grad_scr[...].astype(F32)*ctx_ref[...].astype(F32)
    hrow=lax.broadcasted_iota(jnp.int32,(16,128),0)
    hlane=lax.broadcasted_iota(jnp.int32,(16,128),1)//HEAD_DIM
    hsel=jnp.where(hrow==hlane,1.0,0.0)
    delta_all=lax.dot_general(hsel,prod,(((1,),(1,)),((),())),preferred_element_type=F32,precision=lax.Precision.HIGHEST)
    dk_acc[...]=jnp.zeros_like(dk_acc)
    dv_acc[...]=jnp.zeros_like(dv_acc)
    dk_far=jnp.zeros((16,128),F32); dv_far=jnp.zeros((16,128),F32)
    low_ok,high_ok=edge_masks()
    for start in range(0,length,QB):
        lo,hi=key_range(start,length)
        qq=split_pair(q_ref[start:start+QB,:])
        gg=split_pair(grad_scr[start:start+QB,:])
        lse=jnp.concatenate([lse_ref[0,0:1,start:start+QB],lse_ref[0,1:2,start:start+QB]],axis=1)
        delta=jnp.concatenate([delta_all[0:1,start:start+QB],delta_all[1:2,start:start+QB]],axis=1)
        dq_t=jnp.zeros((128,2*QB),F32)
        def one(scores,vals):
            p=jnp.exp(scores-lse)
            dp=dot_nt(vals,gg)
            return p.astype(BF),(p*(dp-delta)).astype(BF)
        far=jnp.where(far_mask(pos,start),dot_nt(key_far,qq),NEG)
        p,ds=one(far,val_far)
        dv_far=dv_far+dot_nn(p,gg); dk_far=dk_far+dot_nn(ds,qq)
        dq_t=dq_t+dot_nn(key_far_t,ds)
        parts=masked_scores(dot_nt(k_ref[lo:hi,:],qq),start,length,low_ok,high_ok)
        plist=[];dlist=[]
        for n,part in enumerate(parts):
            a=lo+n*QB
            p,ds=one(part,v_ref[a:a+QB,:])
            plist.append(p);dlist.append(ds)
        p=jnp.concatenate(plist,axis=0); ds=jnp.concatenate(dlist,axis=0)
        dv_acc[lo:hi,:]+=dot_nn(p,gg)
        dk_acc[lo:hi,:]+=dot_nn(ds,qq)
        dq_t=dq_t+dot_nn(key_t[:,lo:hi],ds)
        dq_ref[start:start+QB,:]=pick_head(dq_t).T.astype(BF)
    dk_ref[...]=(dk_acc[...]+lax.dot_general(sel_full,dk_far,(((0,),(0,)),((),())),preferred_element_type=F32,precision=lax.Precision.HIGHEST)).astype(BF)
    dv_ref[...]=(dv_acc[...]+lax.dot_general(sel_full,dv_far,(((0,),(0,)),((),())),preferred_element_type=F32,precision=lax.Precision.HIGHEST)).astype(BF)

def attn_bwd(pos,q,k,v,grad,ctx,lse):
    length,width=q.shape
    pairs=width//128
    col=pl.BlockSpec((length,128),lambda i:(0,i))
    out=jax.ShapeDtypeStruct((length,width),BF)
    return pl.pallas_call(bwd_kernel,grid=(pairs,),
        in_specs=[pl.BlockSpec((16,1),lambda i:(0,0)),col,col,col,col,col,pl.BlockSpec((1,8,length),lambda i:(i,0,0))],
        out_specs=[col,col,col],
        out_shape=[out,out,out],
        scratch_shapes=[pltpu.VMEM((length,128),F32),pltpu.VMEM((length,128),F32),pltpu.VMEM((length,128),BF)],
        compiler_params=pltpu.CompilerParams(vmem_limit_bytes=32<<20),
        cost_estimate=pl.CostEstimate(flops=int(40e9),bytes_accessed=12<<20,transcendentals=8<<20),
        name="attend_back")(pos,q,k,v,grad,ctx,lse)


def sequence_step(x, positions, upstream_low, weights):
    w_local, w_global, w_out, b_proj, gains, shifts, w_in, c_in, w_back = weights
    length, width = x.shape
    glob_count = positions.shape[0]
    scale = HEAD_DIM ** (-0.5)
    bias = b_proj.astype(F32)
    gain = gains.astype(F32)
    shift = shifts.astype(F32)
    pos16 = jnp.full((16, 1), -1, jnp.int32).at[:glob_count, 0].set(positions)
    q = ((mm(x, w_local[0]) + bias[0]) * scale).astype(BF)
    k = mm(x, w_local[1]).astype(BF)
    v = (mm(x, w_local[2]) + bias[1]).astype(BF)
    ctx_loc, lse = attn_fwd(pos16, q, k, v)
    places = jnp.arange(length, dtype=jnp.int32)
    select = positions[:, None] == places[None, :]
    select_low = select.astype(BF)
    is_glob = jnp.any(select, axis=0)[:, None]
    rows_glob = mm(select_low, x).astype(BF)
    head_of = jnp.arange(width, dtype=jnp.int32) // HEAD_DIM
    own = head_of[None, :] == jnp.arange(16, dtype=jnp.int32)[:, None]

    def spread(rows):
        return jnp.where(own[None], rows[:, None, :], 0).reshape(-1, width)

    def gather(rows):
        return jnp.sum(jnp.where(own[None], rows.reshape(glob_count, 16, width), 0), axis=1)

    qg = ((mm(rows_glob, w_global[0]) + bias[2]) * scale).astype(BF)
    q_spread = spread(qg)
    key_map = mm_nt(w_global[1], q_spread).astype(BF)
    glob_scores = mm(x, key_map)
    glob_probs = jax.nn.softmax(glob_scores, axis=0)
    glob_low = glob_probs.astype(BF)
    mixed = mm_tn(glob_low, x)
    glob_mass = jnp.sum(glob_low.astype(F32), axis=0)
    ctx_glob = gather(mm(mixed.astype(BF), w_global[2]) + glob_mass[:, None] * bias[3])
    ctx_glob = ctx_glob.astype(BF)
    merged = jnp.where(is_glob, mm_tn(select_low, ctx_glob).astype(BF), ctx_loc)
    attended = mm(merged, w_out) + bias[4]
    normed_one, inverse_one = normalize(x.astype(F32) + attended)
    first_norm = normed_one * gain[0] + shift[0]
    first_low = first_norm.astype(BF)
    inner = mm(first_low, w_in) + c_in.astype(F32)
    act, slope = gelu_pair(inner)
    active = act.astype(BF)
    normed_two, inverse_two = normalize(first_norm + (mm(active, w_back) + bias[5]))
    result = normed_two * gain[1] + shift[1]
    upstream = upstream_low.astype(F32)
    grad_gain_two = jnp.sum(upstream * normed_two, axis=0)
    grad_shift_two = jnp.sum(upstream, axis=0)
    grad_second = norm_back(upstream * gain[1], normed_two, inverse_two)
    branch_grad = grad_second.astype(BF)
    grad_back_w = mm_tn(active, branch_grad)
    grad_out_bias = jnp.sum(branch_grad.astype(F32), axis=0)
    inner_grad = (mm_nt(branch_grad, w_back) * slope).astype(BF)
    grad_in_w = mm_tn(first_low, inner_grad)
    grad_in_bias = jnp.sum(inner_grad.astype(F32), axis=0)
    grad_first = grad_second + mm_nt(inner_grad, w_in)
    grad_gain_one = jnp.sum(grad_first * normed_one, axis=0)
    grad_shift_one = jnp.sum(grad_first, axis=0)
    grad_sum_one = norm_back(grad_first * gain[0], normed_one, inverse_one)
    attn_grad = grad_sum_one.astype(BF)
    grad_out_w = mm_tn(merged, attn_grad)
    grad_att_bias = jnp.sum(attn_grad.astype(F32), axis=0)
    ctx_grad = mm_nt(attn_grad, w_out).astype(BF)
    dq, dk, dv = attn_bwd(pos16, q, k, v, ctx_grad, merged, lse)
    pre_query = dq * scale
    glob_ctx_grad = mm(select_low, ctx_grad).astype(BF)
    c_spread = spread(glob_ctx_grad)
    value_map = mm_nt(w_global[2], c_spread).astype(BF)
    glob_grad_probs = mm(x, value_map) + mm_nt(bias[3:4].astype(BF), c_spread)
    glob_dot = jnp.sum(glob_probs * glob_grad_probs, axis=0, keepdims=True)
    glob_ds = (glob_probs * (glob_grad_probs - glob_dot)).astype(BF)
    key_mixed = mm_tn(glob_ds, x)
    dqg = gather(mm(key_mixed.astype(BF), w_global[1])).astype(BF)
    glob_pre = dqg * scale
    token_grad = (
        grad_sum_one
        + mm_nt(pre_query, w_local[0])
        + mm_nt(dk, w_local[1])
        + mm_nt(dv, w_local[2])
        + mm_nt(glob_ds, key_map)
        + mm_nt(glob_low, value_map)
    )
    rows_grad = mm_nt(glob_pre, w_global[0])
    token_grad = token_grad + mm_tn(select.astype(F32), rows_grad)
    grad_local = jnp.stack([mm_tn(x, pre_query), mm_tn(x, dk), mm_tn(x, dv)])
    grad_global = jnp.stack(
        [
            mm_tn(rows_glob, glob_pre),
            mm_tn(key_mixed.astype(BF), q_spread),
            mm_tn(mixed.astype(BF), c_spread),
        ]
    )

    def total_of(value):
        return jnp.sum(value.astype(F32), axis=0)

    grad_bias = jnp.stack(
        [
            total_of(pre_query),
            total_of(dv),
            total_of(glob_pre),
            jnp.sum(glob_mass[:, None] * c_spread.astype(F32), axis=0),
            grad_att_bias,
            grad_out_bias,
        ]
    )
    grad_gain = jnp.stack([grad_gain_one, grad_gain_two])
    grad_shift = jnp.stack([grad_shift_one, grad_shift_two])
    return (
        result.astype(BF),
        token_grad.astype(BF),
        (
            grad_local,
            grad_global,
            grad_out_w,
            grad_bias,
            grad_gain,
            grad_shift,
            grad_in_w,
            grad_in_bias,
            grad_back_w,
        ),
    )


def per_device(
    inputs,
    global_pos,
    w_local,
    w_global,
    w_out,
    b_proj,
    gains,
    shifts,
    w_in,
    c_in,
    w_back,
    cotangent,
):
    sp_count = lax.axis_size("sp")
    fsdp_count = lax.axis_size("fsdp")
    sp_index = lax.axis_index("sp")
    own_seqs = inputs.shape[0] // sp_count
    shard = w_out.shape[0]
    width = w_out.shape[1]
    ff_shard = w_back.shape[0]
    pieces = w_in.shape[1] // width

    def to_sequence(value):
        return lax.all_to_all(value, "sp", split_axis=0, concat_axis=1, tiled=True)

    def to_tokens(value):
        return lax.all_to_all(value, "sp", split_axis=1, concat_axis=0, tiled=True)

    x_all = to_sequence(inputs)
    up_all = to_sequence(cotangent)
    own_pos = lax.dynamic_slice_in_dim(global_pos, sp_index * own_seqs, own_seqs, 0)

    small = jnp.concatenate(
        [b_proj.reshape(-1), gains.reshape(-1), shifts.reshape(-1), c_in.reshape(-1)]
    )
    small_rows = -(-small.shape[0] // width)
    small = jnp.pad(small, (0, small_rows * width - small.shape[0])).reshape(small_rows, width)
    pack_one = jnp.concatenate(
        [w_local.reshape(-1, width), w_global.reshape(-1, width), w_out, small], axis=0
    )
    pack_two = jnp.concatenate(
        [w_in.reshape(shard, pieces, width).transpose(1, 0, 2).reshape(-1, width), w_back], axis=0
    )
    all_one = lax.all_gather(pack_one, "fsdp")
    all_two = lax.all_gather(pack_two, "fsdp")

    def part(packed, start):
        return packed[:, start : start + shard].reshape(fsdp_count * shard, width)

    full_local = [part(all_one, index * shard) for index in range(3)]
    full_global = [part(all_one, (3 + index) * shard) for index in range(3)]
    full_out = part(all_one, 6 * shard)
    small_all = all_one[:, 7 * shard :].reshape(fsdp_count, -1)

    def vectors(start, count):
        taken = small_all[:, start : start + count * shard].reshape(fsdp_count, count, shard)
        return taken.transpose(1, 0, 2).reshape(count, fsdp_count * shard)

    full_bias = vectors(0, 6)
    full_gain = vectors(6 * shard, 2)
    full_shift = vectors(8 * shard, 2)
    full_c = small_all[:, 10 * shard : 10 * shard + ff_shard].reshape(-1)
    full_in = jnp.concatenate([part(all_two, index * shard) for index in range(pieces)], axis=1)
    full_back = all_two[:, pieces * shard :].reshape(-1, width)
    weights = (
        full_local,
        full_global,
        full_out,
        full_bias,
        full_gain,
        full_shift,
        full_in,
        full_c,
        full_back,
    )
    results = []
    token_grads = []
    totals = None
    for index in range(own_seqs):
        result, token_grad, grads = sequence_step(
            x_all[index], own_pos[index], up_all[index], weights
        )
        results.append(result)
        token_grads.append(token_grad)
        totals = grads if totals is None else tuple(a + b for a, b in zip(totals, grads))
    out = to_tokens(jnp.stack(results))
    grad_inputs = to_tokens(jnp.stack(token_grads))
    g_local, g_global, g_out, g_bias, g_gain, g_shift, g_in, g_c, g_back = totals

    def rows(value):
        return value.astype(BF).reshape(-1, fsdp_count, shard, width).transpose(1, 0, 2, 3)

    def cols(value):
        return value.reshape(-1, fsdp_count, shard).transpose(1, 0, 2).reshape(fsdp_count, -1)

    g_small = jnp.concatenate(
        [cols(g_bias), cols(g_gain), cols(g_shift), g_c.reshape(fsdp_count, ff_shard)], axis=1
    ).astype(BF)
    g_small = jnp.pad(g_small, ((0, 0), (0, small_rows * width - g_small.shape[1])))
    first = jnp.concatenate(
        [
            rows(g_in.reshape(width, pieces, width).transpose(1, 0, 2)).reshape(
                fsdp_count, -1, width
            ),
            g_back.astype(BF).reshape(fsdp_count, ff_shard, width),
        ],
        axis=1,
    )
    second = jnp.concatenate(
        [
            rows(g_local).reshape(fsdp_count, -1, width),
            rows(g_global).reshape(fsdp_count, -1, width),
            rows(g_out).reshape(fsdp_count, -1, width),
            g_small.reshape(fsdp_count, small_rows, width),
        ],
        axis=1,
    )

    def reduce(value):
        mine = lax.psum_scatter(value, "fsdp", scatter_dimension=0, tiled=False)
        return lax.psum(mine, "sp").astype(F32)

    first = reduce(first)
    second = reduce(second)
    small_sum = second[7 * shard :].reshape(-1)
    return (
        out,
        grad_inputs,
        second[: 3 * shard].reshape(3, shard, width),
        second[3 * shard : 6 * shard].reshape(3, shard, width),
        second[6 * shard : 7 * shard],
        small_sum[: 6 * shard].reshape(6, shard),
        small_sum[6 * shard : 8 * shard].reshape(2, shard),
        small_sum[8 * shard : 10 * shard].reshape(2, shard),
        first[: pieces * shard]
        .reshape(pieces, shard, width)
        .transpose(1, 0, 2)
        .reshape(shard, pieces * width),
        small_sum[10 * shard : 10 * shard + ff_shard],
        first[pieces * shard :],
    )


def solution(mesh):
    rows = P("fsdp", None)
    tokens = P("fsdp", "sp", None)
    columns = P(None, "fsdp")
    stacked = P(None, "fsdp", None)
    return jax.shard_map(
        per_device,
        mesh=mesh,
        in_specs=(
            tokens,
            rows,
            stacked,
            stacked,
            rows,
            columns,
            columns,
            columns,
            rows,
            P("fsdp"),
            rows,
            tokens,
        ),
        out_specs=(
            tokens,
            tokens,
            stacked,
            stacked,
            rows,
            columns,
            columns,
            columns,
            rows,
            P("fsdp"),
            rows,
        ),
        check_vma=False,
    )
```

```python
import jax
import jax.numpy as jnp
from jax import lax
from jax.experimental import pallas as pl
from jax.experimental.pallas import tpu as pltpu
from jax.sharding import PartitionSpec as P

HEADS = 12
HEAD_DIM = 64
WIN = 256
QB = 128
NEG = -1e9

HIGHEST = lax.Precision.HIGHEST
NORM_EPS = 1e-05
BF = jnp.bfloat16
F32 = jnp.float32


def normalize(summed):
    center = summed - jnp.mean(summed, axis=-1, keepdims=True)
    inverse = lax.rsqrt(jnp.mean(center * center, axis=-1, keepdims=True) + NORM_EPS)
    return (center * inverse, inverse)


def norm_back(scaled, normed, inverse):
    return inverse * (
        scaled
        - jnp.mean(scaled, axis=-1, keepdims=True)
        - normed * jnp.mean(scaled * normed, axis=-1, keepdims=True)
    )


def mm(a, b):
    return jnp.dot(a, b, preferred_element_type=F32)


def mm_nt(a, b):
    return lax.dot_general(a, b, (((1,), (1,)), ((), ())), preferred_element_type=F32)


def mm_tn(a, b):
    return lax.dot_general(a, b, (((0,), (0,)), ((), ())), preferred_element_type=F32)


def gelu_pair(inner):
    cdf = 0.5 * (1.0 + lax.erf(inner * (0.5**0.5)))
    pdf = jnp.exp(-0.5 * inner * inner) * 0.3989422804014327
    return (inner * cdf, cdf + inner * pdf)


def dot_nn(a,b): return jnp.dot(a,b,preferred_element_type=F32)
def dot_nt(a,b): return lax.dot_general(a,b,(((1,),(1,)),((),())),preferred_element_type=F32)
def dot_tn(a,b): return lax.dot_general(a,b,(((0,),(0,)),((),())),preferred_element_type=F32)

def split_pair(block):
    lane=lax.broadcasted_iota(jnp.int32,block.shape,1)
    zero=jnp.zeros_like(block)
    return jnp.concatenate([jnp.where(lane<HEAD_DIM,block,zero),jnp.where(lane<HEAD_DIM,zero,block)],axis=0)

def far_mask(pos, start):
    place=start+lax.broadcasted_iota(jnp.int32,(16,2*QB),1)%QB
    return (pos>=0)&(jnp.abs(place-pos)>WIN)

def edge_masks():
    row=lax.broadcasted_iota(jnp.int32,(QB,2*QB),0)
    col=lax.broadcasted_iota(jnp.int32,(QB,2*QB),1)%QB
    return row>=col, row<=col

def key_range(start,length):
    return max(0,start-WIN), min(length,start+QB+WIN)

def pick_head(both):
    row=lax.broadcasted_iota(jnp.int32,(2*HEAD_DIM,QB),0)
    return jnp.where(row<HEAD_DIM,both[:,:QB],both[:,QB:])

def masked_scores(raw,start,length,low_ok,high_ok):
    lo,hi=key_range(start,length)
    parts=[]
    for first in range(lo,hi,QB):
        chunk=raw[first-lo:first-lo+QB]
        if first==start-WIN: chunk=jnp.where(low_ok,chunk,NEG)
        elif first==start+WIN: chunk=jnp.where(high_ok,chunk,NEG)
        parts.append(chunk)
    return parts

def fwd_kernel(pos_ref,q_ref,k_ref,v_ref,ctx_ref,lse_ref):
    length=q_ref.shape[0]
    pos=pos_ref[...]
    token=lax.broadcasted_iota(jnp.int32,(16,length),1)
    sel=jnp.where(token==pos,1.0,0.0).astype(BF)
    key_far=dot_nn(sel,k_ref[...]).astype(BF)
    val_far_t=dot_nn(sel,v_ref[...]).astype(BF).T
    val_t=v_ref[...].T
    low_ok,high_ok=edge_masks()
    for start in range(0,length,QB):
        lo,hi=key_range(start,length)
        qq=split_pair(q_ref[start:start+QB,:])
        raw=dot_nt(k_ref[lo:hi,:],qq)
        parts=masked_scores(raw,start,length,low_ok,high_ok)
        far=jnp.where(far_mask(pos,start),dot_nt(key_far,qq),NEG)
        top=jnp.max(far,axis=0,keepdims=True)
        for part in parts: top=jnp.maximum(top,jnp.max(part,axis=0,keepdims=True))
        far_p=jnp.exp(far-top)
        total=jnp.sum(far_p,axis=0,keepdims=True)
        probs=[]
        for part in parts:
            p=jnp.exp(part-top)
            total=total+jnp.sum(p,axis=0,keepdims=True)
            probs.append(p.astype(BF))
        both=dot_nn(val_t[:,lo:hi],jnp.concatenate(probs,axis=0))+dot_nn(val_far_t,far_p.astype(BF))
        both=both*(1.0/total)
        ctx_ref[start:start+QB,:]=pick_head(both).T.astype(BF)
        lse=top+jnp.log(total)
        lse_ref[0,0:1,start:start+QB]=lse[:,:QB]
        lse_ref[0,1:2,start:start+QB]=lse[:,QB:]

def attn_fwd(pos,q,k,v):
    length,width=q.shape
    pairs=width//128
    col=pl.BlockSpec((length,128),lambda i:(0,i))
    return pl.pallas_call(fwd_kernel,grid=(pairs,),
        in_specs=[pl.BlockSpec((16,1),lambda i:(0,0)),col,col,col],
        out_specs=[col,pl.BlockSpec((1,8,length),lambda i:(i,0,0))],
        out_shape=[jax.ShapeDtypeStruct((length,width),BF),jax.ShapeDtypeStruct((pairs,8,length),F32)],
        compiler_params=pltpu.CompilerParams(vmem_limit_bytes=32<<20),
        cost_estimate=pl.CostEstimate(flops=int(20e9),bytes_accessed=8<<20,transcendentals=8<<20),
        name="attend")(pos,q,k,v)

def bwd_kernel(pos_ref,q_ref,k_ref,v_ref,g_ref,ctx_ref,lse_ref,dq_ref,dk_ref,dv_ref,dk_acc,dv_acc,grad_scr):
    length=q_ref.shape[0]
    pos=pos_ref[...]
    token=lax.broadcasted_iota(jnp.int32,(16,length),1)
    sel_bool=token==pos
    sel=jnp.where(sel_bool,1.0,0.0).astype(BF)
    sel_full=jnp.where(sel_bool,1.0,0.0)
    key_far=dot_nn(sel,k_ref[...]).astype(BF)
    val_far=dot_nn(sel,v_ref[...]).astype(BF)
    key_far_t=key_far.T
    key_t=k_ref[...].T
    ones=jnp.ones((16,128),F32)
    is_glob=lax.dot_general(sel_full,ones,(((0,),(0,)),((),())),preferred_element_type=F32)
    grad_scr[...]=jnp.where(is_glob>0.5,0.0,g_ref[...].astype(F32)).astype(BF)
    prod=grad_scr[...].astype(F32)*ctx_ref[...].astype(F32)
    hrow=lax.broadcasted_iota(jnp.int32,(16,128),0)
    hlane=lax.broadcasted_iota(jnp.int32,(16,128),1)//HEAD_DIM
    hsel=jnp.where(hrow==hlane,1.0,0.0)
    delta_all=lax.dot_general(hsel,prod,(((1,),(1,)),((),())),preferred_element_type=F32,precision=lax.Precision.HIGHEST)
    dk_acc[...]=jnp.zeros_like(dk_acc)
    dv_acc[...]=jnp.zeros_like(dv_acc)
    dk_far=jnp.zeros((16,128),F32); dv_far=jnp.zeros((16,128),F32)
    low_ok,high_ok=edge_masks()
    for start in range(0,length,QB):
        lo,hi=key_range(start,length)
        qq=split_pair(q_ref[start:start+QB,:])
        gg=split_pair(grad_scr[start:start+QB,:])
        lse=jnp.concatenate([lse_ref[0,0:1,start:start+QB],lse_ref[0,1:2,start:start+QB]],axis=1)
        delta=jnp.concatenate([delta_all[0:1,start:start+QB],delta_all[1:2,start:start+QB]],axis=1)
        dq_t=jnp.zeros((128,2*QB),F32)
        def one(scores,vals):
            p=jnp.exp(scores-lse)
            dp=dot_nt(vals,gg)
            return p.astype(BF),(p*(dp-delta)).astype(BF)
        far=jnp.where(far_mask(pos,start),dot_nt(key_far,qq),NEG)
        p,ds=one(far,val_far)
        dv_far=dv_far+dot_nn(p,gg); dk_far=dk_far+dot_nn(ds,qq)
        dq_t=dq_t+dot_nn(key_far_t,ds)
        parts=masked_scores(dot_nt(k_ref[lo:hi,:],qq),start,length,low_ok,high_ok)
        plist=[];dlist=[]
        for n,part in enumerate(parts):
            a=lo+n*QB
            p,ds=one(part,v_ref[a:a+QB,:])
            plist.append(p);dlist.append(ds)
        p=jnp.concatenate(plist,axis=0); ds=jnp.concatenate(dlist,axis=0)
        dv_acc[lo:hi,:]+=dot_nn(p,gg)
        dk_acc[lo:hi,:]+=dot_nn(ds,qq)
        dq_t=dq_t+dot_nn(key_t[:,lo:hi],ds)
        dq_ref[start:start+QB,:]=pick_head(dq_t).T.astype(BF)
    dk_ref[...]=(dk_acc[...]+lax.dot_general(sel_full,dk_far,(((0,),(0,)),((),())),preferred_element_type=F32,precision=lax.Precision.HIGHEST)).astype(BF)
    dv_ref[...]=(dv_acc[...]+lax.dot_general(sel_full,dv_far,(((0,),(0,)),((),())),preferred_element_type=F32,precision=lax.Precision.HIGHEST)).astype(BF)

def attn_bwd(pos,q,k,v,grad,ctx,lse):
    length,width=q.shape
    pairs=width//128
    col=pl.BlockSpec((length,128),lambda i:(0,i))
    out=jax.ShapeDtypeStruct((length,width),BF)
    return pl.pallas_call(bwd_kernel,grid=(pairs,),
        in_specs=[pl.BlockSpec((16,1),lambda i:(0,0)),col,col,col,col,col,pl.BlockSpec((1,8,length),lambda i:(i,0,0))],
        out_specs=[col,col,col],
        out_shape=[out,out,out],
        scratch_shapes=[pltpu.VMEM((length,128),F32),pltpu.VMEM((length,128),F32),pltpu.VMEM((length,128),BF)],
        compiler_params=pltpu.CompilerParams(vmem_limit_bytes=32<<20),
        cost_estimate=pl.CostEstimate(flops=int(40e9),bytes_accessed=12<<20,transcendentals=8<<20),
        name="attend_back")(pos,q,k,v,grad,ctx,lse)


def sequence_step(x, positions, upstream_low, weights):
    w_local, w_global, w_out, b_proj, gains, shifts, w_in, c_in, w_back = weights
    length, width = x.shape
    glob_count = positions.shape[0]
    scale = HEAD_DIM ** (-0.5)
    bias = b_proj.astype(F32)
    gain = gains.astype(F32)
    shift = shifts.astype(F32)
    pos16 = jnp.full((16, 1), -1, jnp.int32).at[:glob_count, 0].set(positions)
    q = ((mm(x, w_local[0]) + bias[0]) * scale).astype(BF)
    k = mm(x, w_local[1]).astype(BF)
    v = (mm(x, w_local[2]) + bias[1]).astype(BF)
    ctx_loc, lse = attn_fwd(pos16, q, k, v)
    places = jnp.arange(length, dtype=jnp.int32)
    select = positions[:, None] == places[None, :]
    select_low = select.astype(BF)
    is_glob = jnp.any(select, axis=0)[:, None]
    rows_glob = mm(select_low, x).astype(BF)
    head_of = jnp.arange(width, dtype=jnp.int32) // HEAD_DIM
    own = head_of[None, :] == jnp.arange(16, dtype=jnp.int32)[:, None]

    def spread(rows):
        return jnp.where(own[None], rows[:, None, :], 0).reshape(-1, width)

    def gather(rows):
        return jnp.sum(jnp.where(own[None], rows.reshape(glob_count, 16, width), 0), axis=1)

    qg = ((mm(rows_glob, w_global[0]) + bias[2]) * scale).astype(BF)
    q_spread = spread(qg)
    key_map = mm_nt(w_global[1], q_spread).astype(BF)
    glob_scores = mm(x, key_map)
    glob_probs = jax.nn.softmax(glob_scores, axis=0)
    glob_low = glob_probs.astype(BF)
    mixed = mm_tn(glob_low, x)
    glob_mass = jnp.sum(glob_low.astype(F32), axis=0)
    ctx_glob = gather(mm(mixed.astype(BF), w_global[2]) + glob_mass[:, None] * bias[3])
    ctx_glob = ctx_glob.astype(BF)
    merged = jnp.where(is_glob, mm_tn(select_low, ctx_glob).astype(BF), ctx_loc)
    attended = mm(merged, w_out) + bias[4]
    normed_one, inverse_one = normalize(x.astype(F32) + attended)
    first_norm = normed_one * gain[0] + shift[0]
    first_low = first_norm.astype(BF)
    inner = mm(first_low, w_in) + c_in.astype(F32)
    act, slope = gelu_pair(inner)
    active = act.astype(BF)
    normed_two, inverse_two = normalize(first_norm + (mm(active, w_back) + bias[5]))
    result = normed_two * gain[1] + shift[1]
    upstream = upstream_low.astype(F32)
    grad_gain_two = jnp.sum(upstream * normed_two, axis=0)
    grad_shift_two = jnp.sum(upstream, axis=0)
    grad_second = norm_back(upstream * gain[1], normed_two, inverse_two)
    branch_grad = grad_second.astype(BF)
    grad_back_w = mm_tn(active, branch_grad)
    grad_out_bias = jnp.sum(branch_grad.astype(F32), axis=0)
    inner_grad = (mm_nt(branch_grad, w_back) * slope).astype(BF)
    grad_in_w = mm_tn(first_low, inner_grad)
    grad_in_bias = jnp.sum(inner_grad.astype(F32), axis=0)
    grad_first = grad_second + mm_nt(inner_grad, w_in)
    grad_gain_one = jnp.sum(grad_first * normed_one, axis=0)
    grad_shift_one = jnp.sum(grad_first, axis=0)
    grad_sum_one = norm_back(grad_first * gain[0], normed_one, inverse_one)
    attn_grad = grad_sum_one.astype(BF)
    grad_out_w = mm_tn(merged, attn_grad)
    grad_att_bias = jnp.sum(attn_grad.astype(F32), axis=0)
    ctx_grad = mm_nt(attn_grad, w_out).astype(BF)
    dq, dk, dv = attn_bwd(pos16, q, k, v, ctx_grad, merged, lse)
    pre_query = dq * scale
    glob_ctx_grad = mm(select_low, ctx_grad).astype(BF)
    c_spread = spread(glob_ctx_grad)
    value_map = mm_nt(w_global[2], c_spread).astype(BF)
    glob_grad_probs = mm(x, value_map) + mm_nt(bias[3:4].astype(BF), c_spread)
    glob_dot = jnp.sum(glob_probs * glob_grad_probs, axis=0, keepdims=True)
    glob_ds = (glob_probs * (glob_grad_probs - glob_dot)).astype(BF)
    key_mixed = mm_tn(glob_ds, x)
    dqg = gather(mm(key_mixed.astype(BF), w_global[1])).astype(BF)
    glob_pre = dqg * scale
    token_grad = (
        grad_sum_one
        + mm_nt(pre_query, w_local[0])
        + mm_nt(dk, w_local[1])
        + mm_nt(dv, w_local[2])
        + mm_nt(glob_ds, key_map)
        + mm_nt(glob_low, value_map)
    )
    rows_grad = mm_nt(glob_pre, w_global[0])
    token_grad = token_grad + mm_tn(select.astype(F32), rows_grad)
    grad_local = jnp.stack([mm_tn(x, pre_query), mm_tn(x, dk), mm_tn(x, dv)])
    grad_global = jnp.stack(
        [
            mm_tn(rows_glob, glob_pre),
            mm_tn(key_mixed.astype(BF), q_spread),
            mm_tn(mixed.astype(BF), c_spread),
        ]
    )

    def total_of(value):
        return jnp.sum(value.astype(F32), axis=0)

    grad_bias = jnp.stack(
        [
            total_of(pre_query),
            total_of(dv),
            total_of(glob_pre),
            jnp.sum(glob_mass[:, None] * c_spread.astype(F32), axis=0),
            grad_att_bias,
            grad_out_bias,
        ]
    )
    grad_gain = jnp.stack([grad_gain_one, grad_gain_two])
    grad_shift = jnp.stack([grad_shift_one, grad_shift_two])
    return (
        result.astype(BF),
        token_grad.astype(BF),
        (
            grad_local,
            grad_global,
            grad_out_w,
            grad_bias,
            grad_gain,
            grad_shift,
            grad_in_w,
            grad_in_bias,
            grad_back_w,
        ),
    )


def log2_of(count):
    return count.bit_length() - 1


def flip(value, axis, bit):
    count = lax.axis_size(axis)
    return lax.ppermute(value, axis, [(index, index ^ bit) for index in range(count)])


def after(value, *others):
    return lax.optimization_barrier((value,) + others)[0]


def spread_slots(unit, order):
    slots = {0: unit}
    levels = []
    for bit in order:
        for slot in list(slots):
            slots[slot | bit] = flip(slots[slot], "fsdp", bit)
        levels.append(slots[bit])
    return ([slots[slot] for slot in range(len(slots))], slots)


def assemble(pieces, parts, axis="fsdp"):
    count = len(pieces)
    width = pieces[0].shape[-1]

    def body(*refs):
        ins = refs[:count]
        outs = refs[count : count + len(parts)]
        sems = refs[-1]
        me = lax.axis_index(axis)
        copies = []
        for slot in range(count):
            place = me ^ slot
            for part, (first, planes, rows) in enumerate(parts):
                for plane in range(planes):
                    copies.append(
                        pltpu.make_async_copy(
                            ins[slot].at[pl.ds(first + plane * rows, rows)],
                            outs[part].at[plane, pl.ds(pl.multiple_of(place * rows, rows), rows)],
                            sems.at[len(copies)],
                        )
                    )
        for copy in copies:
            copy.start()
        for copy in copies:
            copy.wait()

    total = count * sum(planes for _, planes, _ in parts)
    size = sum(count * planes * rows for _, planes, rows in parts) * width * 2
    return pl.pallas_call(
        body,
        in_specs=[pl.BlockSpec(memory_space=pl.ANY)] * count,
        out_specs=[pl.BlockSpec(memory_space=pl.ANY)] * len(parts),
        out_shape=[
            jax.ShapeDtypeStruct((planes, count * rows, width), pieces[0].dtype)
            for _, planes, rows in parts
        ],
        scratch_shapes=[pltpu.SemaphoreType.DMA((total,))],
        cost_estimate=pl.CostEstimate(flops=0, bytes_accessed=2 * size, transcendentals=0),
        name="assemble",
    )(*pieces)


def reduce_to_owner(grads, order):
    count = lax.axis_size("fsdp")
    bits = log2_of(count)
    me = lax.axis_index("fsdp")
    grads = grads.reshape((2,) * bits + grads.shape[1:])
    alive = list(range(bits - 1, -1, -1))
    for bit in order:
        place = alive.index(log2_of(bit))
        alive.pop(place)
        mine = (me >> log2_of(bit)) & 1
        send = lax.dynamic_index_in_dim(grads, 1 - mine, place, keepdims=False).astype(BF)
        keep = lax.dynamic_index_in_dim(grads, mine, place, keepdims=False).astype(F32)
        grads = keep + flip(send, "fsdp", bit).astype(F32)
    return grads


def sum_over_sp(value):
    me = lax.axis_index("sp")
    value = value.reshape((2, 2) + (value.shape[0] // 4,) + value.shape[1:])
    low, high = me & 1, me >> 1
    send = lax.dynamic_index_in_dim(value, 1 - low, 0, keepdims=False).astype(BF)
    keep = lax.dynamic_index_in_dim(value, low, 0, keepdims=False)
    value = keep + flip(send, "sp", 1).astype(F32)
    send = lax.dynamic_index_in_dim(value, 1 - high, 0, keepdims=False).astype(BF)
    keep = lax.dynamic_index_in_dim(value, high, 0, keepdims=False)
    mine = (keep + flip(send, "sp", 2).astype(F32)).astype(BF)
    other = flip(mine, "sp", 2)
    pair = jnp.stack([jnp.where(high == 0, mine, other), jnp.where(high == 0, other, mine)])
    there = flip(pair, "sp", 1)
    both = jnp.stack([jnp.where(low == 0, pair, there), jnp.where(low == 0, there, pair)])
    return both.reshape((-1,) + both.shape[3:]).astype(F32)


def per_device(
    inputs,
    global_pos,
    w_local,
    w_global,
    w_out,
    b_proj,
    gains,
    shifts,
    w_in,
    c_in,
    w_back,
    cotangent,
):
    sp_count = lax.axis_size("sp")
    fsdp_count = lax.axis_size("fsdp")
    sp_index = lax.axis_index("sp")
    own_seqs = inputs.shape[0] // sp_count
    shard = w_out.shape[0]
    width = w_out.shape[1]
    ff_shard = w_back.shape[0]
    ff_width = w_in.shape[1]
    tree = fsdp_count == 8 and sp_count == 4 and shard % 32 == 0

    def to_sequence(value):
        if own_seqs == 1:
            moved = lax.all_to_all(value, "sp", split_axis=0, concat_axis=0)
            return moved.reshape(1, -1, width)
        return lax.all_to_all(value, "sp", split_axis=0, concat_axis=1, tiled=True)

    def to_tokens(values):
        if own_seqs == 1:
            return lax.all_to_all(
                values[0].reshape(sp_count, -1, width), "sp", split_axis=0, concat_axis=0
            )
        return lax.all_to_all(jnp.stack(values), "sp", split_axis=1, concat_axis=0, tiled=True)

    own_pos = lax.dynamic_slice_in_dim(global_pos, sp_index * own_seqs, own_seqs, 0)
    small = jnp.concatenate(
        [b_proj.reshape(-1), gains.reshape(-1), shifts.reshape(-1), c_in.reshape(-1)]
    )
    small_rows = 16 * -(-small.shape[0] // (16 * width))
    small = jnp.pad(small, (0, small_rows * width - small.shape[0])).reshape(small_rows, width)
    x_all = to_sequence(inputs)
    if tree:
        first = w_local.reshape(-1, width)
        second = jnp.concatenate([w_global.reshape(-1, width), w_out, small], axis=0)
        slots_one, by_bit = spread_slots(first, (2, 4, 1))
        slots_two, _ = spread_slots(second, (4, 2, 1))
        mark = by_bit[4]
        third, fourth, mark = lax.optimization_barrier((w_in, w_back, mark))
        slots_three, _ = spread_slots(third, (2, 4, 1))
        slots_four, _ = spread_slots(fourth, (4, 2, 1))
        (full_local,) = assemble(slots_one, [(0, 3, shard)])
        full_global, full_out, small_all = assemble(
            slots_two, [(0, 3, shard), (3 * shard, 1, shard), (4 * shard, 1, small_rows)]
        )
        (full_in,) = assemble(slots_three, [(0, 1, shard)])
        (full_back,) = assemble(slots_four, [(0, 1, ff_shard)])
        full_out, full_in, full_back = full_out[0], full_in[0], full_back[0]
    else:
        full_local = lax.all_gather(w_local, "fsdp", axis=1, tiled=True)
        full_global = lax.all_gather(w_global, "fsdp", axis=1, tiled=True)
        full_out = lax.all_gather(w_out, "fsdp", axis=0, tiled=True)
        full_in = lax.all_gather(w_in, "fsdp", axis=0, tiled=True)
        full_back = lax.all_gather(w_back, "fsdp", axis=0, tiled=True)
        small_all = lax.all_gather(small, "fsdp")
    up_all = to_sequence(after(cotangent, x_all))
    small_all = small_all.reshape(fsdp_count, -1)

    def vectors(start, count):
        taken = small_all[:, start : start + count * shard].reshape(fsdp_count, count, shard)
        return taken.transpose(1, 0, 2).reshape(count, fsdp_count * shard)

    weights = (
        full_local,
        full_global,
        full_out,
        vectors(0, 6),
        vectors(6 * shard, 2),
        vectors(8 * shard, 2),
        full_in,
        small_all[:, 10 * shard : 10 * shard + ff_shard].reshape(-1),
        full_back,
    )
    results = []
    token_grads = []
    totals = None
    for index in range(own_seqs):
        result, token_grad, grads = sequence_step(
            x_all[index], own_pos[index], up_all[index], weights
        )
        results.append(result)
        token_grads.append(token_grad)
        totals = grads if totals is None else tuple(a + b for a, b in zip(totals, grads))
    out = to_tokens(results)
    grad_inputs = to_tokens(token_grads)
    g_local, g_global, g_out, g_bias, g_gain, g_shift, g_in, g_c, g_back = totals

    def cols(value):
        return value.reshape(-1, fsdp_count, shard).transpose(1, 0, 2).reshape(fsdp_count, -1)

    g_small = jnp.concatenate(
        [cols(g_bias), cols(g_gain), cols(g_shift), g_c.reshape(fsdp_count, ff_shard)], axis=1
    )
    g_small = jnp.pad(g_small, ((0, 0), (0, small_rows * width - g_small.shape[1])))

    def owned(value):
        planes, rows, columns = value.shape
        split = value.reshape(planes, fsdp_count, rows // fsdp_count, columns)
        return split.transpose(1, 0, 2, 3).reshape(fsdp_count, -1, columns)

    units = [
        (g_back.reshape(fsdp_count, ff_shard, width), (1, 2, 4)),
        (g_in.reshape(fsdp_count, shard, ff_width), (1, 4, 2)),
        (
            jnp.concatenate(
                [
                    owned(g_global),
                    g_out.reshape(fsdp_count, shard, width),
                    g_small.reshape(fsdp_count, small_rows, width),
                ],
                axis=1,
            ),
            (1, 2, 4),
        ),
        (owned(g_local), (1, 4, 2)),
    ]
    summed = []
    for unit, order in units:
        if tree:
            summed.append(sum_over_sp(reduce_to_owner(unit, order)))
        else:
            mine = lax.psum_scatter(unit.astype(BF), "fsdp", scatter_dimension=0, tiled=False)
            summed.append(lax.psum(mine, "sp").astype(F32))
    s_back, s_in, s_mixed, s_local = summed
    small_sum = s_mixed[4 * shard :].reshape(-1)
    return (
        out,
        grad_inputs,
        s_local.reshape(3, shard, width),
        s_mixed[: 3 * shard].reshape(3, shard, width),
        s_mixed[3 * shard : 4 * shard],
        small_sum[: 6 * shard].reshape(6, shard),
        small_sum[6 * shard : 8 * shard].reshape(2, shard),
        small_sum[8 * shard : 10 * shard].reshape(2, shard),
        s_in,
        small_sum[10 * shard : 10 * shard + ff_shard],
        s_back,
    )


def solution(mesh):
    rows = P("fsdp", None)
    tokens = P("fsdp", "sp", None)
    columns = P(None, "fsdp")
    stacked = P(None, "fsdp", None)
    return jax.shard_map(
        per_device,
        mesh=mesh,
        in_specs=(
            tokens,
            rows,
            stacked,
            stacked,
            rows,
            columns,
            columns,
            columns,
            rows,
            P("fsdp"),
            rows,
            tokens,
        ),
        out_specs=(
            tokens,
            tokens,
            stacked,
            stacked,
            rows,
            columns,
            columns,
            columns,
            rows,
            P("fsdp"),
            rows,
        ),
        check_vma=False,
    )
```

```python
import jax
import jax.numpy as jnp
from jax import lax
from jax.experimental import pallas as pl
from jax.experimental.pallas import tpu as pltpu
from jax.sharding import PartitionSpec as P

HEADS = 12
HEAD_DIM = 64
WIN = 256
QB = 128
NEG = -1e9
NORM_EPS = 1e-05
BF = jnp.bfloat16
F32 = jnp.float32
S = jax.ShapeDtypeStruct


def dot_nn(a,b): return jnp.dot(a,b,preferred_element_type=F32)
def dot_nt(a,b): return lax.dot_general(a,b,(((1,),(1,)),((),())),preferred_element_type=F32)
def dot_tn(a,b): return lax.dot_general(a,b,(((0,),(0,)),((),())),preferred_element_type=F32)

def split_pair(block):
    lane=lax.broadcasted_iota(jnp.int32,block.shape,1)
    zero=jnp.zeros_like(block)
    return jnp.concatenate([jnp.where(lane<HEAD_DIM,block,zero),jnp.where(lane<HEAD_DIM,zero,block)],axis=0)

def far_mask(pos, start):
    place=start+lax.broadcasted_iota(jnp.int32,(16,2*QB),1)%QB
    return (pos>=0)&(jnp.abs(place-pos)>WIN)

def edge_masks():
    row=lax.broadcasted_iota(jnp.int32,(QB,2*QB),0)
    col=lax.broadcasted_iota(jnp.int32,(QB,2*QB),1)%QB
    return row>=col, row<=col

def key_range(start,length):
    return max(0,start-WIN), min(length,start+QB+WIN)

def pick_head(both):
    row=lax.broadcasted_iota(jnp.int32,(2*HEAD_DIM,QB),0)
    return jnp.where(row<HEAD_DIM,both[:,:QB],both[:,QB:])

def masked_scores(raw,start,length,low_ok,high_ok):
    lo,hi=key_range(start,length)
    parts=[]
    for first in range(lo,hi,QB):
        chunk=raw[first-lo:first-lo+QB]
        if first==start-WIN: chunk=jnp.where(low_ok,chunk,NEG)
        elif first==start+WIN: chunk=jnp.where(high_ok,chunk,NEG)
        parts.append(chunk)
    return parts

def fwd_kernel(pos_ref,q_ref,k_ref,v_ref,ctx_ref,lse_ref):
    length=q_ref.shape[0]
    pos=pos_ref[...]
    token=lax.broadcasted_iota(jnp.int32,(16,length),1)
    sel=jnp.where(token==pos,1.0,0.0).astype(BF)
    key_far=dot_nn(sel,k_ref[...]).astype(BF)
    val_far_t=dot_nn(sel,v_ref[...]).astype(BF).T
    val_t=v_ref[...].T
    low_ok,high_ok=edge_masks()
    for start in range(0,length,QB):
        lo,hi=key_range(start,length)
        qq=split_pair(q_ref[start:start+QB,:])
        raw=dot_nt(k_ref[lo:hi,:],qq)
        parts=masked_scores(raw,start,length,low_ok,high_ok)
        far=jnp.where(far_mask(pos,start),dot_nt(key_far,qq),NEG)
        top=jnp.max(far,axis=0,keepdims=True)
        for part in parts: top=jnp.maximum(top,jnp.max(part,axis=0,keepdims=True))
        far_p=jnp.exp(far-top)
        total=jnp.sum(far_p,axis=0,keepdims=True)
        probs=[]
        for part in parts:
            p=jnp.exp(part-top)
            total=total+jnp.sum(p,axis=0,keepdims=True)
            probs.append(p.astype(BF))
        both=dot_nn(val_t[:,lo:hi],jnp.concatenate(probs,axis=0))+dot_nn(val_far_t,far_p.astype(BF))
        both=both*(1.0/total)
        ctx_ref[start:start+QB,:]=pick_head(both).T.astype(BF)
        lse=top+jnp.log(total)
        lse_ref[0,0:1,start:start+QB]=lse[:,:QB]
        lse_ref[0,1:2,start:start+QB]=lse[:,QB:]

def attn_fwd(pos,q,k,v):
    length,width=q.shape
    pairs=width//128
    col=pl.BlockSpec((length,128),lambda i:(0,i))
    return pl.pallas_call(fwd_kernel,grid=(pairs,),
        in_specs=[pl.BlockSpec((16,1),lambda i:(0,0)),col,col,col],
        out_specs=[col,pl.BlockSpec((1,8,length),lambda i:(i,0,0))],
        out_shape=[jax.ShapeDtypeStruct((length,width),BF),jax.ShapeDtypeStruct((pairs,8,length),F32)],
        compiler_params=pltpu.CompilerParams(vmem_limit_bytes=32<<20),
        cost_estimate=pl.CostEstimate(flops=int(20e9),bytes_accessed=8<<20,transcendentals=8<<20),
        name="attend")(pos,q,k,v)

def bwd_kernel(pos_ref,q_ref,k_ref,v_ref,g_ref,ctx_ref,lse_ref,dq_ref,dk_ref,dv_ref,dk_acc,dv_acc,grad_scr):
    length=q_ref.shape[0]
    pos=pos_ref[...]
    token=lax.broadcasted_iota(jnp.int32,(16,length),1)
    sel_bool=token==pos
    sel=jnp.where(sel_bool,1.0,0.0).astype(BF)
    sel_full=jnp.where(sel_bool,1.0,0.0)
    key_far=dot_nn(sel,k_ref[...]).astype(BF)
    val_far=dot_nn(sel,v_ref[...]).astype(BF)
    key_far_t=key_far.T
    key_t=k_ref[...].T
    ones=jnp.ones((16,128),F32)
    is_glob=lax.dot_general(sel_full,ones,(((0,),(0,)),((),())),preferred_element_type=F32)
    grad_scr[...]=jnp.where(is_glob>0.5,0.0,g_ref[...].astype(F32)).astype(BF)
    prod=grad_scr[...].astype(F32)*ctx_ref[...].astype(F32)
    hrow=lax.broadcasted_iota(jnp.int32,(16,128),0)
    hlane=lax.broadcasted_iota(jnp.int32,(16,128),1)//HEAD_DIM
    hsel=jnp.where(hrow==hlane,1.0,0.0)
    delta_all=lax.dot_general(hsel,prod,(((1,),(1,)),((),())),preferred_element_type=F32,precision=lax.Precision.HIGHEST)
    dk_acc[...]=jnp.zeros_like(dk_acc)
    dv_acc[...]=jnp.zeros_like(dv_acc)
    dk_far=jnp.zeros((16,128),F32); dv_far=jnp.zeros((16,128),F32)
    low_ok,high_ok=edge_masks()
    for start in range(0,length,QB):
        lo,hi=key_range(start,length)
        qq=split_pair(q_ref[start:start+QB,:])
        gg=split_pair(grad_scr[start:start+QB,:])
        lse=jnp.concatenate([lse_ref[0,0:1,start:start+QB],lse_ref[0,1:2,start:start+QB]],axis=1)
        delta=jnp.concatenate([delta_all[0:1,start:start+QB],delta_all[1:2,start:start+QB]],axis=1)
        dq_t=jnp.zeros((128,2*QB),F32)
        def one(scores,vals):
            p=jnp.exp(scores-lse)
            dp=dot_nt(vals,gg)
            return p.astype(BF),(p*(dp-delta)).astype(BF)
        far=jnp.where(far_mask(pos,start),dot_nt(key_far,qq),NEG)
        p,ds=one(far,val_far)
        dv_far=dv_far+dot_nn(p,gg); dk_far=dk_far+dot_nn(ds,qq)
        dq_t=dq_t+dot_nn(key_far_t,ds)
        parts=masked_scores(dot_nt(k_ref[lo:hi,:],qq),start,length,low_ok,high_ok)
        plist=[];dlist=[]
        for n,part in enumerate(parts):
            a=lo+n*QB
            p,ds=one(part,v_ref[a:a+QB,:])
            plist.append(p);dlist.append(ds)
        p=jnp.concatenate(plist,axis=0); ds=jnp.concatenate(dlist,axis=0)
        dv_acc[lo:hi,:]+=dot_nn(p,gg)
        dk_acc[lo:hi,:]+=dot_nn(ds,qq)
        dq_t=dq_t+dot_nn(key_t[:,lo:hi],ds)
        dq_ref[start:start+QB,:]=(pick_head(dq_t).T.astype(BF).astype(F32)*(HEAD_DIM**-0.5)).astype(BF)
    dk_ref[...]=(dk_acc[...]+lax.dot_general(sel_full,dk_far,(((0,),(0,)),((),())),preferred_element_type=F32,precision=lax.Precision.HIGHEST)).astype(BF)
    dv_ref[...]=(dv_acc[...]+lax.dot_general(sel_full,dv_far,(((0,),(0,)),((),())),preferred_element_type=F32,precision=lax.Precision.HIGHEST)).astype(BF)

def attn_bwd(pos,q,k,v,grad,ctx,lse):
    length,width=q.shape
    pairs=width//128
    col=pl.BlockSpec((length,128),lambda i:(0,i))
    out=jax.ShapeDtypeStruct((length,width),BF)
    return pl.pallas_call(bwd_kernel,grid=(pairs,),
        in_specs=[pl.BlockSpec((16,1),lambda i:(0,0)),col,col,col,col,col,pl.BlockSpec((1,8,length),lambda i:(i,0,0))],
        out_specs=[col,col,col],
        out_shape=[out,out,out],
        scratch_shapes=[pltpu.VMEM((length,128),F32),pltpu.VMEM((length,128),F32),pltpu.VMEM((length,128),BF)],
        compiler_params=pltpu.CompilerParams(vmem_limit_bytes=32<<20),
        cost_estimate=pl.CostEstimate(flops=int(40e9),bytes_accessed=12<<20,transcendentals=8<<20),
        name="attend_back")(pos,q,k,v,grad,ctx,lse)


ANY=pl.BlockSpec(memory_space=pl.ANY)
SMEM=pl.BlockSpec(memory_space=pltpu.SMEM)
RB=256

def cost(flops,nbytes,trans=0):
    return pl.CostEstimate(flops=int(flops),bytes_accessed=int(nbytes),transcendentals=int(trans))

def params(mib=60):
    return pltpu.CompilerParams(vmem_limit_bytes=mib<<20)

def fetches(pieces,place,sems,me,first,rows,sem0):
    out=[]
    for slot,piece in enumerate(pieces):
        owner=me^slot
        out.append(pltpu.make_async_copy(piece.at[pl.ds(first,rows)],place.at[pl.ds(pl.multiple_of(owner*rows,rows),rows)],sems.at[sem0+slot]))
    return out

def stats(value):
    center=value-jnp.mean(value,axis=-1,keepdims=True)
    inverse=lax.rsqrt(jnp.mean(center*center,axis=-1,keepdims=True)+NORM_EPS)
    return center*inverse,inverse

def norm_back(scaled,normed,inverse):
    return inverse*(scaled-jnp.mean(scaled,axis=-1,keepdims=True)-normed*jnp.mean(scaled*normed,axis=-1,keepdims=True))

def gelu_pair(inner):
    cdf=0.5*(1.0+lax.erf(inner*0.7071067811865476))
    return inner*cdf, cdf+inner*(0.3989422804014327*jnp.exp(-0.5*inner*inner))

def ffn_up(me,pos,ctx,ctxg,x,mixed_pieces,in_pieces,vecs,c_row,out_first):
    length,width=x.shape
    n=len(in_pieces); shard=in_pieces[0].shape[0]; ff=in_pieces[0].shape[1]
    def body(me_ref,pos_ref,ctx_ref,glob_ref,x_ref,vec_ref,c_ref,*refs):
        outs_w=refs[:n]; ins_w=refs[n:2*n]
        hat_ref,inv_ref,low_ref,act_ref,slope_ref,merged_ref,wout,win,sems=refs[2*n:]
        @pl.when(pl.program_id(0)==0)
        def _():
            m=me_ref[0]
            cps=fetches(outs_w,wout,sems,m,out_first,shard,0)+fetches(ins_w,win,sems,m,0,shard,n)
            for c in cps: c.start()
            for c in cps: c.wait()
        token=pl.program_id(0)*RB+lax.broadcasted_iota(jnp.int32,(16,RB),1)
        hot=jnp.where(token==pos_ref[...],1.0,0.0).astype(BF)
        is_glob=dot_tn(hot,jnp.ones((16,128),BF))[:,0:1]>0.5
        merged=jnp.where(is_glob,dot_tn(hot,glob_ref[...]),ctx_ref[...].astype(F32)).astype(BF)
        merged_ref[...]=merged
        attended=dot_nn(merged,wout[...])+vec_ref[4:5,:]
        hat,inv=stats(x_ref[...].astype(F32)+attended)
        hat_ref[...]=hat; inv_ref[...]=inv
        low=(hat*vec_ref[6:7,:]+vec_ref[8:9,:]).astype(BF)
        low_ref[...]=low
        for a in range(0,ff,768):
            inner=dot_nn(low,win[:,a:a+768])+c_ref[:,a:a+768]
            act,slope=gelu_pair(inner)
            act_ref[:,a:a+768]=act.astype(BF); slope_ref[:,a:a+768]=slope.astype(BF)
    blk=lambda w:pl.BlockSpec((RB,w),lambda i:(i,0))
    full=lambda s:pl.BlockSpec(s,lambda i:(0,0))
    return pl.pallas_call(body,grid=(length//RB,),
        in_specs=[SMEM,full(pos.shape),blk(width),full(ctxg.shape),blk(width),full(vecs.shape),full(c_row.shape)]+[ANY]*(2*n),
        out_specs=[blk(width),blk(1),blk(width),blk(ff),blk(ff),blk(width)],
        out_shape=[jax.ShapeDtypeStruct((length,width),F32),jax.ShapeDtypeStruct((length,1),F32),jax.ShapeDtypeStruct((length,width),BF),
                   jax.ShapeDtypeStruct((length,ff),BF),jax.ShapeDtypeStruct((length,ff),BF),jax.ShapeDtypeStruct((length,width),BF)],
        scratch_shapes=[pltpu.VMEM((width,width),BF),pltpu.VMEM((width,ff),BF),pltpu.SemaphoreType.DMA((2*n,))],
        compiler_params=params(),cost_estimate=cost(2*length*width*(width+ff),24<<20,2*length*ff),name="ffn_up")(me,pos,ctx,ctxg,x,vecs,c_row,*mixed_pieces,*in_pieces)

def ffn_back(me,active,slope,hat1,inv1,upstream,mixed_pieces,in_pieces,back_pieces,vecs,out_first):
    length,width=hat1.shape
    n=len(in_pieces); shard=in_pieces[0].shape[0]; ff=in_pieces[0].shape[1]; ffs=back_pieces[0].shape[0]
    def body(me_ref,act_ref,slope_ref,hat_ref,inv_ref,up_ref,vec_ref,*refs):
        outs_w=refs[:n]; ins_w=refs[n:2*n]; backs_w=refs[2*n:3*n]
        out_ref,bg_ref,ig_ref,gs_ref,ag_ref,mg_ref,vg_ref,cg_ref,wout,win,wback,sems=refs[3*n:]
        m=me_ref[0]
        cb=fetches(backs_w,wback,sems,m,0,ffs,0)
        ci=fetches(ins_w,win,sems,m,0,shard,n)
        co=fetches(outs_w,wout,sems,m,out_first,shard,2*n)
        first=pl.program_id(0)==0
        @pl.when(first)
        def _():
            for c in cb+ci+co: c.start()
            vg_ref[...]=jnp.zeros_like(vg_ref); cg_ref[...]=jnp.zeros_like(cg_ref)
            for c in cb: c.wait()
        hat1v=hat_ref[...]
        norm1=hat1v*vec_ref[6:7,:]+vec_ref[8:9,:]
        branch=dot_nn(act_ref[...],wback[...])+vec_ref[5:6,:]
        hat2,inv2=stats(norm1+branch)
        out_ref[...]=(hat2*vec_ref[7:8,:]+vec_ref[9:10,:]).astype(BF)
        up=up_ref[...].astype(F32)
        col=lambda v:jnp.sum(v,axis=0,keepdims=True)
        vg_ref[7:8,:]+=col(up*hat2); vg_ref[9:10,:]+=col(up)
        second=norm_back(up*vec_ref[7:8,:],hat2,inv2)
        bg=second.astype(BF)
        bg_ref[...]=bg
        vg_ref[5:6,:]+=col(bg.astype(F32))
        @pl.when(first)
        def _():
            for c in ci+co: c.wait()
        acc=second
        for a in range(0,ff,768):
            ig=(dot_nt(bg,wback[a:a+768,:])*slope_ref[:,a:a+768].astype(F32)).astype(BF)
            ig_ref[:,a:a+768]=ig
            cg_ref[:,a:a+768]+=col(ig.astype(F32))
            acc=acc+dot_nt(ig,win[:,a:a+768])
        vg_ref[6:7,:]+=col(acc*hat1v); vg_ref[8:9,:]+=col(acc)
        gs=norm_back(acc*vec_ref[6:7,:],hat1v,inv_ref[...])
        gs_ref[...]=gs
        ag=gs.astype(BF)
        ag_ref[...]=ag
        vg_ref[4:5,:]+=col(ag.astype(F32))
        mg_ref[...]=dot_nt(ag,wout[...]).astype(BF)
    blk=lambda w:pl.BlockSpec((RB,w),lambda i:(i,0))
    full=lambda s:pl.BlockSpec(s,lambda i:(0,0))
    return pl.pallas_call(body,grid=(length//RB,),
        in_specs=[SMEM,blk(ff),blk(ff),blk(width),blk(1),blk(width),full(vecs.shape)]+[ANY]*(3*n),
        out_specs=[blk(width),blk(width),blk(ff),blk(width),blk(width),blk(width),full((16,width)),full((1,ff))],
        out_shape=[S((length,width),BF),S((length,width),BF),S((length,ff),BF),S((length,width),F32),S((length,width),BF),S((length,width),BF),S((16,width),F32),S((1,ff),F32)],
        scratch_shapes=[pltpu.VMEM((width,width),BF),pltpu.VMEM((width,ff),BF),pltpu.VMEM((ff,width),BF),pltpu.SemaphoreType.DMA((3*n,))],
        compiler_params=params(),cost_estimate=cost(2*length*width*(width+3*ff),40<<20),name="ffn_back")(me,active,slope,hat1,inv1,upstream,vecs,*mixed_pieces,*in_pieces,*back_pieces)

def grad_rows(me,left,right,bit,count=8):
    length,ff=left.shape; width=right.shape[1]; fs=ff//count
    def body(me_ref,l_ref,r_ref,o_ref):
        o_ref[0]=dot_tn(l_ref[...],r_ref[...]).astype(BF)
    return pl.pallas_call(body,
        grid_spec=pltpu.PrefetchScalarGridSpec(num_scalar_prefetch=1,grid=(count//2,),
            in_specs=[pl.BlockSpec((length,fs),lambda j,m:(0,m[0]^(2*j+bit))),pl.BlockSpec((length,width),lambda j,m:(0,0))],
            out_specs=pl.BlockSpec((1,fs,width),lambda j,m:(j,0,0))),
        out_shape=jax.ShapeDtypeStruct((count//2,fs,width),BF),
        compiler_params=params(),cost_estimate=cost(length*ff*width,10<<20),name="grad_rows")(me,left,right)

def grad_cols(me,left,rights,count=8,nb=768):
    length,width=left.shape; cols=rights[0].shape[1]; shard=width//count; half=count//2
    k=len(rights)
    steps=cols//nb
    def body(me_ref,l_ref,*refs):
        r_refs=refs[:k]; keep,send,lt,res=refs[k:]
        @pl.when(pl.program_id(0)==0)
        def _(): lt[...]=l_ref[...].T
        m=me_ref[0]
        for r in range(k):
            res[...]=dot_nn(lt[...],r_refs[r][...])
            for slot in range(count):
                o=keep if slot%2==0 else send
                o[slot//2,r*shard:(r+1)*shard,:]=res[pl.ds(pl.multiple_of((m^slot)*shard,shard),shard),:].astype(BF)
    o=jax.ShapeDtypeStruct((half,k*shard,cols),BF)
    return pl.pallas_call(body,grid=(steps,),
        in_specs=[SMEM,pl.BlockSpec((length,width),lambda i:(0,0))]+[pl.BlockSpec((length,nb),lambda i:(0,i))]*k,
        out_specs=[pl.BlockSpec((half,k*shard,nb),lambda i:(0,0,i))]*2,out_shape=[o,o],
        scratch_shapes=[pltpu.VMEM((width,length),BF),pltpu.VMEM((width,nb),F32)],
        compiler_params=params(),cost_estimate=cost(2*length*width*cols*k,12<<20),name="grad_cols")(me,left,*rights)


def project(me,x,pieces,vecs):
    length,width=x.shape; n=len(pieces); shard=width//n
    def body(me_ref,x_ref,vec_ref,*refs):
        ins=refs[:n]; q_ref,k_ref,v_ref,wts,sems=refs[n:]
        m=me_ref[0]
        cps=[fetches(ins,wts.at[j],sems,m,j*shard,shard,j*n) for j in range(3)]
        for j in range(3):
            for c in cps[j]: c.start()
        for c in cps[0]: c.wait()
        scale=HEAD_DIM**-0.5
        for a in range(0,length,RB):
            q_ref[a:a+RB,:]=((dot_nn(x_ref[a:a+RB,:],wts[0])+vec_ref[0:1,:])*scale).astype(BF)
        for c in cps[1]: c.wait()
        for a in range(0,length,RB):
            k_ref[a:a+RB,:]=dot_nn(x_ref[a:a+RB,:],wts[1]).astype(BF)
        for c in cps[2]: c.wait()
        for a in range(0,length,RB):
            v_ref[a:a+RB,:]=(dot_nn(x_ref[a:a+RB,:],wts[2])+vec_ref[1:2,:]).astype(BF)
    vm=pl.BlockSpec(memory_space=pltpu.VMEM)
    return pl.pallas_call(body,in_specs=[SMEM,vm,vm]+[ANY]*n,out_specs=[vm]*3,out_shape=[S((length,width),BF)]*3,
        scratch_shapes=[pltpu.VMEM((3,width,width),BF),pltpu.SemaphoreType.DMA((3*n,))],
        compiler_params=params(),cost_estimate=cost(6*length*width*width,10<<20),name="project")(me,x,vecs,*pieces)

def own_mask(width):
    return lax.broadcasted_iota(jnp.int32,(16,width),0)==lax.broadcasted_iota(jnp.int32,(16,width),1)//HEAD_DIM

def one_hot(pos,length):
    return jnp.where(lax.broadcasted_iota(jnp.int32,(16,length),1)==pos,1.0,0.0)

def scatter_heads(rows,own,count):
    zero=jnp.zeros((16,rows.shape[1]),F32)
    return jnp.concatenate([jnp.where(own,jnp.broadcast_to(rows[g:g+1,:].astype(F32),zero.shape),zero) for g in range(count)],axis=0).astype(BF)

def gather_heads(value,own,count):
    rows=[jnp.sum(jnp.where(own,value[16*g:16*g+16],0.0),axis=0,keepdims=True) for g in range(count)]
    rows.append(jnp.zeros((16-count,value.shape[1]),F32))
    return jnp.concatenate(rows,axis=0)

def globals_fwd(me,pos,x,pieces,vecs,count):
    length,width=x.shape; n=len(pieces); shard=width//n; wide=16*count
    def body(me_ref,pos_ref,x_ref,vec_ref,*refs):
        ins=refs[:n]; ctx_ref,p_ref,u_ref,y_ref,q_ref,r_ref,wts,sems=refs[n:]
        m=me_ref[0]
        cps=[fetches(ins,wts.at[j],sems,m,j*shard,shard,j*n) for j in range(3)]
        for j in range(3):
            for c in cps[j]: c.start()
        own=own_mask(width)
        sel=one_hot(pos_ref[...],length).astype(BF)
        rows=dot_nn(sel,x_ref[...]).astype(BF)
        r_ref[...]=rows
        for c in cps[0]: c.wait()
        q=((dot_nn(rows,wts[0])+vec_ref[2:3,:])*(HEAD_DIM**-0.5)).astype(BF)
        q_ref[...]=q
        for c in cps[1]: c.wait()
        u=dot_nt(wts[1],scatter_heads(q,own,count)).astype(BF)
        u_ref[...]=u
        s=dot_nn(x_ref[...],u)
        p=jnp.exp(s-jnp.max(s,axis=0,keepdims=True))
        p=p/jnp.sum(p,axis=0,keepdims=True)
        p_ref[...]=p
        low=p.astype(BF)
        y=dot_tn(low,x_ref[...]).astype(BF)
        y_ref[...]=y
        mass=dot_tn(low,jnp.ones((length,128),BF))[:,0:1]
        for c in cps[2]: c.wait()
        ctx_ref[...]=gather_heads(dot_nn(y,wts[2])+mass*vec_ref[3:4,:],own,count).astype(BF)
    vm=pl.BlockSpec(memory_space=pltpu.VMEM)
    return pl.pallas_call(body,in_specs=[SMEM,vm,vm,vm]+[ANY]*n,out_specs=[vm]*6,
        out_shape=[S((16,width),BF),S((length,wide),F32),S((width,wide),BF),S((wide,width),BF),S((16,width),BF),S((16,width),BF)],
        scratch_shapes=[pltpu.VMEM((3,width,width),BF),pltpu.SemaphoreType.DMA((3*n,))],
        compiler_params=params(),cost_estimate=cost(6e9,8<<20),name="globals")(me,pos,x,vecs,*pieces)

def globals_bwd(me,pos,x,mg,gs,p,u,y,q,rows,merged,ag,pieces,vecs,count):
    length,width=x.shape; n=len(pieces); shard=width//n; half=max(n//2,1)
    def body(me_ref,pos_ref,x_ref,mg_ref,gs_ref,p_ref,u_ref,y_ref,q_ref,r_ref,merged_ref,ag_ref,vec_ref,*refs):
        ins=refs[:n]; out_ref,keep,send,vg_ref,wts,res,sems=refs[n:]
        m=me_ref[0]
        cps=[fetches(ins,wts.at[j],sems,m,j*shard,shard,j*n) for j in range(3)]
        for j in (2,1,0):
            for c in cps[j]: c.start()
        own=own_mask(width)
        hot=one_hot(pos_ref[...],length)
        sel=hot.astype(BF)
        x=x_ref[...]
        cs=scatter_heads(dot_nn(sel,mg_ref[...]).astype(BF),own,count)
        qs=scatter_heads(q_ref[...],own,count)
        for c in cps[2]: c.wait()
        v=dot_nt(wts[2],cs).astype(BF)
        shift=dot_nt(jnp.broadcast_to(vec_ref[3:4,:],(16,width)).astype(BF),cs)[0:1,:]
        dp=dot_nn(x,v)+shift
        p=p_ref[...]
        low=p.astype(BF)
        ds=(p*(dp-jnp.sum(p*dp,axis=0,keepdims=True))).astype(BF)
        a=dot_tn(ds,x).astype(BF)
        for c in cps[1]: c.wait()
        pre=(gather_heads(dot_nn(a,wts[1]),own,count).astype(BF).astype(F32)*(HEAD_DIM**-0.5)).astype(BF)
        for c in cps[0]: c.wait()
        rows_grad=dot_nt(pre,wts[0])
        mass=dot_tn(low,jnp.ones((length,128),BF))[:,0:1]
        vg_ref[...]=jnp.zeros_like(vg_ref)
        vg_ref[2:3,:]=jnp.sum(pre.astype(F32),axis=0,keepdims=True)
        vg_ref[3:4,:]=jnp.sum(mass*cs.astype(F32),axis=0,keepdims=True)
        out_ref[...]=gs_ref[...]+dot_nt(ds,u_ref[...])+dot_nt(low,v)+lax.dot_general(hot,rows_grad,(((0,),(0,)),((),())),preferred_element_type=F32,precision=lax.Precision.HIGHEST)
        for j,(l,r) in enumerate(((r_ref[...],pre),(a,qs),(y_ref[...],cs),(merged_ref[...],ag_ref[...]))):
            res[...]=dot_tn(l,r)
            for slot in range(n):
                o=keep if slot%2==0 else send
                o[slot//2,j*shard:(j+1)*shard,:]=res[pl.ds(pl.multiple_of((m^slot)*shard,shard),shard),:].astype(BF)
    vm=pl.BlockSpec(memory_space=pltpu.VMEM)
    o=S((half,4*shard,width),BF)
    return pl.pallas_call(body,in_specs=[SMEM]+[vm]*12+[ANY]*n,out_specs=[vm]*4,
        out_shape=[S((length,width),F32),o,o,S((16,width),F32)],
        scratch_shapes=[pltpu.VMEM((3,width,width),BF),pltpu.VMEM((width,width),F32),pltpu.SemaphoreType.DMA((3*n,))],
        compiler_params=params(),cost_estimate=cost(10e9,16<<20),name="globals_back")(me,pos,x,mg,gs,p,u,y,q,rows,merged,ag,vecs,*pieces)

def inputs_back(me,gs,pq,dk,dv,pieces):
    length,width=gs.shape; n=len(pieces); shard=width//n
    def body(me_ref,gs_ref,q_ref,k_ref,v_ref,*refs):
        ins=refs[:n]; out_ref,vg_ref,wts,sems=refs[n:]
        m=me_ref[0]
        @pl.when(pl.program_id(0)==0)
        def _():
            cps=sum([fetches(ins,wts.at[j],sems,m,j*shard,shard,j*n) for j in range(3)],[])
            for c in cps: c.start()
            vg_ref[...]=jnp.zeros_like(vg_ref)
            for c in cps: c.wait()
        acc=gs_ref[...]+dot_nt(q_ref[...],wts[0])+dot_nt(k_ref[...],wts[1])+dot_nt(v_ref[...],wts[2])
        out_ref[...]=acc.astype(BF)
        vg_ref[0:1,:]+=jnp.sum(q_ref[...].astype(F32),axis=0,keepdims=True)
        vg_ref[1:2,:]+=jnp.sum(v_ref[...].astype(F32),axis=0,keepdims=True)
    blk=pl.BlockSpec((RB,width),lambda i:(i,0))
    return pl.pallas_call(body,grid=(length//RB,),in_specs=[SMEM]+[blk]*4+[ANY]*n,
        out_specs=[blk,pl.BlockSpec((16,width),lambda i:(0,0))],out_shape=[S((length,width),BF),S((16,width),F32)],
        scratch_shapes=[pltpu.VMEM((3,width,width),BF),pltpu.SemaphoreType.DMA((3*n,))],
        compiler_params=params(),cost_estimate=cost(6*length*width*width,14<<20),name="inputs_back")(me,gs,pq,dk,dv,*pieces)


def flip(value, axis, bit):
    count = lax.axis_size(axis)
    return lax.ppermute(value, axis, [(index, index ^ bit) for index in range(count)])


def tie(value, *others):
    return lax.optimization_barrier((value,) + others)[0]


def spread_slots(unit, order):
    slots = {0: unit}
    for bit in order:
        for slot in list(slots):
            slots[slot | bit] = flip(slots[slot], "fsdp", bit)
    return [slots[slot] for slot in range(len(slots))]


def add(one, two):
    return one.astype(F32) + two.astype(F32)


class Reduction:
    def __init__(self, keep, send, x_first):
        self.keep, self.got = keep, flip(send, "fsdp", 1)
        self.x_first = x_first

    def second(self):
        keep = self.keep.reshape((2, 2) + self.keep.shape[1:])
        got = self.got.reshape(keep.shape)
        if self.x_first:
            self.send = add(keep[:, 1], got[:, 1]).astype(BF)
            self.mine = add(keep[:, 0], got[:, 0])
        else:
            self.send = add(keep[1], got[1]).astype(BF)
            self.mine = add(keep[0], got[0])
        self.got = flip(self.send, "fsdp", 2 if self.x_first else 4)
        return self.send

    def third(self):
        self.send = add(self.mine[1], self.got[1]).astype(BF)
        self.mine = add(self.mine[0], self.got[0])
        self.got = flip(self.send, "fsdp", 4 if self.x_first else 2)
        return self.send

    def total(self):
        return add(self.mine, self.got)


def sum_over_sp(value):
    me = lax.axis_index("sp")
    value = value.reshape((2, 2) + (value.shape[0] // 4,) + value.shape[1:])
    low, high = me & 1, me >> 1
    send = lax.dynamic_index_in_dim(value, 1 - low, 0, keepdims=False).astype(BF)
    keep = lax.dynamic_index_in_dim(value, low, 0, keepdims=False)
    value = keep + flip(send, "sp", 1).astype(F32)
    send = lax.dynamic_index_in_dim(value, 1 - high, 0, keepdims=False).astype(BF)
    keep = lax.dynamic_index_in_dim(value, high, 0, keepdims=False)
    mine = (keep + flip(send, "sp", 2).astype(F32)).astype(BF)
    other = flip(mine, "sp", 2)
    pair = jnp.stack([jnp.where(high == 0, mine, other), jnp.where(high == 0, other, mine)])
    there = flip(pair, "sp", 1)
    both = jnp.stack([jnp.where(low == 0, pair, there), jnp.where(low == 0, there, pair)])
    return both.reshape((-1,) + both.shape[3:]).astype(F32)


def per_device(
    inputs,
    global_pos,
    w_local,
    w_global,
    w_out,
    b_proj,
    gains,
    shifts,
    w_in,
    c_in,
    w_back,
    cotangent,
):
    sp_count = lax.axis_size("sp")
    fsdp_count = lax.axis_size("fsdp")
    sp_index = lax.axis_index("sp")
    fsdp_index = lax.axis_index("fsdp")
    own_seqs = inputs.shape[0] // sp_count
    glob_count = global_pos.shape[1]
    shard, width = w_out.shape
    ff_shard = w_back.shape[0]
    ff_width = w_in.shape[1]
    tree = fsdp_count == 8 and sp_count == 4 and own_seqs == 1 and shard % 32 == 0

    def to_sequence(value):
        if own_seqs == 1:
            moved = lax.all_to_all(value, "sp", split_axis=0, concat_axis=0)
            return moved.reshape(1, -1, width)
        return lax.all_to_all(value, "sp", split_axis=0, concat_axis=1, tiled=True)

    def to_tokens(values):
        if own_seqs == 1:
            return lax.all_to_all(
                values[0].reshape(sp_count, -1, width), "sp", split_axis=0, concat_axis=0
            )
        return lax.all_to_all(jnp.stack(values), "sp", split_axis=1, concat_axis=0, tiled=True)

    own_pos = lax.dynamic_slice_in_dim(global_pos, sp_index * own_seqs, own_seqs, 0)
    small = jnp.concatenate(
        [b_proj.reshape(-1), gains.reshape(-1), shifts.reshape(-1), c_in.reshape(-1)]
    )
    small_rows = 16 * -(-small.shape[0] // (16 * width))
    small = jnp.pad(small, (0, small_rows * width - small.shape[0])).reshape(small_rows, width)
    x_all = to_sequence(inputs)
    if tree:
        me = fsdp_index.reshape(1).astype(jnp.int32)
        first = jnp.concatenate([w_local.reshape(-1, width), small], axis=0)
        second = jnp.concatenate([w_global.reshape(-1, width), w_out], axis=0)
        local_w = spread_slots(first, (2, 4, 1))
        mixed_w = spread_slots(second, (4, 2, 1))
        third, fourth, _ = lax.optimization_barrier((w_in, w_back, local_w[6]))
        in_w = spread_slots(third, (2, 4, 1))
        back_w = spread_slots(fourth, (4, 2, 1))
        small_all = jnp.stack([piece[3 * shard :] for piece in local_w])
        small_all = small_all[me[0] ^ jnp.arange(fsdp_count, dtype=jnp.int32)]
        out_first = 3 * shard
    else:
        me = jnp.zeros((1,), jnp.int32)
        local_w = [lax.all_gather(w_local, "fsdp", axis=1, tiled=True).reshape(-1, width)]
        full_global = lax.all_gather(w_global, "fsdp", axis=1, tiled=True).reshape(-1, width)
        full_out = lax.all_gather(w_out, "fsdp", axis=0, tiled=True)
        mixed_w = [jnp.concatenate([full_global, full_out], axis=0)]
        in_w = [lax.all_gather(w_in, "fsdp", axis=0, tiled=True)]
        back_w = [lax.all_gather(w_back, "fsdp", axis=0, tiled=True)]
        small_all = lax.all_gather(small, "fsdp")
        out_first = 3 * width
    up_all = to_sequence(tie(cotangent, x_all))
    small_all = small_all.reshape(fsdp_count, -1)
    vecs = small_all[:, : 10 * shard].reshape(fsdp_count, 10, shard).transpose(1, 0, 2)
    vecs = jnp.pad(vecs.reshape(10, width), ((0, 6), (0, 0))).astype(F32)
    c_row = small_all[:, 10 * shard : 10 * shard + ff_shard].reshape(1, ff_width).astype(F32)

    outs, input_grads, totals = [], [], None
    for index in range(own_seqs):
        x = x_all[index]
        pos = jnp.full((16, 1), -1, jnp.int32).at[:glob_count, 0].set(own_pos[index])
        q, k, v = project(me, x, local_w, vecs)
        ctx, lse = attn_fwd(pos, q, k, v)
        ctx_glob, probs, keys, mixed, query, rows = globals_fwd(
            me, pos, x, mixed_w, vecs, glob_count
        )
        hat, inv, low, active, slope, merged = ffn_up(
            me, pos, ctx, ctx_glob, x, mixed_w, in_w, vecs, c_row, out_first
        )
        out, branch, inner, grad_sum, attn_grad, merged_grad, vec_one, c_grad = ffn_back(
            me, active, slope, hat, inv, up_all[index], mixed_w, in_w, back_w, vecs, out_first
        )
        outs.append(out)
        if tree:
            back_send = grad_rows(me, active, branch, 1)
            back_keep = grad_rows(me, tie(active, back_send), branch, 0)
            in_keep, in_send = grad_cols(me, tie(low, back_keep), [inner])
            back = Reduction(back_keep, back_send, True)
            ffin = Reduction(in_keep, in_send, False)
            merged_grad = tie(merged_grad, in_send, back.second())
        grad_sum, glob_keep, glob_send, vec_two = globals_bwd(
            me,
            pos,
            x,
            merged_grad,
            grad_sum,
            probs,
            keys,
            mixed,
            query,
            rows,
            merged,
            attn_grad,
            mixed_w,
            vecs,
            glob_count,
        )
        if tree:
            glob = Reduction(glob_keep, glob_send, True)
            merged_grad = tie(merged_grad, glob_send, ffin.second())
        pre_query, dk, dv = attn_bwd(pos, q, k, v, merged_grad, ctx, lse)
        if tree:
            grad_sum = tie(grad_sum, pre_query, back.third(), ffin.third(), glob.second())
        input_grad, vec_three = inputs_back(me, grad_sum, pre_query, dk, dv, local_w)
        input_grads.append(input_grad)
        vec = vec_one + vec_two + vec_three
        vec = jnp.concatenate(
            [vec[:10], c_grad.reshape(-1, width), jnp.zeros((2, width), F32)], axis=0
        )
        if not tree:
            grads = (
                dot_tn(active, branch),
                dot_tn(low, inner),
                glob_keep[0].astype(F32),
                jnp.stack([dot_tn(x, value) for value in (pre_query, dk, dv)]),
                vec,
            )
            totals = grads if totals is None else tuple(a + b for a, b in zip(totals, grads))
    out = to_tokens(outs)
    grad_inputs = to_tokens(input_grads)
    if tree:
        local_keep, local_send = grad_cols(
            me, tie(x, input_grad), [pre_query, dk, dv], nb=width // 2
        )
        local = Reduction(local_keep, local_send, False)
        glob.third()
        local.second()
        local.third()
        for bit in (1, 2, 4):
            vec = vec + flip(vec, "fsdp", bit)
        for bit in (1, 2):
            vec = vec + flip(vec, "sp", bit)
        s_back, s_in, s_mixed, s_local = (
            sum_over_sp(unit.total()) for unit in (back, ffin, glob, local)
        )
        s_local = s_local.reshape(3, shard, width)
        s_mixed = s_mixed.reshape(4, shard, width)
    else:
        g_back, g_in, g_mixed, g_local, vec = totals

        def reduce(value, dim):
            mine = lax.psum_scatter(value.astype(BF), "fsdp", scatter_dimension=dim, tiled=True)
            return lax.psum(mine, "sp").astype(F32)

        s_back, s_in = reduce(g_back, 0), reduce(g_in, 0)
        s_mixed = reduce(g_mixed.reshape(4, width, width), 1)
        s_local = reduce(g_local, 1)
        vec = lax.psum(vec, ("fsdp", "sp"))
    mine = lax.dynamic_slice_in_dim(vec[:10], fsdp_index * shard, shard, 1)
    c_mine = lax.dynamic_slice_in_dim(
        vec[10 : 10 + ff_width // width].reshape(-1), fsdp_index * ff_shard, ff_shard, 0
    )
    return (
        out,
        grad_inputs,
        s_local,
        s_mixed[:3],
        s_mixed[3],
        mine[:6],
        mine[6:8],
        mine[8:10],
        s_in,
        c_mine,
        s_back,
    )


def solution(mesh):
    rows = P("fsdp", None)
    tokens = P("fsdp", "sp", None)
    columns = P(None, "fsdp")
    stacked = P(None, "fsdp", None)
    return jax.shard_map(
        per_device,
        mesh=mesh,
        in_specs=(
            tokens,
            rows,
            stacked,
            stacked,
            rows,
            columns,
            columns,
            columns,
            rows,
            P("fsdp"),
            rows,
            tokens,
        ),
        out_specs=(
            tokens,
            tokens,
            stacked,
            stacked,
            rows,
            columns,
            columns,
            columns,
            rows,
            P("fsdp"),
            rows,
        ),
        check_vma=False,
    )
```

```python
import jax
import jax.numpy as jnp
from jax import lax
from jax.experimental import pallas as pl
from jax.experimental.pallas import tpu as pltpu
from jax.sharding import PartitionSpec as P

HEADS = 12
HEAD_DIM = 64
WIN = 256
QB = 128
NEG = -1e9
GROUPS = 2
COST = 10**9
NORM_EPS = 1e-05
BF = jnp.bfloat16
F32 = jnp.float32
S = jax.ShapeDtypeStruct


def dot_nn(a,b): return jnp.dot(a,b,preferred_element_type=F32)
def dot_nt(a,b): return lax.dot_general(a,b,(((1,),(1,)),((),())),preferred_element_type=F32)
def dot_tn(a,b): return lax.dot_general(a,b,(((0,),(0,)),((),())),preferred_element_type=F32)

def split_pair(block):
    lane=lax.broadcasted_iota(jnp.int32,block.shape,1)
    zero=jnp.zeros_like(block)
    return jnp.concatenate([jnp.where(lane<HEAD_DIM,block,zero),jnp.where(lane<HEAD_DIM,zero,block)],axis=0)

def far_mask(pos, start):
    place=start+lax.broadcasted_iota(jnp.int32,(16,2*QB),1)%QB
    return (pos>=0)&(jnp.abs(place-pos)>WIN)

def edge_masks():
    row=lax.broadcasted_iota(jnp.int32,(QB,2*QB),0)
    col=lax.broadcasted_iota(jnp.int32,(QB,2*QB),1)%QB
    return row>=col, row<=col

def key_range(start,length):
    return max(0,start-WIN), min(length,start+QB+WIN)

def pick_head(both):
    row=lax.broadcasted_iota(jnp.int32,(2*HEAD_DIM,QB),0)
    return jnp.where(row<HEAD_DIM,both[:,:QB],both[:,QB:])

def masked_scores(raw,start,length,low_ok,high_ok):
    lo,hi=key_range(start,length)
    parts=[]
    for first in range(lo,hi,QB):
        chunk=raw[first-lo:first-lo+QB]
        if first==start-WIN: chunk=jnp.where(low_ok,chunk,NEG)
        elif first==start+WIN: chunk=jnp.where(high_ok,chunk,NEG)
        parts.append(chunk)
    return parts

def fwd_kernel(pos_ref,q_ref,k_ref,v_ref,ctx_ref,lse_ref):
    length=q_ref.shape[0]
    pos=pos_ref[...]
    token=lax.broadcasted_iota(jnp.int32,(16,length),1)
    sel=jnp.where(token==pos,1.0,0.0).astype(BF)
    key_far=dot_nn(sel,k_ref[...]).astype(BF)
    val_far_t=dot_nn(sel,v_ref[...]).astype(BF).T
    val_t=v_ref[...].T
    low_ok,high_ok=edge_masks()
    for start in range(0,length,QB):
        lo,hi=key_range(start,length)
        qq=split_pair(q_ref[start:start+QB,:])
        raw=dot_nt(k_ref[lo:hi,:],qq)
        parts=masked_scores(raw,start,length,low_ok,high_ok)
        far=jnp.where(far_mask(pos,start),dot_nt(key_far,qq),NEG)
        top=jnp.max(far,axis=0,keepdims=True)
        for part in parts: top=jnp.maximum(top,jnp.max(part,axis=0,keepdims=True))
        far_p=jnp.exp(far-top)
        total=jnp.sum(far_p,axis=0,keepdims=True)
        probs=[]
        for part in parts:
            p=jnp.exp(part-top)
            total=total+jnp.sum(p,axis=0,keepdims=True)
            probs.append(p.astype(BF))
        both=dot_nn(val_t[:,lo:hi],jnp.concatenate(probs,axis=0))+dot_nn(val_far_t,far_p.astype(BF))
        both=both*(1.0/total)
        ctx_ref[start:start+QB,:]=pick_head(both).T.astype(BF)
        lse=top+jnp.log(total)
        lse_ref[0,0:1,start:start+QB]=lse[:,:QB]
        lse_ref[0,1:2,start:start+QB]=lse[:,QB:]

def attn_fwd(pos,q,k,v):
    length,width=q.shape
    pairs=width//128
    col=pl.BlockSpec((length,128),lambda i:(0,i))
    return pl.pallas_call(fwd_kernel,grid=(pairs,),
        in_specs=[pl.BlockSpec((16,1),lambda i:(0,0)),col,col,col],
        out_specs=[col,pl.BlockSpec((1,8,length),lambda i:(i,0,0))],
        out_shape=[jax.ShapeDtypeStruct((length,width),BF),jax.ShapeDtypeStruct((pairs,8,length),F32)],
        compiler_params=params(),
        cost_estimate=cost(COST,1<<20),
        name="attend")(pos,q,k,v)

def bwd_kernel(pos_ref,q_ref,k_ref,v_ref,g_ref,ctx_ref,lse_ref,dq_ref,dk_ref,dv_ref,dk_acc,dv_acc,grad_scr):
    length=q_ref.shape[0]
    pos=pos_ref[...]
    token=lax.broadcasted_iota(jnp.int32,(16,length),1)
    sel_bool=token==pos
    sel=jnp.where(sel_bool,1.0,0.0).astype(BF)
    sel_full=jnp.where(sel_bool,1.0,0.0)
    key_far=dot_nn(sel,k_ref[...]).astype(BF)
    val_far=dot_nn(sel,v_ref[...]).astype(BF)
    key_far_t=key_far.T
    key_t=k_ref[...].T
    ones=jnp.ones((16,128),F32)
    is_glob=lax.dot_general(sel_full,ones,(((0,),(0,)),((),())),preferred_element_type=F32)
    grad_scr[...]=jnp.where(is_glob>0.5,0.0,g_ref[...].astype(F32)).astype(BF)
    prod=grad_scr[...].astype(F32)*ctx_ref[...].astype(F32)
    hrow=lax.broadcasted_iota(jnp.int32,(16,128),0)
    hlane=lax.broadcasted_iota(jnp.int32,(16,128),1)//HEAD_DIM
    hsel=jnp.where(hrow==hlane,1.0,0.0)
    delta_all=lax.dot_general(hsel,prod,(((1,),(1,)),((),())),preferred_element_type=F32,precision=lax.Precision.HIGHEST)
    dk_acc[...]=jnp.zeros_like(dk_acc)
    dv_acc[...]=jnp.zeros_like(dv_acc)
    dk_far=jnp.zeros((16,128),F32); dv_far=jnp.zeros((16,128),F32)
    low_ok,high_ok=edge_masks()
    for start in range(0,length,QB):
        lo,hi=key_range(start,length)
        qq=split_pair(q_ref[start:start+QB,:])
        gg=split_pair(grad_scr[start:start+QB,:])
        lse=jnp.concatenate([lse_ref[0,0:1,start:start+QB],lse_ref[0,1:2,start:start+QB]],axis=1)
        delta=jnp.concatenate([delta_all[0:1,start:start+QB],delta_all[1:2,start:start+QB]],axis=1)
        dq_t=jnp.zeros((128,2*QB),F32)
        def one(scores,vals):
            p=jnp.exp(scores-lse)
            dp=dot_nt(vals,gg)
            return p.astype(BF),(p*(dp-delta)).astype(BF)
        far=jnp.where(far_mask(pos,start),dot_nt(key_far,qq),NEG)
        p,ds=one(far,val_far)
        dv_far=dv_far+dot_nn(p,gg); dk_far=dk_far+dot_nn(ds,qq)
        dq_t=dq_t+dot_nn(key_far_t,ds)
        parts=masked_scores(dot_nt(k_ref[lo:hi,:],qq),start,length,low_ok,high_ok)
        plist=[];dlist=[]
        for n,part in enumerate(parts):
            a=lo+n*QB
            p,ds=one(part,v_ref[a:a+QB,:])
            plist.append(p);dlist.append(ds)
        p=jnp.concatenate(plist,axis=0); ds=jnp.concatenate(dlist,axis=0)
        dv_acc[lo:hi,:]+=dot_nn(p,gg)
        dk_acc[lo:hi,:]+=dot_nn(ds,qq)
        dq_t=dq_t+dot_nn(key_t[:,lo:hi],ds)
        dq_ref[start:start+QB,:]=(pick_head(dq_t).T.astype(BF).astype(F32)*(HEAD_DIM**-0.5)).astype(BF)
    dk_ref[...]=(dk_acc[...]+lax.dot_general(sel_full,dk_far,(((0,),(0,)),((),())),preferred_element_type=F32,precision=lax.Precision.HIGHEST)).astype(BF)
    dv_ref[...]=(dv_acc[...]+lax.dot_general(sel_full,dv_far,(((0,),(0,)),((),())),preferred_element_type=F32,precision=lax.Precision.HIGHEST)).astype(BF)

def attn_bwd(pos,q,k,v,grad,ctx,lse,first,pairs):
    length,width=q.shape
    col=pl.BlockSpec((length,128),lambda i:(0,first+i))
    out_col=pl.BlockSpec((length,128),lambda i:(0,i))
    out=jax.ShapeDtypeStruct((length,128*pairs),BF)
    return pl.pallas_call(bwd_kernel,grid=(pairs,),
        in_specs=[pl.BlockSpec((16,1),lambda i:(0,0)),col,col,col,col,col,pl.BlockSpec((1,8,length),lambda i:(first+i,0,0))],
        out_specs=[out_col,out_col,out_col],
        out_shape=[out,out,out],
        scratch_shapes=[pltpu.VMEM((length,128),F32),pltpu.VMEM((length,128),F32),pltpu.VMEM((length,128),BF)],
        compiler_params=params(),
        cost_estimate=cost(COST,1<<20),
        name="attend_back")(pos,q,k,v,grad,ctx,lse)


ANY=pl.BlockSpec(memory_space=pl.ANY)
SMEM=pl.BlockSpec(memory_space=pltpu.SMEM)
RB=256

def cost(flops,nbytes,trans=0):
    return pl.CostEstimate(flops=int(flops),bytes_accessed=int(nbytes),transcendentals=int(trans))

def params(mib=60):
    return pltpu.CompilerParams(vmem_limit_bytes=mib<<20)

def fetches(pieces,place,sems,me,first,rows,sem0):
    out=[]
    for slot,piece in enumerate(pieces):
        owner=me^slot
        out.append(pltpu.make_async_copy(piece.at[pl.ds(first,rows)],place.at[pl.ds(pl.multiple_of(owner*rows,rows),rows)],sems.at[sem0+slot]))
    return out

def ffn_in_copies(refs,place,sems,sem0):
    if len(refs)>1: return [pltpu.make_async_copy(refs[0],place,sems.at[sem0])]
    pack=refs[0]; n,_,width=pack.shape; shard=place.shape[0]//n
    return [pltpu.make_async_copy(pack.at[s,pl.ds(j*shard,shard)],place.at[pl.ds(s*shard,shard),pl.ds(j*width,width)],sems.at[sem0+s*(place.shape[1]//width)+j])
            for s in range(n) for j in range(place.shape[1]//width)]


def ffn_back_copies(refs,place,sems,sem0):
    if len(refs)>1: return [pltpu.make_async_copy(refs[1],place,sems.at[sem0])]
    pack=refs[0]; n,rows,width=pack.shape; shard=place.shape[0]//n; first=rows-4*(width//n)-shard
    return [pltpu.make_async_copy(pack.at[s,pl.ds(first,shard)],place.at[pl.ds(s*shard,shard)],sems.at[sem0+s]) for s in range(n)]


def plane_copies(refs,plane,place,sems,sem0):
    width=place.shape[0]
    if len(refs)>1: return [pltpu.make_async_copy(refs[2].at[pl.ds(plane*width,width)],place,sems.at[sem0])]
    pack=refs[0]; n,rows,_=pack.shape; shard=width//n; first=rows-(4-plane)*shard
    return [pltpu.make_async_copy(pack.at[s,pl.ds(first,shard)],place.at[pl.ds(s*shard,shard)],sems.at[sem0+s]) for s in range(n)]


def stats(value):
    center=value-jnp.mean(value,axis=-1,keepdims=True)
    inverse=lax.rsqrt(jnp.mean(center*center,axis=-1,keepdims=True)+NORM_EPS)
    return center*inverse,inverse

def norm_back(scaled,normed,inverse):
    return inverse*(scaled-jnp.mean(scaled,axis=-1,keepdims=True)-normed*jnp.mean(scaled*normed,axis=-1,keepdims=True))

def gelu_pair(inner):
    cdf=0.5*(1.0+lax.erf(inner*0.7071067811865476))
    return inner*cdf, cdf+inner*(0.3989422804014327*jnp.exp(-0.5*inner*inner))

def ffn_up(pos,ctx,ctxg,x,ffw,vecs,c_row,n):
    length,width=x.shape
    ff=c_row.shape[1]; w=len(ffw)
    def body(pos_ref,ctx_ref,glob_ref,x_ref,vec_ref,c_ref,*refs):
        ff_w=refs[:w]
        hat_ref,inv_ref,low_ref,act_ref,slope_ref,merged_ref,wout,win,sems=refs[w:]
        @pl.when(pl.program_id(0)==0)
        def _():
            cps=plane_copies(ff_w,3,wout,sems,0)+ffn_in_copies(ff_w,win,sems,n)
            for c in cps: c.start()
            for c in cps: c.wait()
        token=pl.program_id(0)*RB+lax.broadcasted_iota(jnp.int32,(16,RB),1)
        hot=jnp.where(token==pos_ref[...],1.0,0.0).astype(BF)
        is_glob=dot_tn(hot,jnp.ones((16,128),BF))[:,0:1]>0.5
        merged=jnp.where(is_glob,dot_tn(hot,glob_ref[...]),ctx_ref[...].astype(F32)).astype(BF)
        merged_ref[...]=merged
        attended=dot_nn(merged,wout[...])+vec_ref[4:5,:]
        hat,inv=stats(x_ref[...].astype(F32)+attended)
        hat_ref[...]=hat; inv_ref[...]=inv
        low=(hat*vec_ref[6:7,:]+vec_ref[8:9,:]).astype(BF)
        low_ref[...]=low
        for a in range(0,ff,768):
            inner=dot_nn(low,win[:,a:a+768])+c_ref[:,a:a+768]
            act,slope=gelu_pair(inner)
            act_ref[:,a:a+768]=act.astype(BF); slope_ref[:,a:a+768]=slope.astype(BF)
    blk=lambda w:pl.BlockSpec((RB,w),lambda i:(i,0))
    full=lambda s:pl.BlockSpec(s,lambda i:(0,0))
    return pl.pallas_call(body,grid=(length//RB,),
        in_specs=[full(pos.shape),blk(width),full(ctxg.shape),blk(width),full(vecs.shape),full(c_row.shape)]+[ANY]*w,
        out_specs=[blk(width),blk(1),blk(width),blk(ff),blk(ff),blk(width)],
        out_shape=[jax.ShapeDtypeStruct((length,width),F32),jax.ShapeDtypeStruct((length,1),F32),jax.ShapeDtypeStruct((length,width),BF),
                   jax.ShapeDtypeStruct((length,ff),BF),jax.ShapeDtypeStruct((length,ff),BF),jax.ShapeDtypeStruct((length,width),BF)],
        scratch_shapes=[pltpu.VMEM((width,width),BF),pltpu.VMEM((width,ff),BF),pltpu.SemaphoreType.DMA((n+n*(ff//width),))],
        compiler_params=params(),cost_estimate=cost(COST,1<<20),name="ffn_up")(pos,ctx,ctxg,x,vecs,c_row,*ffw)

def chunk_store(chunks,me,value):
    for slot,chunk in enumerate(chunks):
        @pl.when(pl.program_id(0)^me==slot)
        def _(chunk=chunk): chunk[...]=value


def ffn_back(mez,active,slope,hat1,inv1,upstream,ffw,vecs,n):
    length,width=hat1.shape
    ff=active.shape[1]; w=len(ffw); steps=length//RB
    def body(mez_ref,act_ref,slope_ref,hat_ref,inv_ref,up_ref,vec_ref,*refs):
        ff_w=refs[:w]; chunks=refs[w:w+steps]; refs=refs[:w]+refs[w+steps:]
        bg_ref,ig_ref,gs_ref,ag_ref,mg_ref,vg_ref,cg_ref,wout,win,wback,sems=refs[w:]
        cb=ffn_back_copies(ff_w,wback,sems,0)
        ci=ffn_in_copies(ff_w,win,sems,2*n)
        co=plane_copies(ff_w,3,wout,sems,n)
        first=pl.program_id(0)==0
        @pl.when(first)
        def _():
            for c in cb+ci+co: c.start()
            vg_ref[...]=jnp.zeros_like(vg_ref); cg_ref[...]=jnp.zeros_like(cg_ref)
            for c in cb: c.wait()
        hat1v=hat_ref[...]
        norm1=hat1v*vec_ref[6:7,:]+vec_ref[8:9,:]
        branch=dot_nn(act_ref[...],wback[...])+vec_ref[5:6,:]
        hat2,inv2=stats(norm1+branch)
        chunk_store(chunks,mez_ref[0],(hat2*vec_ref[7:8,:]+vec_ref[9:10,:]).astype(BF))
        up=up_ref[...].astype(F32)
        col=lambda v:jnp.sum(v,axis=0,keepdims=True)
        vg_ref[7:8,:]+=col(up*hat2); vg_ref[9:10,:]+=col(up)
        second=norm_back(up*vec_ref[7:8,:],hat2,inv2)
        bg=second.astype(BF)
        bg_ref[...]=bg
        vg_ref[5:6,:]+=col(bg.astype(F32))
        @pl.when(first)
        def _():
            for c in ci+co: c.wait()
        acc=second
        for a in range(0,ff,768):
            ig=(dot_nt(bg,wback[a:a+768,:])*slope_ref[:,a:a+768].astype(F32)).astype(BF)
            ig_ref[:,a:a+768]=ig
            cg_ref[:,a:a+768]+=col(ig.astype(F32))
            acc=acc+dot_nt(ig,win[:,a:a+768])
        vg_ref[6:7,:]+=col(acc*hat1v); vg_ref[8:9,:]+=col(acc)
        gs=norm_back(acc*vec_ref[6:7,:],hat1v,inv_ref[...])
        gs_ref[...]=gs
        ag=gs.astype(BF)
        ag_ref[...]=ag
        vg_ref[4:5,:]+=col(ag.astype(F32))
        mg_ref[...]=dot_nt(ag,wout[...]).astype(BF)
    blk=lambda w:pl.BlockSpec((RB,w),lambda i:(i,0))
    full=lambda s:pl.BlockSpec(s,lambda i:(0,0))
    return pl.pallas_call(body,grid=(length//RB,),
        in_specs=[SMEM,blk(ff),blk(ff),blk(width),blk(1),blk(width),full(vecs.shape)]+[ANY]*w,
        out_specs=[full((RB,width))]*steps+[blk(width),blk(ff),blk(width),blk(width),blk(width),full((16,width)),full((1,ff))],
        out_shape=[S((RB,width),BF)]*steps+[S((length,width),BF),S((length,ff),BF),S((length,width),F32),S((length,width),BF),S((length,width),BF),S((16,width),F32),S((1,ff),F32)],
        scratch_shapes=[pltpu.VMEM((width,width),BF),pltpu.VMEM((width,ff),BF),pltpu.VMEM((ff,width),BF),pltpu.SemaphoreType.DMA((2*n+n*(ff//width),))],
        compiler_params=params(),cost_estimate=cost(COST,1<<20),name="ffn_back")(mez,active,slope,hat1,inv1,upstream,vecs,*ffw)

def ffn_grads(low,inner,active,branch,count):
    length,width=low.shape; ff=active.shape[1]; shard=width//count; fs=ff//count; blocks=ff//width
    shape=S((count,blocks*shard+fs,width),BF)
    def in_body(l_ref,r_ref,o_ref,lt):
        @pl.when(pl.program_id(0)==0)
        def _(): lt[...]=l_ref[...].T
        o_ref[...]=dot_nn(lt[...],r_ref[...]).reshape(count,shard,width).astype(BF)
    pack=pl.pallas_call(in_body,grid=(blocks,),
        in_specs=[pl.BlockSpec((length,width),lambda j:(0,0)),pl.BlockSpec((length,width),lambda j:(0,j))],
        out_specs=pl.BlockSpec((count,shard,width),lambda j:(0,j,0)),out_shape=shape,
        scratch_shapes=[pltpu.VMEM((width,length),BF)],
        compiler_params=params(),cost_estimate=cost(COST,1<<20),name="ffn_in_grad")(low,inner)
    def back_body(p_ref,l_ref,r_ref,o_ref):
        o_ref[0]=dot_tn(l_ref[...],r_ref[...]).astype(BF)
    return pl.pallas_call(back_body,grid=(count,),
        in_specs=[ANY,pl.BlockSpec((length,fs),lambda s:(0,s)),pl.BlockSpec((length,width),lambda s:(0,0))],
        out_specs=pl.BlockSpec((1,fs,width),lambda s:(s,blocks*shard//fs,0)),out_shape=shape,
        input_output_aliases={0:0},
        compiler_params=params(),cost_estimate=cost(COST,1<<20),name="ffn_back_grad")(pack,active,branch)


def local_grads(me,x,grads,unit=None,vec=None,count=8):
    length,width=x.shape; cols=grads[0].shape[1]; shard=width//count; half=count//2; k=len(grads)
    tail=0 if vec is None else 16
    rows=k*shard+tail
    base=0 if unit is None else unit[0].shape[1]-rows
    extra=([] if vec is None else [vec])+([] if unit is None else list(unit))
    def body(me_ref,x_ref,*refs):
        outs=refs[k+len(extra):]
        keep,send,res,keep_v,send_v,vec_v,sems=outs
        m=me_ref[0]
        xt=x_ref[...].T
        for r in range(k):
            res[...]=dot_nn(xt,refs[r][...])
            for slot in range(count):
                part=res[pl.ds(pl.multiple_of((m^slot)*shard,shard),shard),:]
                (send_v if slot%2 else keep_v)[slot//2,r*shard:(r+1)*shard,:]=part.astype(BF)
        if vec is not None:
            vec_v[...]=jnp.zeros_like(vec_v)
            for s in range(count):
                vec_v[s,:,0:shard]=refs[k][:,s*shard:(s+1)*shard]
            for slot in range(count):
                (send_v if slot%2 else keep_v)[slot//2,k*shard:rows,:]=vec_v[m^slot].astype(BF)
        cps=[pltpu.make_async_copy(v,o.at[:,pl.ds(base,rows)],sems.at[i]) for i,(v,o) in enumerate(((keep_v,keep),(send_v,send)))]
        for c in cps: c.start()
        for c in cps: c.wait()
    o=S((half,base+rows,cols),BF)
    vm=pl.BlockSpec(memory_space=pltpu.VMEM)
    first=1+1+k+(0 if vec is None else 1)
    return pl.pallas_call(body,in_specs=[SMEM]+[vm]*(first-1)+[ANY]*(0 if unit is None else 2),out_specs=[ANY]*2,out_shape=[o,o],
        input_output_aliases={} if unit is None else {first:0,first+1:1},
        scratch_shapes=[pltpu.VMEM((width,cols),F32),pltpu.VMEM((half,rows,cols),BF),pltpu.VMEM((half,rows,cols),BF),pltpu.VMEM((count,16,cols),F32),pltpu.SemaphoreType.DMA((2,))],
        compiler_params=params(),cost_estimate=cost(COST,1<<20),name="local_grads")(me,x,*grads,*extra)


def collect(mez,pieces):
    def body(mez_ref,*refs):
        for slot in range(len(pieces)):
            @pl.when(pl.program_id(0)^mez_ref[0]==slot)
            def _(slot=slot): refs[-1][0]=refs[slot][...]
    rows,width=pieces[0].shape; n=len(pieces)
    return pl.pallas_call(body,grid=(n,),in_specs=[SMEM]+[pl.BlockSpec((rows,width),lambda i:(0,0))]*n,
        out_specs=pl.BlockSpec((1,rows,width),lambda i:(i,0,0)),out_shape=S((n,rows,width),BF),
        compiler_params=params(),cost_estimate=cost(COST,1<<20),name="collect")(mez,*pieces)


def project(me,x,pieces,vecs):
    length,width=x.shape; n=len(pieces); shard=width//n
    def body(me_ref,x_ref,vec_ref,*refs):
        ins=refs[:n]; q_ref,k_ref,v_ref,wts,sems=refs[n:]
        m=me_ref[0]
        cps=[fetches(ins,wts.at[j],sems,m,j*shard,shard,j*n) for j in range(3)]
        for j in range(3):
            for c in cps[j]: c.start()
        for c in cps[0]: c.wait()
        scale=HEAD_DIM**-0.5
        for a in range(0,length,RB):
            q_ref[a:a+RB,:]=((dot_nn(x_ref[a:a+RB,:],wts[0])+vec_ref[0:1,:])*scale).astype(BF)
        for c in cps[1]: c.wait()
        for a in range(0,length,RB):
            k_ref[a:a+RB,:]=dot_nn(x_ref[a:a+RB,:],wts[1]).astype(BF)
        for c in cps[2]: c.wait()
        for a in range(0,length,RB):
            v_ref[a:a+RB,:]=(dot_nn(x_ref[a:a+RB,:],wts[2])+vec_ref[1:2,:]).astype(BF)
    vm=pl.BlockSpec(memory_space=pltpu.VMEM)
    return pl.pallas_call(body,in_specs=[SMEM,vm,vm]+[ANY]*n,out_specs=[vm]*3,out_shape=[S((length,width),BF)]*3,
        scratch_shapes=[pltpu.VMEM((3,width,width),BF),pltpu.SemaphoreType.DMA((3*n,))],
        compiler_params=params(),cost_estimate=cost(COST,1<<20),name="project")(me,x,vecs,*pieces)

def own_mask(width):
    return lax.broadcasted_iota(jnp.int32,(16,width),0)==lax.broadcasted_iota(jnp.int32,(16,width),1)//HEAD_DIM

def one_hot(pos,length):
    return jnp.where(lax.broadcasted_iota(jnp.int32,(16,length),1)==pos,1.0,0.0)

def scatter_heads(rows,own,count):
    zero=jnp.zeros((16,rows.shape[1]),F32)
    return jnp.concatenate([jnp.where(own,jnp.broadcast_to(rows[g:g+1,:].astype(F32),zero.shape),zero) for g in range(count)],axis=0).astype(BF)

def gather_heads(value,own,count):
    rows=[jnp.sum(jnp.where(own,value[16*g:16*g+16],0.0),axis=0,keepdims=True) for g in range(count)]
    rows.append(jnp.zeros((16-count,value.shape[1]),F32))
    return jnp.concatenate(rows,axis=0)

def globals_fwd(pos,x,ffw,vecs,count,n):
    length,width=x.shape; wide=16*count; w=len(ffw)
    def body(pos_ref,x_ref,vec_ref,*refs):
        ins=refs[:w]; ctx_ref,p_ref,u_ref,y_ref,q_ref,r_ref,wts,sems=refs[w:]
        cps=[plane_copies(ins,j,wts.at[j],sems,j*n) for j in range(3)]
        for j in range(3):
            for c in cps[j]: c.start()
        own=own_mask(width)
        sel=one_hot(pos_ref[...],length).astype(BF)
        rows=dot_nn(sel,x_ref[...]).astype(BF)
        r_ref[...]=rows
        for c in cps[0]: c.wait()
        q=((dot_nn(rows,wts[0])+vec_ref[2:3,:])*(HEAD_DIM**-0.5)).astype(BF)
        q_ref[...]=q
        for c in cps[1]: c.wait()
        u=dot_nt(wts[1],scatter_heads(q,own,count)).astype(BF)
        u_ref[...]=u
        s=dot_nn(x_ref[...],u)
        p=jnp.exp(s-jnp.max(s,axis=0,keepdims=True))
        p=p/jnp.sum(p,axis=0,keepdims=True)
        p_ref[...]=p
        low=p.astype(BF)
        y=dot_tn(low,x_ref[...]).astype(BF)
        y_ref[...]=y
        mass=dot_tn(low,jnp.ones((length,128),BF))[:,0:1]
        for c in cps[2]: c.wait()
        ctx_ref[...]=gather_heads(dot_nn(y,wts[2])+mass*vec_ref[3:4,:],own,count).astype(BF)
    vm=pl.BlockSpec(memory_space=pltpu.VMEM)
    return pl.pallas_call(body,in_specs=[vm,vm,vm]+[ANY]*w,out_specs=[vm]*6,
        out_shape=[S((16,width),BF),S((length,wide),F32),S((width,wide),BF),S((wide,width),BF),S((16,width),BF),S((16,width),BF)],
        scratch_shapes=[pltpu.VMEM((3,width,width),BF),pltpu.SemaphoreType.DMA((3*n,))],
        compiler_params=params(),cost_estimate=cost(COST,1<<20),name="globals")(pos,x,vecs,*ffw)

def globals_bwd(me,pos,x,mg,gs,p,u,y,q,rows,merged,ag,ffw,vecs,count,n,extra):
    length,width=x.shape; shard=width//n; half=max(n//2,1); w=len(ffw); cols=width//2
    def body(me_ref,pos_ref,x_ref,mg_ref,gs_ref,p_ref,u_ref,y_ref,q_ref,r_ref,merged_ref,ag_ref,vec_ref,*refs):
        ins=refs[:w]; out_ref,keep,send,keep2,send2,vg_ref,wts,res,keep_v,send_v,sems=refs[w:]
        m=me_ref[0]
        cps=[plane_copies(ins,j,wts.at[j],sems,j*n) for j in range(3)]
        for j in (2,1,0):
            for c in cps[j]: c.start()
        own=own_mask(width)
        hot=one_hot(pos_ref[...],length)
        sel=hot.astype(BF)
        x=x_ref[...]
        cs=scatter_heads(dot_nn(sel,mg_ref[...]).astype(BF),own,count)
        qs=scatter_heads(q_ref[...],own,count)
        for c in cps[2]: c.wait()
        v=dot_nt(wts[2],cs).astype(BF)
        shift=dot_nt(jnp.broadcast_to(vec_ref[3:4,:],(16,width)).astype(BF),cs)[0:1,:]
        dp=dot_nn(x,v)+shift
        p=p_ref[...]
        low=p.astype(BF)
        ds=(p*(dp-jnp.sum(p*dp,axis=0,keepdims=True))).astype(BF)
        a=dot_tn(ds,x).astype(BF)
        for c in cps[1]: c.wait()
        pre=(gather_heads(dot_nn(a,wts[1]),own,count).astype(BF).astype(F32)*(HEAD_DIM**-0.5)).astype(BF)
        for c in cps[0]: c.wait()
        rows_grad=dot_nt(pre,wts[0])
        mass=dot_tn(low,jnp.ones((length,128),BF))[:,0:1]
        vg_ref[...]=jnp.zeros_like(vg_ref)
        vg_ref[2:3,:]=jnp.sum(pre.astype(F32),axis=0,keepdims=True)
        vg_ref[3:4,:]=jnp.sum(mass*cs.astype(F32),axis=0,keepdims=True)
        out_ref[...]=gs_ref[...]+dot_nt(ds,u_ref[...])+dot_nt(low,v)+lax.dot_general(hot,rows_grad,(((0,),(0,)),((),())),preferred_element_type=F32,precision=lax.Precision.HIGHEST)
        for j,(l,r) in enumerate(((r_ref[...],pre),(a,qs),(y_ref[...],cs),(merged_ref[...],ag_ref[...]))):
            res[...]=dot_tn(l,r)
            for slot in range(n):
                for h in range(2):
                    part=res[pl.ds(pl.multiple_of((m^slot)*shard,shard),shard),h*cols:(h+1)*cols]
                    (send_v if slot%2 else keep_v)[slot//2,(2*j+h)*shard:(2*j+h+1)*shard,:]=part.astype(BF)
        cps=[]
        for here,first,there in ((keep_v,0,keep),(keep_v,6*shard,keep2),(send_v,0,send),(send_v,6*shard,send2)):
            if n==1 and here is send_v: continue
            rows_out=6*shard if first==0 else 2*shard
            cps.append(pltpu.make_async_copy(here.at[:,pl.ds(first,rows_out)],there.at[:,pl.ds(0,rows_out)],sems.at[3*n+len(cps)]))
        for c in cps: c.start()
        for c in cps: c.wait()
    vm=pl.BlockSpec(memory_space=pltpu.VMEM)
    o1=S((half,6*shard,cols),BF)
    o2=S((half,2*shard+extra,cols),BF)
    return pl.pallas_call(body,in_specs=[SMEM]+[vm]*12+[ANY]*w,out_specs=[vm,ANY,ANY,ANY,ANY,vm],
        out_shape=[S((length,width),F32),o1,o1,o2,o2,S((16,width),F32)],
        scratch_shapes=[pltpu.VMEM((3,width,width),BF),pltpu.VMEM((width,width),F32),pltpu.VMEM((half,8*shard,cols),BF),pltpu.VMEM((half,8*shard,cols),BF),pltpu.SemaphoreType.DMA((3*n+4,))],
        compiler_params=params(),cost_estimate=cost(COST,1<<20),name="globals_back")(me,pos,x,mg,gs,p,u,y,q,rows,merged,ag,vecs,*ffw)


def inputs_back(me,mez,gs,groups,pieces):
    length,width=gs.shape; n=len(pieces); shard=width//n; g=len(groups); cols=width//g
    steps=length//RB
    def body(me_ref,mez_ref,gs_ref,*refs):
        parts=refs[:3*g]; ins=refs[3*g:3*g+n]; chunks=refs[3*g+n:3*g+n+steps]; vg_ref,wts,sems=refs[3*g+n+steps:]
        m=me_ref[0]
        @pl.when(pl.program_id(0)==0)
        def _():
            cps=sum([fetches(ins,wts.at[j],sems,m,j*shard,shard,j*n) for j in range(3)],[])
            for c in cps: c.start()
            vg_ref[...]=jnp.zeros_like(vg_ref)
            for c in cps: c.wait()
        acc=gs_ref[...]
        for j in range(g):
            a=j*cols
            for w in range(3): acc=acc+dot_nt(parts[3*j+w][...],wts[w,:,a:a+cols])
            vg_ref[0:1,a:a+cols]+=jnp.sum(parts[3*j][...].astype(F32),axis=0,keepdims=True)
            vg_ref[1:2,a:a+cols]+=jnp.sum(parts[3*j+2][...].astype(F32),axis=0,keepdims=True)
        chunk_store(chunks,mez_ref[0],acc.astype(BF))
    blk=pl.BlockSpec((RB,width),lambda i:(i,0))
    part=pl.BlockSpec((RB,cols),lambda i:(i,0))
    return pl.pallas_call(body,grid=(length//RB,),in_specs=[SMEM,SMEM,blk]+[part]*(3*g)+[ANY]*n,
        out_specs=[pl.BlockSpec((RB,width),lambda i:(0,0))]*steps+[pl.BlockSpec((16,width),lambda i:(0,0))],out_shape=[S((RB,width),BF)]*steps+[S((16,width),F32)],
        scratch_shapes=[pltpu.VMEM((3,width,width),BF),pltpu.SemaphoreType.DMA((3*n,))],
        compiler_params=params(),cost_estimate=cost(COST,1<<20),name="inputs_back")(me,mez,gs,*[p for t in groups for p in t],*pieces)


def flip(value, axis, bit):
    count = lax.axis_size(axis)
    return lax.ppermute(value, axis, [(index, index ^ bit) for index in range(count)])


def tie(value, *others):
    return lax.optimization_barrier((value,) + others)[0]


def spread_slots(unit, order):
    slots = {0: unit}
    for bit in order:
        for slot in list(slots):
            slots[slot | bit] = flip(slots[slot], "fsdp", bit)
    return [slots[slot] for slot in range(len(slots))]


def add(one, two):
    return one.astype(F32) + two.astype(F32)


def meet(values, parts, *others):
    flat = [list(part.got) if isinstance(part.got, list) else [part.got] for part in parts]
    joined = tuple(values) + tuple(got for gots in flat for got in gots) + others
    joined = list(lax.optimization_barrier(joined))
    values = [joined.pop(0) for _ in values]
    for part, gots in zip(parts, flat):
        new = [joined.pop(0) for _ in gots]
        part.got = new if isinstance(part.got, list) else new[0]
    return values


class Exchange:
    def __init__(self, chunks):
        self.got = [chunks[0]] + [flip(chunks[k], "sp", k) for k in range(1, len(chunks))]


class Reduction:
    def __init__(self, keep, send, x_first):
        self.keep, self.first, self.step = keep, send, 0
        self.got = flip(send, "fsdp", 1)
        self.x_first = x_first

    def advance(self, *gates):
        got = tie(self.got, *gates)
        x_now = self.x_first == (self.step == 0)
        if self.step == 0:
            keep = self.keep.reshape((2, 2) + self.keep.shape[1:])
            got = got.reshape(keep.shape)
            if self.x_first:
                away, here = (keep[:, 1], got[:, 1]), (keep[:, 0], got[:, 0])
            else:
                away, here = (keep[1], got[1]), (keep[0], got[0])
        else:
            away, here = (self.mine[1], got[1]), (self.mine[0], got[0])
        self.send, self.mine = add(*away).astype(BF), add(*here)
        self.got = flip(self.send, "fsdp", 2 if x_now else 4)
        self.step += 1
        return self.send

    def total(self):
        return add(self.mine, self.got)


class SpSum:
    def __init__(self, value, start=True):
        self.low, self.high = lax.axis_index("sp") & 1, lax.axis_index("sp") >> 1
        rows = value.shape[0] // 4
        self.shape = value.shape
        self.value = value.reshape(2, 2, rows, value.shape[1])
        self.got = self.value
        self.step = 0
        if start:
            self.start()

    def start(self):
        self.value = self.got
        self.exchange(self.low, 1)

    def exchange(self, mine, bit):
        send = lax.dynamic_index_in_dim(self.value, 1 - mine, 0, keepdims=False).astype(BF)
        self.value = lax.dynamic_index_in_dim(self.value, mine, 0, keepdims=False)
        self.got = flip(send, "sp", bit)

    def join(self, mine):
        return jnp.stack(
            [jnp.where(mine == 0, self.value, self.got), jnp.where(mine == 0, self.got, self.value)]
        )

    def advance(self):
        if self.step == 0:
            self.value = add(self.value, self.got)
            self.exchange(self.high, 2)
        elif self.step == 1:
            self.value = add(self.value, self.got).astype(BF)
            self.got = flip(self.value, "sp", 2)
        else:
            self.value = self.join(self.high)
            self.got = flip(self.value, "sp", 1)
        self.step += 1

    def total(self):
        return self.join(self.low).reshape(self.shape).astype(F32)


def per_device(
    inputs,
    global_pos,
    w_local,
    w_global,
    w_out,
    b_proj,
    gains,
    shifts,
    w_in,
    c_in,
    w_back,
    cotangent,
):
    sp_count = lax.axis_size("sp")
    fsdp_count = lax.axis_size("fsdp")
    sp_index = lax.axis_index("sp")
    fsdp_index = lax.axis_index("fsdp")
    own_seqs = inputs.shape[0] // sp_count
    glob_count = global_pos.shape[1]
    shard, width = w_out.shape
    ff_shard = w_back.shape[0]
    ff_width = w_in.shape[1]
    tree = fsdp_count == 8 and sp_count == 4 and own_seqs == 1 and shard % 32 == 0
    tree = tree and inputs.shape[1] == RB

    def to_sequence(value):
        if own_seqs == 1:
            moved = lax.all_to_all(value, "sp", split_axis=0, concat_axis=0)
            return moved.reshape(1, -1, width)
        return lax.all_to_all(value, "sp", split_axis=0, concat_axis=1, tiled=True)

    def to_tokens(values):
        if own_seqs == 1:
            return lax.all_to_all(
                values[0].reshape(sp_count, -1, width), "sp", split_axis=0, concat_axis=0
            )
        return lax.all_to_all(jnp.stack(values), "sp", split_axis=1, concat_axis=0, tiled=True)

    own_pos = lax.dynamic_slice_in_dim(global_pos, sp_index * own_seqs, own_seqs, 0)
    blocks = ff_width // width
    x_all = to_sequence(inputs)
    vec_rows = [b_proj, gains, shifts, c_in.reshape(-1, shard)]
    small = jnp.concatenate(vec_rows, axis=0)
    small = jnp.pad(small, ((0, 16 - small.shape[0]), (0, 0)))
    if tree:
        me = fsdp_index.reshape(1).astype(jnp.int32)
        mez = sp_index.reshape(1).astype(jnp.int32)
        first = jnp.concatenate(
            [w_local.reshape(-1, width), jnp.pad(small, ((0, 0), (0, width - shard)))], axis=0
        )
        local_w = spread_slots(first, (2, 4, 1))
        pack = jnp.concatenate(
            [
                w_in.reshape(shard, blocks, width).transpose(1, 0, 2).reshape(-1, width),
                w_back,
                w_global.reshape(-1, width),
                w_out,
            ],
            axis=0,
        )
        ffw = [lax.all_gather(pack, "fsdp")]
        small_all = jnp.stack([piece[3 * shard :, :shard] for piece in local_w])
        small_all = small_all[me[0] ^ jnp.arange(fsdp_count, dtype=jnp.int32)]
    else:
        me = mez = jnp.zeros((1,), jnp.int32)
        local_w = [lax.all_gather(w_local, "fsdp", axis=1, tiled=True).reshape(-1, width)]
        full_global = lax.all_gather(w_global, "fsdp", axis=1, tiled=True).reshape(-1, width)
        full_out = lax.all_gather(w_out, "fsdp", axis=0, tiled=True)
        ffw = [lax.all_gather(value, "fsdp", axis=0, tiled=True) for value in (w_in, w_back)]
        ffw.append(jnp.concatenate([full_global, full_out], axis=0))
        small_all = lax.all_gather(small, "fsdp")
    count = len(local_w)
    up_all = to_sequence(tie(cotangent, x_all))
    vecs = small_all.transpose(1, 0, 2).reshape(16, width).astype(F32)
    c_rows = small_all[:, 10 : 10 + ff_shard // shard].astype(F32)
    c_row = c_rows.reshape(1, ff_width)

    outs, input_grads, totals = [], [], None
    for index in range(own_seqs):
        x = x_all[index]
        pos = jnp.full((16, 1), -1, jnp.int32).at[:glob_count, 0].set(own_pos[index])
        q, k, v = project(me, x, local_w, vecs)
        ctx, lse = attn_fwd(pos, q, k, v)
        ctx_glob, probs, keys, mixed, query, rows = globals_fwd(
            pos, x, ffw, vecs, glob_count, count
        )
        hat, inv, low, active, slope, merged = ffn_up(
            pos, ctx, ctx_glob, x, ffw, vecs, c_row, count
        )
        *out, branch, inner, grad_sum, attn_grad, merged_grad, vec_one, c_grad = ffn_back(
            mez, active, slope, hat, inv, up_all[index], ffw, vecs, count
        )
        if tree:
            out_moved = Exchange(out)
        else:
            outs.append(jnp.concatenate(out, axis=0))
        if tree:
            ff_pack = ffn_grads(low, inner, active, branch, fsdp_count)
            ff_mine = lax.psum_scatter(ff_pack, "fsdp", scatter_dimension=0, tiled=False)
            merged_grad = tie(merged_grad, ff_pack)
        grad_sum, keep_one, send_one, keep_two, send_two, vec_two = globals_bwd(
            me,
            pos,
            x,
            merged_grad,
            grad_sum,
            probs,
            keys,
            mixed,
            query,
            rows,
            merged,
            attn_grad,
            ffw,
            vecs,
            glob_count,
            count,
            3 * shard if tree else 0,
        )
        group_pairs = width // 128 // GROUPS
        groups = []
        if tree:
            one = Reduction(keep_one, send_one, True)
            merged_grad = tie(merged_grad, send_one)
        for group in range(GROUPS):
            parts = attn_bwd(
                pos, q, k, v, merged_grad, ctx, lse, group * group_pairs, group_pairs
            )
            groups.append(parts)
            if tree and group == 0:
                two = Reduction(*local_grads(me, x, parts, unit=(keep_two, send_two)), False)
                merged_grad = tie(merged_grad, two.first)
        if tree:
            (grad_sum,) = meet([grad_sum], [one, two, out_moved], parts[0])
            grad_sum = tie(grad_sum, one.advance(), two.advance())
        *input_grad, vec_three = inputs_back(me, mez, grad_sum, groups, local_w)
        if tree:
            grads_moved = Exchange(input_grad)
        else:
            input_grads.append(jnp.concatenate(input_grad, axis=0))
        c_grad = c_grad.reshape(fsdp_count, -1, shard).transpose(1, 0, 2).reshape(-1, width)
        vec = vec_one + vec_two + vec_three + jnp.pad(c_grad, ((10, 6 - c_grad.shape[0]), (0, 0)))
        if not tree:
            g_mixed = jnp.concatenate([keep_one[0], keep_two[0]], axis=0)
            g_mixed = g_mixed.reshape(4, 2, width, width // 2).transpose(0, 2, 1, 3)
            grads = (
                dot_tn(active, branch),
                dot_tn(low, inner),
                g_mixed.reshape(4, width, width).astype(F32),
                jnp.stack(
                    [
                        jnp.concatenate([dot_tn(x, part[w]) for part in groups], axis=1)
                        for w in range(3)
                    ]
                ),
                vec,
            )
            totals = grads if totals is None else tuple(a + b for a, b in zip(totals, grads))
    if tree:
        late = Reduction(*local_grads(me, tie(x, ff_mine), groups[-1], vec=vec), False)
        (ff_mine,) = meet([ff_mine], [one, two], late.first)
        ff_sum = SpSum(ff_mine.astype(F32))
        one.advance()
        two.advance()
        meet([], [one, two, late])
        late.advance()
        early_sum = SpSum(jnp.concatenate([one.total(), two.total()], axis=0), start=False)
        meet([], [late, ff_sum, grads_moved, early_sum])
        late.advance()
        ff_sum.advance()
        early_sum.start()
        meet([], [late, ff_sum, early_sum])
        late_sum = SpSum(late.total())
        ff_sum.advance()
        early_sum.advance()
        out = collect(mez, out_moved.got)
        meet([], [ff_sum, early_sum, late_sum])
        ff_sum.advance()
        early_sum.advance()
        late_sum.advance()
        grad_inputs = collect(mez, grads_moved.got)
        meet([], [ff_sum, early_sum, late_sum])
        early_sum.advance()
        late_sum.advance()
        s_ff = ff_sum.total()
        meet([], [early_sum, late_sum])
        late_sum.advance()
        s_early, s_late = early_sum.total(), late_sum.total()
        half_mixed = s_early[: 8 * shard].reshape(4, 2, shard, -1).transpose(0, 2, 1, 3)
        s_mixed = half_mixed.reshape(4, shard, width)
        s_local = jnp.concatenate(
            [
                s_early[8 * shard :].reshape(3, shard, -1),
                s_late[: 3 * shard].reshape(3, shard, -1),
            ],
            axis=2,
        )
        mine = s_late[3 * shard :, :shard]
        s_in = s_ff[: blocks * shard].reshape(blocks, shard, width).transpose(1, 0, 2)
        s_in = s_in.reshape(shard, ff_width)
        s_back = s_ff[blocks * shard :]
    else:
        out, grad_inputs = to_tokens(outs), to_tokens(input_grads)
        g_back, g_in, g_mixed, g_local, vec = totals

        def reduce(value, dim):
            mine = lax.psum_scatter(value.astype(BF), "fsdp", scatter_dimension=dim, tiled=True)
            return lax.psum(mine, "sp").astype(F32)

        s_back, s_in = reduce(g_back, 0), reduce(g_in, 0)
        s_mixed = reduce(g_mixed, 1)
        s_local = reduce(g_local, 1)
        vec = lax.psum(vec, ("fsdp", "sp"))
        mine = lax.dynamic_slice_in_dim(vec, fsdp_index * shard, shard, 1)
    c_mine = mine[10 : 10 + ff_shard // shard].reshape(-1)
    return (
        out,
        grad_inputs,
        s_local,
        s_mixed[:3],
        s_mixed[3],
        mine[:6],
        mine[6:8],
        mine[8:10],
        s_in,
        c_mine,
        s_back,
    )


def solution(mesh):
    rows = P("fsdp", None)
    tokens = P("fsdp", "sp", None)
    columns = P(None, "fsdp")
    stacked = P(None, "fsdp", None)
    return jax.shard_map(
        per_device,
        mesh=mesh,
        in_specs=(
            tokens,
            rows,
            stacked,
            stacked,
            rows,
            columns,
            columns,
            columns,
            rows,
            P("fsdp"),
            rows,
            tokens,
        ),
        out_specs=(
            tokens,
            tokens,
            stacked,
            stacked,
            rows,
            columns,
            columns,
            columns,
            rows,
            P("fsdp"),
            rows,
        ),
        check_vma=False,
    )
```

```python
import jax
import jax.numpy as jnp
from jax import lax
from jax.experimental import pallas as pl
from jax.experimental.pallas import tpu as pltpu
from jax.sharding import PartitionSpec as P

HEADS = 12
HEAD_DIM = 64
WIN = 256
QB = 128
NEG = -1e9
GROUPS = 2
COST = 2 * 10**10
NORM_EPS = 1e-05
BF = jnp.bfloat16
F32 = jnp.float32
S = jax.ShapeDtypeStruct


def dot_nn(a,b): return jnp.dot(a,b,preferred_element_type=F32)
def dot_nt(a,b): return lax.dot_general(a,b,(((1,),(1,)),((),())),preferred_element_type=F32)
def dot_tn(a,b): return lax.dot_general(a,b,(((0,),(0,)),((),())),preferred_element_type=F32)

def split_pair(block):
    lane=lax.broadcasted_iota(jnp.int32,block.shape,1)
    zero=jnp.zeros_like(block)
    return jnp.concatenate([jnp.where(lane<HEAD_DIM,block,zero),jnp.where(lane<HEAD_DIM,zero,block)],axis=0)

def far_mask(pos, start):
    place=start+lax.broadcasted_iota(jnp.int32,(16,2*QB),1)%QB
    return (pos>=0)&(jnp.abs(place-pos)>WIN)

def edge_masks():
    row=lax.broadcasted_iota(jnp.int32,(QB,2*QB),0)
    col=lax.broadcasted_iota(jnp.int32,(QB,2*QB),1)%QB
    return row>=col, row<=col

def key_range(start,length):
    return max(0,start-WIN), min(length,start+QB+WIN)

def pick_head(both):
    row=lax.broadcasted_iota(jnp.int32,(2*HEAD_DIM,QB),0)
    return jnp.where(row<HEAD_DIM,both[:,:QB],both[:,QB:])

def masked_scores(raw,start,length,low_ok,high_ok):
    lo,hi=key_range(start,length)
    parts=[]
    for first in range(lo,hi,QB):
        chunk=raw[first-lo:first-lo+QB]
        if first==start-WIN: chunk=jnp.where(low_ok,chunk,NEG)
        elif first==start+WIN: chunk=jnp.where(high_ok,chunk,NEG)
        parts.append(chunk)
    return parts

def fwd_kernel(pos_ref,q_ref,k_ref,v_ref,ctx_ref,lse_ref):
    length=q_ref.shape[0]
    pos=pos_ref[...]
    token=lax.broadcasted_iota(jnp.int32,(16,length),1)
    sel=jnp.where(token==pos,1.0,0.0).astype(BF)
    key_far=dot_nn(sel,k_ref[...]).astype(BF)
    val_far_t=dot_nn(sel,v_ref[...]).astype(BF).T
    val_t=v_ref[...].T
    low_ok,high_ok=edge_masks()
    for start in range(0,length,QB):
        lo,hi=key_range(start,length)
        qq=split_pair(q_ref[start:start+QB,:])
        raw=dot_nt(k_ref[lo:hi,:],qq)
        parts=masked_scores(raw,start,length,low_ok,high_ok)
        far=jnp.where(far_mask(pos,start),dot_nt(key_far,qq),NEG)
        top=jnp.max(far,axis=0,keepdims=True)
        for part in parts: top=jnp.maximum(top,jnp.max(part,axis=0,keepdims=True))
        far_p=jnp.exp(far-top)
        total=jnp.sum(far_p,axis=0,keepdims=True)
        probs=[]
        for part in parts:
            p=jnp.exp(part-top)
            total=total+jnp.sum(p,axis=0,keepdims=True)
            probs.append(p.astype(BF))
        both=dot_nn(val_t[:,lo:hi],jnp.concatenate(probs,axis=0))+dot_nn(val_far_t,far_p.astype(BF))
        both=both*(1.0/total)
        ctx_ref[start:start+QB,:]=pick_head(both).T.astype(BF)
        lse=top+jnp.log(total)
        lse_ref[0,0:1,start:start+QB]=lse[:,:QB]
        lse_ref[0,1:2,start:start+QB]=lse[:,QB:]

def attn_fwd(pos,q,k,v):
    length,width=q.shape
    pairs=width//128
    col=pl.BlockSpec((length,128),lambda i:(0,i))
    return pl.pallas_call(fwd_kernel,grid=(pairs,),
        in_specs=[pl.BlockSpec((16,1),lambda i:(0,0)),col,col,col],
        out_specs=[col,pl.BlockSpec((1,8,length),lambda i:(i,0,0))],
        out_shape=[jax.ShapeDtypeStruct((length,width),BF),jax.ShapeDtypeStruct((pairs,8,length),F32)],
        compiler_params=params(),
        cost_estimate=cost(COST,1<<20),
        name="attend")(pos,q,k,v)

def bwd_kernel(pos_ref,q_ref,k_ref,v_ref,g_ref,ctx_ref,lse_ref,dq_ref,dk_ref,dv_ref,dk_acc,dv_acc,grad_scr):
    length=q_ref.shape[0]
    pos=pos_ref[...]
    token=lax.broadcasted_iota(jnp.int32,(16,length),1)
    sel_bool=token==pos
    sel=jnp.where(sel_bool,1.0,0.0).astype(BF)
    sel_full=jnp.where(sel_bool,1.0,0.0)
    key_far=dot_nn(sel,k_ref[...]).astype(BF)
    val_far=dot_nn(sel,v_ref[...]).astype(BF)
    key_far_t=key_far.T
    key_t=k_ref[...].T
    ones=jnp.ones((16,128),F32)
    is_glob=lax.dot_general(sel_full,ones,(((0,),(0,)),((),())),preferred_element_type=F32)
    grad_scr[...]=jnp.where(is_glob>0.5,0.0,g_ref[...].astype(F32)).astype(BF)
    prod=grad_scr[...].astype(F32)*ctx_ref[...].astype(F32)
    hrow=lax.broadcasted_iota(jnp.int32,(16,128),0)
    hlane=lax.broadcasted_iota(jnp.int32,(16,128),1)//HEAD_DIM
    hsel=jnp.where(hrow==hlane,1.0,0.0)
    delta_all=lax.dot_general(hsel,prod,(((1,),(1,)),((),())),preferred_element_type=F32,precision=lax.Precision.HIGHEST)
    dk_acc[...]=jnp.zeros_like(dk_acc)
    dv_acc[...]=jnp.zeros_like(dv_acc)
    dk_far=jnp.zeros((16,128),F32); dv_far=jnp.zeros((16,128),F32)
    low_ok,high_ok=edge_masks()
    for start in range(0,length,QB):
        lo,hi=key_range(start,length)
        qq=split_pair(q_ref[start:start+QB,:])
        gg=split_pair(grad_scr[start:start+QB,:])
        lse=jnp.concatenate([lse_ref[0,0:1,start:start+QB],lse_ref[0,1:2,start:start+QB]],axis=1)
        delta=jnp.concatenate([delta_all[0:1,start:start+QB],delta_all[1:2,start:start+QB]],axis=1)
        dq_t=jnp.zeros((128,2*QB),F32)
        def one(scores,vals):
            p=jnp.exp(scores-lse)
            dp=dot_nt(vals,gg)
            return p.astype(BF),(p*(dp-delta)).astype(BF)
        far=jnp.where(far_mask(pos,start),dot_nt(key_far,qq),NEG)
        p,ds=one(far,val_far)
        dv_far=dv_far+dot_nn(p,gg); dk_far=dk_far+dot_nn(ds,qq)
        dq_t=dq_t+dot_nn(key_far_t,ds)
        parts=masked_scores(dot_nt(k_ref[lo:hi,:],qq),start,length,low_ok,high_ok)
        plist=[];dlist=[]
        for n,part in enumerate(parts):
            a=lo+n*QB
            p,ds=one(part,v_ref[a:a+QB,:])
            plist.append(p);dlist.append(ds)
        p=jnp.concatenate(plist,axis=0); ds=jnp.concatenate(dlist,axis=0)
        dv_acc[lo:hi,:]+=dot_nn(p,gg)
        dk_acc[lo:hi,:]+=dot_nn(ds,qq)
        dq_t=dq_t+dot_nn(key_t[:,lo:hi],ds)
        dq_ref[start:start+QB,:]=(pick_head(dq_t).T.astype(BF).astype(F32)*(HEAD_DIM**-0.5)).astype(BF)
    dk_ref[...]=(dk_acc[...]+lax.dot_general(sel_full,dk_far,(((0,),(0,)),((),())),preferred_element_type=F32,precision=lax.Precision.HIGHEST)).astype(BF)
    dv_ref[...]=(dv_acc[...]+lax.dot_general(sel_full,dv_far,(((0,),(0,)),((),())),preferred_element_type=F32,precision=lax.Precision.HIGHEST)).astype(BF)

def attn_bwd(pos,q,k,v,grad,ctx,lse,first,pairs):
    length,width=q.shape
    col=pl.BlockSpec((length,128),lambda i:(0,first+i))
    out_col=pl.BlockSpec((length,128),lambda i:(0,i))
    out=jax.ShapeDtypeStruct((length,128*pairs),BF)
    return pl.pallas_call(bwd_kernel,grid=(pairs,),
        in_specs=[pl.BlockSpec((16,1),lambda i:(0,0)),col,col,col,col,col,pl.BlockSpec((1,8,length),lambda i:(first+i,0,0))],
        out_specs=[out_col,out_col,out_col],
        out_shape=[out,out,out],
        scratch_shapes=[pltpu.VMEM((length,128),F32),pltpu.VMEM((length,128),F32),pltpu.VMEM((length,128),BF)],
        compiler_params=params(),
        cost_estimate=cost(COST,1<<20),
        name="attend_back")(pos,q,k,v,grad,ctx,lse)


ANY=pl.BlockSpec(memory_space=pl.ANY)
SMEM=pl.BlockSpec(memory_space=pltpu.SMEM)
RB=256

def cost(flops,nbytes,trans=0):
    return pl.CostEstimate(flops=int(flops),bytes_accessed=int(nbytes),transcendentals=int(trans))

def params(mib=60):
    return pltpu.CompilerParams(vmem_limit_bytes=mib<<20)

def fetches(pieces,place,sems,me,first,rows,sem0):
    out=[]
    for slot,piece in enumerate(pieces):
        owner=me^slot
        out.append(pltpu.make_async_copy(piece.at[pl.ds(first,rows)],place.at[pl.ds(pl.multiple_of(owner*rows,rows),rows)],sems.at[sem0+slot]))
    return out

def ffn_in_copies(refs,place,sems,sem0):
    if len(refs)>1: return [pltpu.make_async_copy(refs[0],place,sems.at[sem0])]
    pack=refs[0]; n,_,width=pack.shape; shard=place.shape[0]//n
    return [pltpu.make_async_copy(pack.at[s,pl.ds(j*shard,shard)],place.at[pl.ds(s*shard,shard),pl.ds(j*width,width)],sems.at[sem0+s*(place.shape[1]//width)+j])
            for s in range(n) for j in range(place.shape[1]//width)]


def ffn_back_copies(refs,place,sems,sem0):
    if len(refs)>1: return [pltpu.make_async_copy(refs[1],place,sems.at[sem0])]
    pack=refs[0]; n,rows,width=pack.shape; shard=place.shape[0]//n; first=rows-4*(width//n)-shard
    return [pltpu.make_async_copy(pack.at[s,pl.ds(first,shard)],place.at[pl.ds(s*shard,shard)],sems.at[sem0+s]) for s in range(n)]


def plane_copies(refs,plane,place,sems,sem0):
    width=place.shape[0]
    if len(refs)>1: return [pltpu.make_async_copy(refs[2].at[pl.ds(plane*width,width)],place,sems.at[sem0])]
    pack=refs[0]; n,rows,_=pack.shape; shard=width//n; first=rows-(4-plane)*shard
    return [pltpu.make_async_copy(pack.at[s,pl.ds(first,shard)],place.at[pl.ds(s*shard,shard)],sems.at[sem0+s]) for s in range(n)]


def stats(value):
    center=value-jnp.mean(value,axis=-1,keepdims=True)
    inverse=lax.rsqrt(jnp.mean(center*center,axis=-1,keepdims=True)+NORM_EPS)
    return center*inverse,inverse

def norm_back(scaled,normed,inverse):
    return inverse*(scaled-jnp.mean(scaled,axis=-1,keepdims=True)-normed*jnp.mean(scaled*normed,axis=-1,keepdims=True))

def gelu_pair(inner):
    cdf=0.5*(1.0+lax.erf(inner*0.7071067811865476))
    return inner*cdf, cdf+inner*(0.3989422804014327*jnp.exp(-0.5*inner*inner))

def ffn_up(pos,ctx,ctxg,x,ffw,vecs,c_row,n):
    length,width=x.shape
    ff=c_row.shape[1]; w=len(ffw)
    def body(pos_ref,ctx_ref,glob_ref,x_ref,vec_ref,c_ref,*refs):
        ff_w=refs[:w]
        hat_ref,inv_ref,low_ref,act_ref,slope_ref,merged_ref,wout,win,sems=refs[w:]
        @pl.when(pl.program_id(0)==0)
        def _():
            cps=plane_copies(ff_w,3,wout,sems,0)+ffn_in_copies(ff_w,win,sems,n)
            for c in cps: c.start()
            for c in cps: c.wait()
        token=pl.program_id(0)*RB+lax.broadcasted_iota(jnp.int32,(16,RB),1)
        hot=jnp.where(token==pos_ref[...],1.0,0.0).astype(BF)
        is_glob=dot_tn(hot,jnp.ones((16,128),BF))[:,0:1]>0.5
        merged=jnp.where(is_glob,dot_tn(hot,glob_ref[...]),ctx_ref[...].astype(F32)).astype(BF)
        merged_ref[...]=merged
        attended=dot_nn(merged,wout[...])+vec_ref[4:5,:]
        hat,inv=stats(x_ref[...].astype(F32)+attended)
        hat_ref[...]=hat; inv_ref[...]=inv
        low=(hat*vec_ref[6:7,:]+vec_ref[8:9,:]).astype(BF)
        low_ref[...]=low
        for a in range(0,ff,768):
            inner=dot_nn(low,win[:,a:a+768])+c_ref[:,a:a+768]
            act,slope=gelu_pair(inner)
            act_ref[:,a:a+768]=act.astype(BF); slope_ref[:,a:a+768]=slope.astype(BF)
    blk=lambda w:pl.BlockSpec((RB,w),lambda i:(i,0))
    full=lambda s:pl.BlockSpec(s,lambda i:(0,0))
    return pl.pallas_call(body,grid=(length//RB,),
        in_specs=[full(pos.shape),blk(width),full(ctxg.shape),blk(width),full(vecs.shape),full(c_row.shape)]+[ANY]*w,
        out_specs=[blk(width),blk(1),blk(width),blk(ff),blk(ff),blk(width)],
        out_shape=[jax.ShapeDtypeStruct((length,width),F32),jax.ShapeDtypeStruct((length,1),F32),jax.ShapeDtypeStruct((length,width),BF),
                   jax.ShapeDtypeStruct((length,ff),BF),jax.ShapeDtypeStruct((length,ff),BF),jax.ShapeDtypeStruct((length,width),BF)],
        scratch_shapes=[pltpu.VMEM((width,width),BF),pltpu.VMEM((width,ff),BF),pltpu.SemaphoreType.DMA((n+n*(ff//width),))],
        compiler_params=params(),cost_estimate=cost(COST,1<<20),name="ffn_up")(pos,ctx,ctxg,x,vecs,c_row,*ffw)

def chunk_store(chunks,me,value):
    for slot,chunk in enumerate(chunks):
        @pl.when(pl.program_id(0)^me==slot)
        def _(chunk=chunk): chunk[...]=value


def ffn_back(mez,active,slope,hat1,inv1,upstream,ffw,vecs,n):
    length,width=hat1.shape
    ff=active.shape[1]; w=len(ffw); steps=length//RB
    def body(mez_ref,act_ref,slope_ref,hat_ref,inv_ref,up_ref,vec_ref,*refs):
        ff_w=refs[:w]; chunks=refs[w:w+steps]; refs=refs[:w]+refs[w+steps:]
        bg_ref,ig_ref,gs_ref,ag_ref,mg_ref,vg_ref,cg_ref,wout,win,wback,sems=refs[w:]
        cb=ffn_back_copies(ff_w,wback,sems,0)
        ci=ffn_in_copies(ff_w,win,sems,2*n)
        co=plane_copies(ff_w,3,wout,sems,n)
        first=pl.program_id(0)==0
        @pl.when(first)
        def _():
            for c in cb+ci+co: c.start()
            vg_ref[...]=jnp.zeros_like(vg_ref); cg_ref[...]=jnp.zeros_like(cg_ref)
            for c in cb: c.wait()
        hat1v=hat_ref[...]
        norm1=hat1v*vec_ref[6:7,:]+vec_ref[8:9,:]
        branch=dot_nn(act_ref[...],wback[...])+vec_ref[5:6,:]
        hat2,inv2=stats(norm1+branch)
        chunk_store(chunks,mez_ref[0],(hat2*vec_ref[7:8,:]+vec_ref[9:10,:]).astype(BF))
        up=up_ref[...].astype(F32)
        col=lambda v:jnp.sum(v,axis=0,keepdims=True)
        vg_ref[7:8,:]+=col(up*hat2); vg_ref[9:10,:]+=col(up)
        second=norm_back(up*vec_ref[7:8,:],hat2,inv2)
        bg=second.astype(BF)
        bg_ref[...]=bg
        vg_ref[5:6,:]+=col(bg.astype(F32))
        @pl.when(first)
        def _():
            for c in ci+co: c.wait()
        acc=second
        for a in range(0,ff,768):
            ig=(dot_nt(bg,wback[a:a+768,:])*slope_ref[:,a:a+768].astype(F32)).astype(BF)
            ig_ref[:,a:a+768]=ig
            cg_ref[:,a:a+768]+=col(ig.astype(F32))
            acc=acc+dot_nt(ig,win[:,a:a+768])
        vg_ref[6:7,:]+=col(acc*hat1v); vg_ref[8:9,:]+=col(acc)
        gs=norm_back(acc*vec_ref[6:7,:],hat1v,inv_ref[...])
        gs_ref[...]=gs
        ag=gs.astype(BF)
        ag_ref[...]=ag
        vg_ref[4:5,:]+=col(ag.astype(F32))
        mg_ref[...]=dot_nt(ag,wout[...]).astype(BF)
    blk=lambda w:pl.BlockSpec((RB,w),lambda i:(i,0))
    full=lambda s:pl.BlockSpec(s,lambda i:(0,0))
    return pl.pallas_call(body,grid=(length//RB,),
        in_specs=[SMEM,blk(ff),blk(ff),blk(width),blk(1),blk(width),full(vecs.shape)]+[ANY]*w,
        out_specs=[full((RB,width))]*steps+[blk(width),blk(ff),blk(width),blk(width),blk(width),full((16,width)),full((1,ff))],
        out_shape=[S((RB,width),BF)]*steps+[S((length,width),BF),S((length,ff),BF),S((length,width),F32),S((length,width),BF),S((length,width),BF),S((16,width),F32),S((1,ff),F32)],
        scratch_shapes=[pltpu.VMEM((width,width),BF),pltpu.VMEM((width,ff),BF),pltpu.VMEM((ff,width),BF),pltpu.SemaphoreType.DMA((2*n+n*(ff//width),))],
        compiler_params=params(),cost_estimate=cost(COST,1<<20),name="ffn_back")(mez,active,slope,hat1,inv1,upstream,vecs,*ffw)

def ffn_grads(low,inner,active,branch,count):
    length,width=low.shape; ff=active.shape[1]; shard=width//count; fs=ff//count; blocks=ff//width
    shape=S((count,blocks*shard+fs,width),BF)
    def in_body(l_ref,r_ref,o_ref,lt):
        @pl.when(pl.program_id(0)==0)
        def _(): lt[...]=l_ref[...].T
        o_ref[...]=dot_nn(lt[...],r_ref[...]).reshape(count,shard,width).astype(BF)
    pack=pl.pallas_call(in_body,grid=(blocks,),
        in_specs=[pl.BlockSpec((length,width),lambda j:(0,0)),pl.BlockSpec((length,width),lambda j:(0,j))],
        out_specs=pl.BlockSpec((count,shard,width),lambda j:(0,j,0)),out_shape=shape,
        scratch_shapes=[pltpu.VMEM((width,length),BF)],
        compiler_params=params(),cost_estimate=cost(COST,1<<20),name="ffn_in_grad")(low,inner)
    def back_body(p_ref,l_ref,r_ref,o_ref):
        o_ref[0]=dot_tn(l_ref[...],r_ref[...]).astype(BF)
    return pl.pallas_call(back_body,grid=(count,),
        in_specs=[ANY,pl.BlockSpec((length,fs),lambda s:(0,s)),pl.BlockSpec((length,width),lambda s:(0,0))],
        out_specs=pl.BlockSpec((1,fs,width),lambda s:(s,blocks*shard//fs,0)),out_shape=shape,
        input_output_aliases={0:0},
        compiler_params=params(),cost_estimate=cost(COST,1<<20),name="ffn_back_grad")(pack,active,branch)


def local_grads(me,x,grads,unit=None,vec=None,count=8):
    length,width=x.shape; cols=grads[0].shape[1]; shard=width//count; half=count//2; k=len(grads)
    tail=0 if vec is None else 16
    rows=k*shard+tail
    base=0 if unit is None else unit[0].shape[1]-rows
    extra=([] if vec is None else [vec])+([] if unit is None else list(unit))
    def body(me_ref,x_ref,*refs):
        outs=refs[k+len(extra):]
        keep,send,res,keep_v,send_v,vec_v,sems=outs
        m=me_ref[0]
        xt=x_ref[...].T
        for r in range(k):
            res[...]=dot_nn(xt,refs[r][...])
            for slot in range(count):
                part=res[pl.ds(pl.multiple_of((m^slot)*shard,shard),shard),:]
                (send_v if slot%2 else keep_v)[slot//2,r*shard:(r+1)*shard,:]=part.astype(BF)
        if vec is not None:
            vec_v[...]=jnp.zeros_like(vec_v)
            for s in range(count):
                vec_v[s,:,0:shard]=refs[k][:,s*shard:(s+1)*shard]
            for slot in range(count):
                (send_v if slot%2 else keep_v)[slot//2,k*shard:rows,:]=vec_v[m^slot].astype(BF)
        cps=[pltpu.make_async_copy(v,o.at[:,pl.ds(base,rows)],sems.at[i]) for i,(v,o) in enumerate(((keep_v,keep),(send_v,send)))]
        for c in cps: c.start()
        for c in cps: c.wait()
    o=S((half,base+rows,cols),BF)
    vm=pl.BlockSpec(memory_space=pltpu.VMEM)
    first=1+1+k+(0 if vec is None else 1)
    return pl.pallas_call(body,in_specs=[SMEM]+[vm]*(first-1)+[ANY]*(0 if unit is None else 2),out_specs=[ANY]*2,out_shape=[o,o],
        input_output_aliases={} if unit is None else {first:0,first+1:1},
        scratch_shapes=[pltpu.VMEM((width,cols),F32),pltpu.VMEM((half,rows,cols),BF),pltpu.VMEM((half,rows,cols),BF),pltpu.VMEM((count,16,cols),F32),pltpu.SemaphoreType.DMA((2,))],
        compiler_params=params(),cost_estimate=cost(COST,1<<20),name="local_grads")(me,x,*grads,*extra)


def collect(mez,pieces):
    def body(mez_ref,*refs):
        for slot in range(len(pieces)):
            @pl.when(pl.program_id(0)^mez_ref[0]==slot)
            def _(slot=slot): refs[-1][0]=refs[slot][...]
    rows,width=pieces[0].shape; n=len(pieces)
    return pl.pallas_call(body,grid=(n,),in_specs=[SMEM]+[pl.BlockSpec((rows,width),lambda i:(0,0))]*n,
        out_specs=pl.BlockSpec((1,rows,width),lambda i:(i,0,0)),out_shape=S((n,rows,width),BF),
        compiler_params=params(),cost_estimate=cost(COST,1<<20),name="collect")(mez,*pieces)


def project(me,x,pieces,vecs):
    length,width=x.shape; n=len(pieces); shard=width//n
    def body(me_ref,x_ref,vec_ref,*refs):
        ins=refs[:n]; q_ref,k_ref,v_ref,wts,sems=refs[n:]
        m=me_ref[0]
        cps=[fetches(ins,wts.at[j],sems,m,j*shard,shard,j*n) for j in range(3)]
        for j in range(3):
            for c in cps[j]: c.start()
        for c in cps[0]: c.wait()
        scale=HEAD_DIM**-0.5
        for a in range(0,length,RB):
            q_ref[a:a+RB,:]=((dot_nn(x_ref[a:a+RB,:],wts[0])+vec_ref[0:1,:])*scale).astype(BF)
        for c in cps[1]: c.wait()
        for a in range(0,length,RB):
            k_ref[a:a+RB,:]=dot_nn(x_ref[a:a+RB,:],wts[1]).astype(BF)
        for c in cps[2]: c.wait()
        for a in range(0,length,RB):
            v_ref[a:a+RB,:]=(dot_nn(x_ref[a:a+RB,:],wts[2])+vec_ref[1:2,:]).astype(BF)
    vm=pl.BlockSpec(memory_space=pltpu.VMEM)
    return pl.pallas_call(body,in_specs=[SMEM,vm,vm]+[ANY]*n,out_specs=[vm]*3,out_shape=[S((length,width),BF)]*3,
        scratch_shapes=[pltpu.VMEM((3,width,width),BF),pltpu.SemaphoreType.DMA((3*n,))],
        compiler_params=params(),cost_estimate=cost(COST,1<<20),name="project")(me,x,vecs,*pieces)

def own_mask(width):
    return lax.broadcasted_iota(jnp.int32,(16,width),0)==lax.broadcasted_iota(jnp.int32,(16,width),1)//HEAD_DIM

def one_hot(pos,length):
    return jnp.where(lax.broadcasted_iota(jnp.int32,(16,length),1)==pos,1.0,0.0)

def scatter_heads(rows,own,count):
    zero=jnp.zeros((16,rows.shape[1]),F32)
    return jnp.concatenate([jnp.where(own,jnp.broadcast_to(rows[g:g+1,:].astype(F32),zero.shape),zero) for g in range(count)],axis=0).astype(BF)

def gather_heads(value,own,count):
    rows=[jnp.sum(jnp.where(own,value[16*g:16*g+16],0.0),axis=0,keepdims=True) for g in range(count)]
    rows.append(jnp.zeros((16-count,value.shape[1]),F32))
    return jnp.concatenate(rows,axis=0)

def globals_fwd(pos,x,ffw,vecs,count,n):
    length,width=x.shape; wide=16*count; w=len(ffw)
    def body(pos_ref,x_ref,vec_ref,*refs):
        ins=refs[:w]; ctx_ref,p_ref,u_ref,y_ref,q_ref,r_ref,wts,sems=refs[w:]
        cps=[plane_copies(ins,j,wts.at[j],sems,j*n) for j in range(3)]
        for j in range(3):
            for c in cps[j]: c.start()
        own=own_mask(width)
        sel=one_hot(pos_ref[...],length).astype(BF)
        rows=dot_nn(sel,x_ref[...]).astype(BF)
        r_ref[...]=rows
        for c in cps[0]: c.wait()
        q=((dot_nn(rows,wts[0])+vec_ref[2:3,:])*(HEAD_DIM**-0.5)).astype(BF)
        q_ref[...]=q
        for c in cps[1]: c.wait()
        u=dot_nt(wts[1],scatter_heads(q,own,count)).astype(BF)
        u_ref[...]=u
        s=dot_nn(x_ref[...],u)
        p=jnp.exp(s-jnp.max(s,axis=0,keepdims=True))
        p=p/jnp.sum(p,axis=0,keepdims=True)
        p_ref[...]=p
        low=p.astype(BF)
        y=dot_tn(low,x_ref[...]).astype(BF)
        y_ref[...]=y
        mass=dot_tn(low,jnp.ones((length,128),BF))[:,0:1]
        for c in cps[2]: c.wait()
        ctx_ref[...]=gather_heads(dot_nn(y,wts[2])+mass*vec_ref[3:4,:],own,count).astype(BF)
    vm=pl.BlockSpec(memory_space=pltpu.VMEM)
    return pl.pallas_call(body,in_specs=[vm,vm,vm]+[ANY]*w,out_specs=[vm]*6,
        out_shape=[S((16,width),BF),S((length,wide),F32),S((width,wide),BF),S((wide,width),BF),S((16,width),BF),S((16,width),BF)],
        scratch_shapes=[pltpu.VMEM((3,width,width),BF),pltpu.SemaphoreType.DMA((3*n,))],
        compiler_params=params(),cost_estimate=cost(COST,1<<20),name="globals")(pos,x,vecs,*ffw)

def globals_bwd(me,pos,x,mg,gs,p,u,y,q,rows,merged,ag,ffw,vecs,count,n,extra):
    length,width=x.shape; shard=width//n; half=max(n//2,1); w=len(ffw); cols=width//2
    def body(me_ref,pos_ref,x_ref,mg_ref,gs_ref,p_ref,u_ref,y_ref,q_ref,r_ref,merged_ref,ag_ref,vec_ref,*refs):
        ins=refs[:w]; out_ref,keep,send,keep2,send2,vg_ref,wts,res,keep_v,send_v,sems=refs[w:]
        m=me_ref[0]
        cps=[plane_copies(ins,j,wts.at[j],sems,j*n) for j in range(3)]
        for j in (2,1,0):
            for c in cps[j]: c.start()
        own=own_mask(width)
        hot=one_hot(pos_ref[...],length)
        sel=hot.astype(BF)
        x=x_ref[...]
        cs=scatter_heads(dot_nn(sel,mg_ref[...]).astype(BF),own,count)
        qs=scatter_heads(q_ref[...],own,count)
        for c in cps[2]: c.wait()
        v=dot_nt(wts[2],cs).astype(BF)
        shift=dot_nt(jnp.broadcast_to(vec_ref[3:4,:],(16,width)).astype(BF),cs)[0:1,:]
        dp=dot_nn(x,v)+shift
        p=p_ref[...]
        low=p.astype(BF)
        ds=(p*(dp-jnp.sum(p*dp,axis=0,keepdims=True))).astype(BF)
        a=dot_tn(ds,x).astype(BF)
        for c in cps[1]: c.wait()
        pre=(gather_heads(dot_nn(a,wts[1]),own,count).astype(BF).astype(F32)*(HEAD_DIM**-0.5)).astype(BF)
        for c in cps[0]: c.wait()
        rows_grad=dot_nt(pre,wts[0])
        mass=dot_tn(low,jnp.ones((length,128),BF))[:,0:1]
        vg_ref[...]=jnp.zeros_like(vg_ref)
        vg_ref[2:3,:]=jnp.sum(pre.astype(F32),axis=0,keepdims=True)
        vg_ref[3:4,:]=jnp.sum(mass*cs.astype(F32),axis=0,keepdims=True)
        out_ref[...]=gs_ref[...]+dot_nt(ds,u_ref[...])+dot_nt(low,v)+lax.dot_general(hot,rows_grad,(((0,),(0,)),((),())),preferred_element_type=F32,precision=lax.Precision.HIGHEST)
        for j,(l,r) in enumerate(((r_ref[...],pre),(a,qs),(y_ref[...],cs),(merged_ref[...],ag_ref[...]))):
            res[...]=dot_tn(l,r)
            for slot in range(n):
                for h in range(2):
                    part=res[pl.ds(pl.multiple_of((m^slot)*shard,shard),shard),h*cols:(h+1)*cols]
                    (send_v if slot%2 else keep_v)[slot//2,(2*j+h)*shard:(2*j+h+1)*shard,:]=part.astype(BF)
        cps=[]
        for here,first,there in ((keep_v,0,keep),(keep_v,6*shard,keep2),(send_v,0,send),(send_v,6*shard,send2)):
            if n==1 and here is send_v: continue
            rows_out=6*shard if first==0 else 2*shard
            cps.append(pltpu.make_async_copy(here.at[:,pl.ds(first,rows_out)],there.at[:,pl.ds(0,rows_out)],sems.at[3*n+len(cps)]))
        for c in cps: c.start()
        for c in cps: c.wait()
    vm=pl.BlockSpec(memory_space=pltpu.VMEM)
    o1=S((half,6*shard,cols),BF)
    o2=S((half,2*shard+extra,cols),BF)
    return pl.pallas_call(body,in_specs=[SMEM]+[vm]*12+[ANY]*w,out_specs=[vm,ANY,ANY,ANY,ANY,vm],
        out_shape=[S((length,width),F32),o1,o1,o2,o2,S((16,width),F32)],
        scratch_shapes=[pltpu.VMEM((3,width,width),BF),pltpu.VMEM((width,width),F32),pltpu.VMEM((half,8*shard,cols),BF),pltpu.VMEM((half,8*shard,cols),BF),pltpu.SemaphoreType.DMA((3*n+4,))],
        compiler_params=params(),cost_estimate=cost(COST,1<<20),name="globals_back")(me,pos,x,mg,gs,p,u,y,q,rows,merged,ag,vecs,*ffw)


def inputs_back(me,mez,gs,groups,pieces):
    length,width=gs.shape; n=len(pieces); shard=width//n; g=len(groups); cols=width//g
    steps=length//RB
    def body(me_ref,mez_ref,gs_ref,*refs):
        parts=refs[:3*g]; ins=refs[3*g:3*g+n]; chunks=refs[3*g+n:3*g+n+steps]; vg_ref,wts,sems=refs[3*g+n+steps:]
        m=me_ref[0]
        @pl.when(pl.program_id(0)==0)
        def _():
            cps=sum([fetches(ins,wts.at[j],sems,m,j*shard,shard,j*n) for j in range(3)],[])
            for c in cps: c.start()
            vg_ref[...]=jnp.zeros_like(vg_ref)
            for c in cps: c.wait()
        acc=gs_ref[...]
        for j in range(g):
            a=j*cols
            for w in range(3): acc=acc+dot_nt(parts[3*j+w][...],wts[w,:,a:a+cols])
            vg_ref[0:1,a:a+cols]+=jnp.sum(parts[3*j][...].astype(F32),axis=0,keepdims=True)
            vg_ref[1:2,a:a+cols]+=jnp.sum(parts[3*j+2][...].astype(F32),axis=0,keepdims=True)
        chunk_store(chunks,mez_ref[0],acc.astype(BF))
    blk=pl.BlockSpec((RB,width),lambda i:(i,0))
    part=pl.BlockSpec((RB,cols),lambda i:(i,0))
    return pl.pallas_call(body,grid=(length//RB,),in_specs=[SMEM,SMEM,blk]+[part]*(3*g)+[ANY]*n,
        out_specs=[pl.BlockSpec((RB,width),lambda i:(0,0))]*steps+[pl.BlockSpec((16,width),lambda i:(0,0))],out_shape=[S((RB,width),BF)]*steps+[S((16,width),F32)],
        scratch_shapes=[pltpu.VMEM((3,width,width),BF),pltpu.SemaphoreType.DMA((3*n,))],
        compiler_params=params(),cost_estimate=cost(COST,1<<20),name="inputs_back")(me,mez,gs,*[p for t in groups for p in t],*pieces)


def flip(value, axis, bit):
    count = lax.axis_size(axis)
    return lax.ppermute(value, axis, [(index, index ^ bit) for index in range(count)])


def tie(value, *others):
    return lax.optimization_barrier((value,) + others)[0]


def spread_slots(unit, order):
    slots = {0: unit}
    for bit in order:
        for slot in list(slots):
            slots[slot | bit] = flip(slots[slot], "fsdp", bit)
    return [slots[slot] for slot in range(len(slots))]


def add(one, two):
    return one.astype(F32) + two.astype(F32)


def meet(values, parts, *others):
    flat = [list(part.got) if isinstance(part.got, list) else [part.got] for part in parts]
    joined = tuple(values) + tuple(got for gots in flat for got in gots) + others
    joined = list(lax.optimization_barrier(joined))
    values = [joined.pop(0) for _ in values]
    for part, gots in zip(parts, flat):
        new = [joined.pop(0) for _ in gots]
        part.got = new if isinstance(part.got, list) else new[0]
    return values


class Exchange:
    def __init__(self, chunks):
        self.got = [chunks[0]] + [flip(chunks[k], "sp", k) for k in range(1, len(chunks))]


class Reduction:
    def __init__(self, keep, send, x_first):
        self.keep, self.first, self.step = keep, send, 0
        self.got = flip(send, "fsdp", 1)
        self.x_first = x_first

    def advance(self, *gates):
        got = tie(self.got, *gates)
        x_now = self.x_first == (self.step == 0)
        if self.step == 0:
            keep = self.keep.reshape((2, 2) + self.keep.shape[1:])
            got = got.reshape(keep.shape)
            if self.x_first:
                away, here = (keep[:, 1], got[:, 1]), (keep[:, 0], got[:, 0])
            else:
                away, here = (keep[1], got[1]), (keep[0], got[0])
        else:
            away, here = (self.mine[1], got[1]), (self.mine[0], got[0])
        self.send, self.mine = add(*away).astype(BF), add(*here)
        self.got = flip(self.send, "fsdp", 2 if x_now else 4)
        self.step += 1
        return self.send

    def total(self):
        return add(self.mine, self.got)


class SpSum:
    def __init__(self, value, start=True):
        self.low, self.high = lax.axis_index("sp") & 1, lax.axis_index("sp") >> 1
        rows = value.shape[0] // 4
        self.shape = value.shape
        self.value = value.reshape(2, 2, rows, value.shape[1])
        self.got = self.value
        self.step = 0
        if start:
            self.start()

    def start(self):
        self.value = self.got
        self.exchange(self.low, 1)

    def exchange(self, mine, bit):
        send = lax.dynamic_index_in_dim(self.value, 1 - mine, 0, keepdims=False).astype(BF)
        self.value = lax.dynamic_index_in_dim(self.value, mine, 0, keepdims=False)
        self.send, self.got = send, flip(send, "sp", bit)

    def join(self, mine):
        return jnp.stack(
            [jnp.where(mine == 0, self.value, self.got), jnp.where(mine == 0, self.got, self.value)]
        )

    def advance(self):
        if self.step == 0:
            self.value = add(self.value, self.got)
            self.exchange(self.high, 2)
        elif self.step == 1:
            self.value = add(self.value, self.got).astype(BF)
            self.got = flip(self.value, "sp", 2)
        else:
            self.value = self.join(self.high)
            self.got = flip(self.value, "sp", 1)
        self.step += 1

    def total(self):
        return self.join(self.low).reshape(self.shape).astype(F32)


def per_device(
    inputs,
    global_pos,
    w_local,
    w_global,
    w_out,
    b_proj,
    gains,
    shifts,
    w_in,
    c_in,
    w_back,
    cotangent,
):
    sp_count = lax.axis_size("sp")
    fsdp_count = lax.axis_size("fsdp")
    sp_index = lax.axis_index("sp")
    fsdp_index = lax.axis_index("fsdp")
    own_seqs = inputs.shape[0] // sp_count
    glob_count = global_pos.shape[1]
    shard, width = w_out.shape
    ff_shard = w_back.shape[0]
    ff_width = w_in.shape[1]
    tree = fsdp_count == 8 and sp_count == 4 and own_seqs == 1 and shard % 32 == 0
    tree = tree and inputs.shape[1] == RB

    def to_sequence(value):
        if own_seqs == 1:
            moved = lax.all_to_all(value, "sp", split_axis=0, concat_axis=0)
            return moved.reshape(1, -1, width)
        return lax.all_to_all(value, "sp", split_axis=0, concat_axis=1, tiled=True)

    def to_tokens(values):
        if own_seqs == 1:
            return lax.all_to_all(
                values[0].reshape(sp_count, -1, width), "sp", split_axis=0, concat_axis=0
            )
        return lax.all_to_all(jnp.stack(values), "sp", split_axis=1, concat_axis=0, tiled=True)

    own_pos = lax.dynamic_slice_in_dim(global_pos, sp_index * own_seqs, own_seqs, 0)
    blocks = ff_width // width
    x_all = to_sequence(inputs)
    vec_rows = [b_proj, gains, shifts, c_in.reshape(-1, shard)]
    small = jnp.concatenate(vec_rows, axis=0)
    small = jnp.pad(small, ((0, 16 - small.shape[0]), (0, 0)))
    if tree:
        me = fsdp_index.reshape(1).astype(jnp.int32)
        mez = sp_index.reshape(1).astype(jnp.int32)
        first = jnp.concatenate(
            [w_local.reshape(-1, width), jnp.pad(small, ((0, 0), (0, width - shard)))], axis=0
        )
        local_w = spread_slots(first, (2, 4, 1))
        pack = jnp.concatenate(
            [
                w_in.reshape(shard, blocks, width).transpose(1, 0, 2).reshape(-1, width),
                w_back,
                w_global.reshape(-1, width),
                w_out,
            ],
            axis=0,
        )
        ffw = [lax.all_gather(pack, "fsdp")]
        small_all = jnp.stack([piece[3 * shard :, :shard] for piece in local_w])
        small_all = small_all[me[0] ^ jnp.arange(fsdp_count, dtype=jnp.int32)]
    else:
        me = mez = jnp.zeros((1,), jnp.int32)
        local_w = [lax.all_gather(w_local, "fsdp", axis=1, tiled=True).reshape(-1, width)]
        full_global = lax.all_gather(w_global, "fsdp", axis=1, tiled=True).reshape(-1, width)
        full_out = lax.all_gather(w_out, "fsdp", axis=0, tiled=True)
        ffw = [lax.all_gather(value, "fsdp", axis=0, tiled=True) for value in (w_in, w_back)]
        ffw.append(jnp.concatenate([full_global, full_out], axis=0))
        small_all = lax.all_gather(small, "fsdp")
    count = len(local_w)
    up_all = to_sequence(tie(cotangent, x_all))
    vecs = small_all.transpose(1, 0, 2).reshape(16, width).astype(F32)
    c_rows = small_all[:, 10 : 10 + ff_shard // shard].astype(F32)
    c_row = c_rows.reshape(1, ff_width)

    outs, input_grads, totals = [], [], None
    for index in range(own_seqs):
        x = x_all[index]
        pos = jnp.full((16, 1), -1, jnp.int32).at[:glob_count, 0].set(own_pos[index])
        q, k, v = project(me, x, local_w, vecs)
        ctx, lse = attn_fwd(pos, q, k, v)
        ctx_glob, probs, keys, mixed, query, rows = globals_fwd(
            pos, x, ffw, vecs, glob_count, count
        )
        hat, inv, low, active, slope, merged = ffn_up(
            pos, ctx, ctx_glob, x, ffw, vecs, c_row, count
        )
        *out, branch, inner, grad_sum, attn_grad, merged_grad, vec_one, c_grad = ffn_back(
            mez, active, slope, hat, inv, up_all[index], ffw, vecs, count
        )
        if tree:
            out_moved = Exchange(out)
        else:
            outs.append(jnp.concatenate(out, axis=0))
        if tree:
            ff_pack = ffn_grads(low, inner, active, branch, fsdp_count)
            ff_mine = lax.psum_scatter(ff_pack, "fsdp", scatter_dimension=0, tiled=False)
            merged_grad = tie(merged_grad, ff_pack)
        grad_sum, keep_one, send_one, keep_two, send_two, vec_two = globals_bwd(
            me,
            pos,
            x,
            merged_grad,
            grad_sum,
            probs,
            keys,
            mixed,
            query,
            rows,
            merged,
            attn_grad,
            ffw,
            vecs,
            glob_count,
            count,
            3 * shard if tree else 0,
        )
        group_pairs = width // 128 // GROUPS
        groups = []
        if tree:
            one = Reduction(keep_one, send_one, True)
            merged_grad = tie(merged_grad, send_one)
        for group in range(GROUPS):
            parts = attn_bwd(
                pos, q, k, v, merged_grad, ctx, lse, group * group_pairs, group_pairs
            )
            groups.append(parts)
            if tree and group == 0:
                two = Reduction(*local_grads(me, x, parts, unit=(keep_two, send_two)), False)
                (merged_grad,) = meet([merged_grad], [out_moved], two.first)
        if tree:
            (grad_sum,) = meet([grad_sum], [one, two], parts[0])
            grad_sum = tie(grad_sum, one.advance(), two.advance())
        *input_grad, vec_three = inputs_back(me, mez, grad_sum, groups, local_w)
        if tree:
            grads_moved = Exchange(input_grad)
        else:
            input_grads.append(jnp.concatenate(input_grad, axis=0))
        c_grad = c_grad.reshape(fsdp_count, -1, shard).transpose(1, 0, 2).reshape(-1, width)
        vec = vec_one + vec_two + vec_three + jnp.pad(c_grad, ((10, 6 - c_grad.shape[0]), (0, 0)))
        if not tree:
            g_mixed = jnp.concatenate([keep_one[0], keep_two[0]], axis=0)
            g_mixed = g_mixed.reshape(4, 2, width, width // 2).transpose(0, 2, 1, 3)
            grads = (
                dot_tn(active, branch),
                dot_tn(low, inner),
                g_mixed.reshape(4, width, width).astype(F32),
                jnp.stack(
                    [
                        jnp.concatenate([dot_tn(x, part[w]) for part in groups], axis=1)
                        for w in range(3)
                    ]
                ),
                vec,
            )
            totals = grads if totals is None else tuple(a + b for a, b in zip(totals, grads))
    if tree:
        x_late, ff_mine = meet([x, ff_mine], [], *input_grad)
        ff_sum = SpSum(ff_mine.astype(F32))
        x_late = tie(x_late, ff_sum.send)
        late = Reduction(*local_grads(me, x_late, groups[-1], vec=vec), False)
        meet([], [one, two, ff_sum, grads_moved], late.first)
        one.advance()
        two.advance()
        ff_sum.advance()
        meet([], [late], one.send, two.send, ff_sum.send)
        late.advance()
        meet([], [one, two, late, ff_sum])
        early_sum = SpSum(jnp.concatenate([one.total(), two.total()], axis=0))
        late.advance()
        ff_sum.advance()
        out = collect(mez, out_moved.got)
        meet([], [late, ff_sum, early_sum])
        late_sum = SpSum(late.total())
        early_sum.advance()
        ff_sum.advance()
        grad_inputs = collect(mez, grads_moved.got)
        meet([], [early_sum, late_sum, ff_sum])
        early_sum.advance()
        late_sum.advance()
        s_ff = ff_sum.total()
        meet([], [early_sum, late_sum])
        early_sum.advance()
        late_sum.advance()
        meet([], [early_sum, late_sum])
        late_sum.advance()
        s_early, s_late = early_sum.total(), late_sum.total()
        half_mixed = s_early[: 8 * shard].reshape(4, 2, shard, -1).transpose(0, 2, 1, 3)
        s_mixed = half_mixed.reshape(4, shard, width)
        s_local = jnp.concatenate(
            [
                s_early[8 * shard :].reshape(3, shard, -1),
                s_late[: 3 * shard].reshape(3, shard, -1),
            ],
            axis=2,
        )
        mine = s_late[3 * shard :, :shard]
        s_in = s_ff[: blocks * shard].reshape(blocks, shard, width).transpose(1, 0, 2)
        s_in = s_in.reshape(shard, ff_width)
        s_back = s_ff[blocks * shard :]
    else:
        out, grad_inputs = to_tokens(outs), to_tokens(input_grads)
        g_back, g_in, g_mixed, g_local, vec = totals

        def reduce(value, dim):
            mine = lax.psum_scatter(value.astype(BF), "fsdp", scatter_dimension=dim, tiled=True)
            return lax.psum(mine, "sp").astype(F32)

        s_back, s_in = reduce(g_back, 0), reduce(g_in, 0)
        s_mixed = reduce(g_mixed, 1)
        s_local = reduce(g_local, 1)
        vec = lax.psum(vec, ("fsdp", "sp"))
        mine = lax.dynamic_slice_in_dim(vec, fsdp_index * shard, shard, 1)
    c_mine = mine[10 : 10 + ff_shard // shard].reshape(-1)
    return (
        out,
        grad_inputs,
        s_local,
        s_mixed[:3],
        s_mixed[3],
        mine[:6],
        mine[6:8],
        mine[8:10],
        s_in,
        c_mine,
        s_back,
    )


def solution(mesh):
    rows = P("fsdp", None)
    tokens = P("fsdp", "sp", None)
    columns = P(None, "fsdp")
    stacked = P(None, "fsdp", None)
    return jax.shard_map(
        per_device,
        mesh=mesh,
        in_specs=(
            tokens,
            rows,
            stacked,
            stacked,
            rows,
            columns,
            columns,
            columns,
            rows,
            P("fsdp"),
            rows,
            tokens,
        ),
        out_specs=(
            tokens,
            tokens,
            stacked,
            stacked,
            rows,
            columns,
            columns,
            columns,
            rows,
            P("fsdp"),
            rows,
        ),
        check_vma=False,
    )
```

```python
import jax
import jax.numpy as jnp
from jax import lax
from jax.experimental import pallas as pl
from jax.experimental.pallas import tpu as pltpu
from jax.sharding import PartitionSpec as P

HEADS = 12
HEAD_DIM = 64
WIN = 256
QB = 128
NEG = -1e9
GROUPS = 2
COST = 2 * 10**10
NORM_EPS = 1e-05
BF = jnp.bfloat16
F32 = jnp.float32
S = jax.ShapeDtypeStruct


def dot_nn(a,b): return jnp.dot(a,b,preferred_element_type=F32)
def dot_nt(a,b): return lax.dot_general(a,b,(((1,),(1,)),((),())),preferred_element_type=F32)
def dot_tn(a,b): return lax.dot_general(a,b,(((0,),(0,)),((),())),preferred_element_type=F32)

def split_pair(block):
    lane=lax.broadcasted_iota(jnp.int32,block.shape,1)
    zero=jnp.zeros_like(block)
    return jnp.concatenate([jnp.where(lane<HEAD_DIM,block,zero),jnp.where(lane<HEAD_DIM,zero,block)],axis=0)

def far_mask(pos, start):
    place=start+lax.broadcasted_iota(jnp.int32,(16,2*QB),1)%QB
    return (pos>=0)&(jnp.abs(place-pos)>WIN)

def edge_masks():
    row=lax.broadcasted_iota(jnp.int32,(QB,2*QB),0)
    col=lax.broadcasted_iota(jnp.int32,(QB,2*QB),1)%QB
    return row>=col, row<=col

def key_range(start,length):
    return max(0,start-WIN), min(length,start+QB+WIN)

def pick_head(both):
    row=lax.broadcasted_iota(jnp.int32,(2*HEAD_DIM,QB),0)
    return jnp.where(row<HEAD_DIM,both[:,:QB],both[:,QB:])

def masked_scores(raw,start,length,low_ok,high_ok):
    lo,hi=key_range(start,length)
    parts=[]
    for first in range(lo,hi,QB):
        chunk=raw[first-lo:first-lo+QB]
        if first==start-WIN: chunk=jnp.where(low_ok,chunk,NEG)
        elif first==start+WIN: chunk=jnp.where(high_ok,chunk,NEG)
        parts.append(chunk)
    return parts

def fwd_kernel(pos_ref,q_ref,k_ref,v_ref,ctx_ref,lse_ref):
    length=q_ref.shape[0]
    pos=pos_ref[...]
    token=lax.broadcasted_iota(jnp.int32,(16,length),1)
    sel=jnp.where(token==pos,1.0,0.0).astype(BF)
    key_far=dot_nn(sel,k_ref[...]).astype(BF)
    val_far_t=dot_nn(sel,v_ref[...]).astype(BF).T
    val_t=v_ref[...].T
    low_ok,high_ok=edge_masks()
    for start in range(0,length,QB):
        lo,hi=key_range(start,length)
        qq=split_pair(q_ref[start:start+QB,:])
        raw=dot_nt(k_ref[lo:hi,:],qq)
        parts=masked_scores(raw,start,length,low_ok,high_ok)
        far=jnp.where(far_mask(pos,start),dot_nt(key_far,qq),NEG)
        top=jnp.max(far,axis=0,keepdims=True)
        for part in parts: top=jnp.maximum(top,jnp.max(part,axis=0,keepdims=True))
        far_p=jnp.exp(far-top)
        total=jnp.sum(far_p,axis=0,keepdims=True)
        probs=[]
        for part in parts:
            p=jnp.exp(part-top)
            total=total+jnp.sum(p,axis=0,keepdims=True)
            probs.append(p.astype(BF))
        both=dot_nn(val_t[:,lo:hi],jnp.concatenate(probs,axis=0))+dot_nn(val_far_t,far_p.astype(BF))
        both=both*(1.0/total)
        ctx_ref[start:start+QB,:]=pick_head(both).T.astype(BF)
        lse=top+jnp.log(total)
        lse_ref[0,0:1,start:start+QB]=lse[:,:QB]
        lse_ref[0,1:2,start:start+QB]=lse[:,QB:]

def attn_fwd(pos,q,k,v):
    length,width=q.shape
    pairs=width//128
    col=pl.BlockSpec((length,128),lambda i:(0,i))
    return pl.pallas_call(fwd_kernel,grid=(pairs,),
        in_specs=[pl.BlockSpec((16,1),lambda i:(0,0)),col,col,col],
        out_specs=[col,pl.BlockSpec((1,8,length),lambda i:(i,0,0))],
        out_shape=[jax.ShapeDtypeStruct((length,width),BF),jax.ShapeDtypeStruct((pairs,8,length),F32)],
        compiler_params=params(),
        cost_estimate=cost(COST,1<<20),
        name="attend")(pos,q,k,v)

def bwd_kernel(pos_ref,q_ref,k_ref,v_ref,g_ref,ctx_ref,lse_ref,dq_ref,dk_ref,dv_ref,dk_acc,dv_acc,grad_scr):
    length=q_ref.shape[0]
    pos=pos_ref[...]
    token=lax.broadcasted_iota(jnp.int32,(16,length),1)
    sel_bool=token==pos
    sel=jnp.where(sel_bool,1.0,0.0).astype(BF)
    sel_full=jnp.where(sel_bool,1.0,0.0)
    key_far=dot_nn(sel,k_ref[...]).astype(BF)
    val_far=dot_nn(sel,v_ref[...]).astype(BF)
    key_far_t=key_far.T
    key_t=k_ref[...].T
    ones=jnp.ones((16,128),F32)
    is_glob=lax.dot_general(sel_full,ones,(((0,),(0,)),((),())),preferred_element_type=F32)
    grad_scr[...]=jnp.where(is_glob>0.5,0.0,g_ref[...].astype(F32)).astype(BF)
    prod=grad_scr[...].astype(F32)*ctx_ref[...].astype(F32)
    hrow=lax.broadcasted_iota(jnp.int32,(16,128),0)
    hlane=lax.broadcasted_iota(jnp.int32,(16,128),1)//HEAD_DIM
    hsel=jnp.where(hrow==hlane,1.0,0.0)
    delta_all=lax.dot_general(hsel,prod,(((1,),(1,)),((),())),preferred_element_type=F32,precision=lax.Precision.HIGHEST)
    dk_acc[...]=jnp.zeros_like(dk_acc)
    dv_acc[...]=jnp.zeros_like(dv_acc)
    dk_far=jnp.zeros((16,128),F32); dv_far=jnp.zeros((16,128),F32)
    low_ok,high_ok=edge_masks()
    for start in range(0,length,QB):
        lo,hi=key_range(start,length)
        qq=split_pair(q_ref[start:start+QB,:])
        gg=split_pair(grad_scr[start:start+QB,:])
        lse=jnp.concatenate([lse_ref[0,0:1,start:start+QB],lse_ref[0,1:2,start:start+QB]],axis=1)
        delta=jnp.concatenate([delta_all[0:1,start:start+QB],delta_all[1:2,start:start+QB]],axis=1)
        dq_t=jnp.zeros((128,2*QB),F32)
        def one(scores,vals):
            p=jnp.exp(scores-lse)
            dp=dot_nt(vals,gg)
            return p.astype(BF),(p*(dp-delta)).astype(BF)
        far=jnp.where(far_mask(pos,start),dot_nt(key_far,qq),NEG)
        p,ds=one(far,val_far)
        dv_far=dv_far+dot_nn(p,gg); dk_far=dk_far+dot_nn(ds,qq)
        dq_t=dq_t+dot_nn(key_far_t,ds)
        parts=masked_scores(dot_nt(k_ref[lo:hi,:],qq),start,length,low_ok,high_ok)
        plist=[];dlist=[]
        for n,part in enumerate(parts):
            a=lo+n*QB
            p,ds=one(part,v_ref[a:a+QB,:])
            plist.append(p);dlist.append(ds)
        p=jnp.concatenate(plist,axis=0); ds=jnp.concatenate(dlist,axis=0)
        dv_acc[lo:hi,:]+=dot_nn(p,gg)
        dk_acc[lo:hi,:]+=dot_nn(ds,qq)
        dq_t=dq_t+dot_nn(key_t[:,lo:hi],ds)
        dq_ref[start:start+QB,:]=(pick_head(dq_t).T.astype(BF).astype(F32)*(HEAD_DIM**-0.5)).astype(BF)
    dk_ref[...]=(dk_acc[...]+lax.dot_general(sel_full,dk_far,(((0,),(0,)),((),())),preferred_element_type=F32,precision=lax.Precision.HIGHEST)).astype(BF)
    dv_ref[...]=(dv_acc[...]+lax.dot_general(sel_full,dv_far,(((0,),(0,)),((),())),preferred_element_type=F32,precision=lax.Precision.HIGHEST)).astype(BF)

def attn_bwd(pos,q,k,v,grad,ctx,lse,first,pairs):
    length,width=q.shape
    col=pl.BlockSpec((length,128),lambda i:(0,first+i))
    out_col=pl.BlockSpec((length,128),lambda i:(0,i))
    out=jax.ShapeDtypeStruct((length,128*pairs),BF)
    return pl.pallas_call(bwd_kernel,grid=(pairs,),
        in_specs=[pl.BlockSpec((16,1),lambda i:(0,0)),col,col,col,col,col,pl.BlockSpec((1,8,length),lambda i:(first+i,0,0))],
        out_specs=[out_col,out_col,out_col],
        out_shape=[out,out,out],
        scratch_shapes=[pltpu.VMEM((length,128),F32),pltpu.VMEM((length,128),F32),pltpu.VMEM((length,128),BF)],
        compiler_params=params(),
        cost_estimate=cost(COST,1<<20),
        name="attend_back")(pos,q,k,v,grad,ctx,lse)


ANY=pl.BlockSpec(memory_space=pl.ANY)
SMEM=pl.BlockSpec(memory_space=pltpu.SMEM)
RB=256

def cost(flops,nbytes,trans=0):
    return pl.CostEstimate(flops=int(flops),bytes_accessed=int(nbytes),transcendentals=int(trans))

def params(mib=60):
    return pltpu.CompilerParams(vmem_limit_bytes=mib<<20)

def fetches(pieces,place,sems,me,first,rows,sem0):
    out=[]
    for slot,piece in enumerate(pieces):
        owner=me^slot
        out.append(pltpu.make_async_copy(piece.at[pl.ds(first,rows)],place.at[pl.ds(pl.multiple_of(owner*rows,rows),rows)],sems.at[sem0+slot]))
    return out

def ffn_in_copies(refs,place,sems,sem0):
    if len(refs)>1: return [pltpu.make_async_copy(refs[0],place,sems.at[sem0])]
    pack=refs[0]; n,_,width=pack.shape; shard=place.shape[0]//n
    return [pltpu.make_async_copy(pack.at[s,pl.ds(j*shard,shard)],place.at[pl.ds(s*shard,shard),pl.ds(j*width,width)],sems.at[sem0+s*(place.shape[1]//width)+j])
            for s in range(n) for j in range(place.shape[1]//width)]


def ffn_back_copies(refs,place,sems,sem0):
    if len(refs)>1: return [pltpu.make_async_copy(refs[1],place,sems.at[sem0])]
    pack=refs[0]; n,rows,width=pack.shape; shard=place.shape[0]//n; first=rows-4*(width//n)-shard
    return [pltpu.make_async_copy(pack.at[s,pl.ds(first,shard)],place.at[pl.ds(s*shard,shard)],sems.at[sem0+s]) for s in range(n)]


def plane_copies(refs,plane,place,sems,sem0):
    width=place.shape[0]
    if len(refs)>1: return [pltpu.make_async_copy(refs[2].at[pl.ds(plane*width,width)],place,sems.at[sem0])]
    pack=refs[0]; n,rows,_=pack.shape; shard=width//n; first=rows-(4-plane)*shard
    return [pltpu.make_async_copy(pack.at[s,pl.ds(first,shard)],place.at[pl.ds(s*shard,shard)],sems.at[sem0+s]) for s in range(n)]


def stats(value):
    center=value-jnp.mean(value,axis=-1,keepdims=True)
    inverse=lax.rsqrt(jnp.mean(center*center,axis=-1,keepdims=True)+NORM_EPS)
    return center*inverse,inverse

def norm_back(scaled,normed,inverse):
    return inverse*(scaled-jnp.mean(scaled,axis=-1,keepdims=True)-normed*jnp.mean(scaled*normed,axis=-1,keepdims=True))

def gelu_pair(inner):
    cdf=0.5*(1.0+lax.erf(inner*0.7071067811865476))
    return inner*cdf, cdf+inner*(0.3989422804014327*jnp.exp(-0.5*inner*inner))

def chunk_store(chunks,me,value):
    for slot,chunk in enumerate(chunks):
        @pl.when(pl.program_id(0)^me==slot)
        def _(chunk=chunk): chunk[...]=value


def layer(mez,pos,ctx,ctxg,x,upstream,ffw,vecs,c_row,n):
    length,width=x.shape; ff=c_row.shape[1]; w=len(ffw); steps=length//RB; blocks=ff//width; shard=width//n; fs=ff//n
    def body(mez_ref,pos_ref,ctx_ref,glob_ref,x_ref,up_ref,vec_ref,c_ref,*refs):
        ff_w=refs[:w]; chunks=refs[w:w+steps]
        gs_ref,ag_ref,mg_ref,merged_ref,vg_ref,cg_ref,pack,wout,win,wback,acc_in,acc_back,act,slope,stage,sems,out_sems=refs[w+steps:]
        step=pl.program_id(0)
        first=step==0
        co=plane_copies(ff_w,3,wout,sems,0)
        ci=ffn_in_copies(ff_w,win,sems,n)
        cb=ffn_back_copies(ff_w,wback,sems,n+n*blocks)
        @pl.when(first)
        def _():
            for c in co+ci+cb: c.start()
            vg_ref[...]=jnp.zeros_like(vg_ref); cg_ref[...]=jnp.zeros_like(cg_ref)
            acc_in[...]=jnp.zeros_like(acc_in); acc_back[...]=jnp.zeros_like(acc_back)
            for c in co: c.wait()
        token=step*RB+lax.broadcasted_iota(jnp.int32,(16,RB),1)
        hot=jnp.where(token==pos_ref[...],1.0,0.0).astype(BF)
        is_glob=dot_tn(hot,jnp.ones((16,128),BF))[:,0:1]>0.5
        merged=jnp.where(is_glob,dot_tn(hot,glob_ref[...]),ctx_ref[...].astype(F32)).astype(BF)
        merged_ref[...]=merged
        hat1,inv1=stats(x_ref[...].astype(F32)+(dot_nn(merged,wout[...])+vec_ref[4:5,:]))
        norm1=hat1*vec_ref[6:7,:]+vec_ref[8:9,:]
        low=norm1.astype(BF)
        @pl.when(first)
        def _():
            for c in ci: c.wait()
        for a in range(0,ff,width):
            one,two=gelu_pair(dot_nn(low,win[:,a:a+width])+c_ref[:,a:a+width])
            act[:,a:a+width]=one.astype(BF); slope[:,a:a+width]=two.astype(BF)
        @pl.when(first)
        def _():
            for c in cb: c.wait()
        hat2,inv2=stats(norm1+(dot_nn(act[...],wback[...])+vec_ref[5:6,:]))
        chunk_store(chunks,mez_ref[0],(hat2*vec_ref[7:8,:]+vec_ref[9:10,:]).astype(BF))
        up=up_ref[...].astype(F32)
        col=lambda v:jnp.sum(v,axis=0,keepdims=True)
        vg_ref[7:8,:]+=col(up*hat2); vg_ref[9:10,:]+=col(up)
        second=norm_back(up*vec_ref[7:8,:],hat2,inv2)
        bg=second.astype(BF)
        vg_ref[5:6,:]+=col(bg.astype(F32))
        acc=second
        for a in range(0,ff,width):
            ig=(dot_nt(bg,wback[a:a+width,:])*slope[:,a:a+width].astype(F32)).astype(BF)
            cg_ref[:,a:a+width]+=col(ig.astype(F32))
            acc=acc+dot_nt(ig,win[:,a:a+width])
            acc_in[:,a:a+width]+=dot_tn(low,ig)
            acc_back[a:a+width,:]+=dot_tn(act[:,a:a+width],bg)
        vg_ref[6:7,:]+=col(acc*hat1); vg_ref[8:9,:]+=col(acc)
        gs=norm_back(acc*vec_ref[6:7,:],hat1,inv1)
        gs_ref[...]=gs
        ag=gs.astype(BF)
        ag_ref[...]=ag
        vg_ref[4:5,:]+=col(ag.astype(F32))
        mg_ref[...]=dot_nt(ag,wout[...]).astype(BF)
        @pl.when(step==steps-1)
        def _():
            copies=[]
            for b in range(2*blocks):
                slot=b%2
                if b>=2: copies[b-2].wait()
                if b<blocks:
                    stage[slot]=acc_in[:,b*width:(b+1)*width].astype(BF)
                    here=stage.at[slot].reshape(n,shard,width)
                    there=pack.at[:,pl.ds(b*shard,shard)]
                else:
                    at=(b-blocks)*width
                    stage[slot]=acc_back[at:at+width,:].astype(BF)
                    if n==1:
                        here,there=stage.at[slot],pack.at[0,pl.ds(blocks*shard+at,width)]
                    else:
                        here=stage.at[slot].reshape(width//fs,fs,width)
                        there=pack.at[pl.ds(at//fs,width//fs),pl.ds(blocks*shard,fs)]
                copies.append(pltpu.make_async_copy(here,there,out_sems.at[b]))
                copies[b].start()
            for c in copies[-2:]: c.wait()
    blk=lambda w:pl.BlockSpec((RB,w),lambda i:(i,0))
    full=lambda s:pl.BlockSpec(s,lambda i:(0,0))
    return pl.pallas_call(body,grid=(steps,),
        in_specs=[SMEM,full(pos.shape),blk(width),full(ctxg.shape),blk(width),blk(width),full(vecs.shape),full(c_row.shape)]+[ANY]*w,
        out_specs=[full((RB,width))]*steps+[blk(width)]*4+[full((16,width)),full((1,ff)),ANY],
        out_shape=[S((RB,width),BF)]*steps+[S((length,width),F32)]+[S((length,width),BF)]*3+[S((16,width),F32),S((1,ff),F32),S((n,blocks*shard+fs,width),BF)],
        scratch_shapes=[pltpu.VMEM((width,width),BF),pltpu.VMEM((width,ff),BF),pltpu.VMEM((ff,width),BF),pltpu.VMEM((width,ff),F32),pltpu.VMEM((ff,width),F32),
            pltpu.VMEM((RB,ff),BF),pltpu.VMEM((RB,ff),BF),pltpu.VMEM((2,width,width),BF),pltpu.SemaphoreType.DMA((2*n+n*blocks,)),pltpu.SemaphoreType.DMA((2*blocks,))],
        compiler_params=params(),cost_estimate=cost(COST,1<<20),name="layer")(mez,pos,ctx,ctxg,x,upstream,vecs,c_row,*ffw)


def local_grads(me,x,grads,unit=None,vec=None,count=8):
    length,width=x.shape; cols=grads[0].shape[1]; shard=width//count; half=count//2; k=len(grads)
    tail=0 if vec is None else 16
    rows=k*shard+tail
    base=0 if unit is None else unit[0].shape[1]-rows
    extra=([] if vec is None else [vec])+([] if unit is None else list(unit))
    def body(me_ref,x_ref,*refs):
        outs=refs[k+len(extra):]
        keep,send,res,keep_v,send_v,vec_v,sems=outs
        m=me_ref[0]
        xt=x_ref[...].T
        for r in range(k):
            res[...]=dot_nn(xt,refs[r][...])
            for slot in range(count):
                part=res[pl.ds(pl.multiple_of((m^slot)*shard,shard),shard),:]
                (send_v if slot%2 else keep_v)[slot//2,r*shard:(r+1)*shard,:]=part.astype(BF)
        if vec is not None:
            vec_v[...]=jnp.zeros_like(vec_v)
            for s in range(count):
                vec_v[s,:,0:shard]=refs[k][:,s*shard:(s+1)*shard]
            for slot in range(count):
                (send_v if slot%2 else keep_v)[slot//2,k*shard:rows,:]=vec_v[m^slot].astype(BF)
        cps=[pltpu.make_async_copy(v,o.at[:,pl.ds(base,rows)],sems.at[i]) for i,(v,o) in enumerate(((keep_v,keep),(send_v,send)))]
        for c in cps: c.start()
        for c in cps: c.wait()
    o=S((half,base+rows,cols),BF)
    vm=pl.BlockSpec(memory_space=pltpu.VMEM)
    first=1+1+k+(0 if vec is None else 1)
    return pl.pallas_call(body,in_specs=[SMEM]+[vm]*(first-1)+[ANY]*(0 if unit is None else 2),out_specs=[ANY]*2,out_shape=[o,o],
        input_output_aliases={} if unit is None else {first:0,first+1:1},
        scratch_shapes=[pltpu.VMEM((width,cols),F32),pltpu.VMEM((half,rows,cols),BF),pltpu.VMEM((half,rows,cols),BF),pltpu.VMEM((count,16,cols),F32),pltpu.SemaphoreType.DMA((2,))],
        compiler_params=params(),cost_estimate=cost(COST,1<<20),name="local_grads")(me,x,*grads,*extra)


def collect(mez,pieces):
    def body(mez_ref,*refs):
        for slot in range(len(pieces)):
            @pl.when(pl.program_id(0)^mez_ref[0]==slot)
            def _(slot=slot): refs[-1][0]=refs[slot][...]
    rows,width=pieces[0].shape; n=len(pieces)
    return pl.pallas_call(body,grid=(n,),in_specs=[SMEM]+[pl.BlockSpec((rows,width),lambda i:(0,0))]*n,
        out_specs=pl.BlockSpec((1,rows,width),lambda i:(i,0,0)),out_shape=S((n,rows,width),BF),
        compiler_params=params(),cost_estimate=cost(COST,1<<20),name="collect")(mez,*pieces)


def project(me,x,pieces,vecs):
    length,width=x.shape; n=len(pieces); shard=width//n
    def body(me_ref,x_ref,vec_ref,*refs):
        ins=refs[:n]; q_ref,k_ref,v_ref,wts,sems=refs[n:]
        m=me_ref[0]
        cps=[fetches(ins,wts.at[j],sems,m,j*shard,shard,j*n) for j in range(3)]
        for j in range(3):
            for c in cps[j]: c.start()
        for c in cps[0]: c.wait()
        scale=HEAD_DIM**-0.5
        for a in range(0,length,RB):
            q_ref[a:a+RB,:]=((dot_nn(x_ref[a:a+RB,:],wts[0])+vec_ref[0:1,:])*scale).astype(BF)
        for c in cps[1]: c.wait()
        for a in range(0,length,RB):
            k_ref[a:a+RB,:]=dot_nn(x_ref[a:a+RB,:],wts[1]).astype(BF)
        for c in cps[2]: c.wait()
        for a in range(0,length,RB):
            v_ref[a:a+RB,:]=(dot_nn(x_ref[a:a+RB,:],wts[2])+vec_ref[1:2,:]).astype(BF)
    vm=pl.BlockSpec(memory_space=pltpu.VMEM)
    return pl.pallas_call(body,in_specs=[SMEM,vm,vm]+[ANY]*n,out_specs=[vm]*3,out_shape=[S((length,width),BF)]*3,
        scratch_shapes=[pltpu.VMEM((3,width,width),BF),pltpu.SemaphoreType.DMA((3*n,))],
        compiler_params=params(),cost_estimate=cost(COST,1<<20),name="project")(me,x,vecs,*pieces)

def own_mask(width):
    return lax.broadcasted_iota(jnp.int32,(16,width),0)==lax.broadcasted_iota(jnp.int32,(16,width),1)//HEAD_DIM

def one_hot(pos,length):
    return jnp.where(lax.broadcasted_iota(jnp.int32,(16,length),1)==pos,1.0,0.0)

def scatter_heads(rows,own,count):
    zero=jnp.zeros((16,rows.shape[1]),F32)
    return jnp.concatenate([jnp.where(own,jnp.broadcast_to(rows[g:g+1,:].astype(F32),zero.shape),zero) for g in range(count)],axis=0).astype(BF)

def gather_heads(value,own,count):
    rows=[jnp.sum(jnp.where(own,value[16*g:16*g+16],0.0),axis=0,keepdims=True) for g in range(count)]
    rows.append(jnp.zeros((16-count,value.shape[1]),F32))
    return jnp.concatenate(rows,axis=0)

def globals_fwd(pos,x,ffw,vecs,count,n):
    length,width=x.shape; wide=16*count; w=len(ffw)
    def body(pos_ref,x_ref,vec_ref,*refs):
        ins=refs[:w]; ctx_ref,p_ref,u_ref,y_ref,q_ref,r_ref,wts,sems=refs[w:]
        cps=[plane_copies(ins,j,wts.at[j],sems,j*n) for j in range(3)]
        for j in range(3):
            for c in cps[j]: c.start()
        own=own_mask(width)
        sel=one_hot(pos_ref[...],length).astype(BF)
        rows=dot_nn(sel,x_ref[...]).astype(BF)
        r_ref[...]=rows
        for c in cps[0]: c.wait()
        q=((dot_nn(rows,wts[0])+vec_ref[2:3,:])*(HEAD_DIM**-0.5)).astype(BF)
        q_ref[...]=q
        for c in cps[1]: c.wait()
        u=dot_nt(wts[1],scatter_heads(q,own,count)).astype(BF)
        u_ref[...]=u
        s=dot_nn(x_ref[...],u)
        p=jnp.exp(s-jnp.max(s,axis=0,keepdims=True))
        p=p/jnp.sum(p,axis=0,keepdims=True)
        p_ref[...]=p
        low=p.astype(BF)
        y=dot_tn(low,x_ref[...]).astype(BF)
        y_ref[...]=y
        mass=dot_tn(low,jnp.ones((length,128),BF))[:,0:1]
        for c in cps[2]: c.wait()
        ctx_ref[...]=gather_heads(dot_nn(y,wts[2])+mass*vec_ref[3:4,:],own,count).astype(BF)
    vm=pl.BlockSpec(memory_space=pltpu.VMEM)
    return pl.pallas_call(body,in_specs=[vm,vm,vm]+[ANY]*w,out_specs=[vm]*6,
        out_shape=[S((16,width),BF),S((length,wide),F32),S((width,wide),BF),S((wide,width),BF),S((16,width),BF),S((16,width),BF)],
        scratch_shapes=[pltpu.VMEM((3,width,width),BF),pltpu.SemaphoreType.DMA((3*n,))],
        compiler_params=params(),cost_estimate=cost(COST,1<<20),name="globals")(pos,x,vecs,*ffw)

def globals_bwd(me,pos,x,mg,gs,p,u,y,q,rows,merged,ag,ffw,vecs,count,n,extra):
    length,width=x.shape; shard=width//n; half=max(n//2,1); w=len(ffw); cols=width//2
    def body(me_ref,pos_ref,x_ref,mg_ref,gs_ref,p_ref,u_ref,y_ref,q_ref,r_ref,merged_ref,ag_ref,vec_ref,*refs):
        ins=refs[:w]; out_ref,keep,send,keep2,send2,vg_ref,wts,res,keep_v,send_v,sems=refs[w:]
        m=me_ref[0]
        cps=[plane_copies(ins,j,wts.at[j],sems,j*n) for j in range(3)]
        for j in (2,1,0):
            for c in cps[j]: c.start()
        own=own_mask(width)
        hot=one_hot(pos_ref[...],length)
        sel=hot.astype(BF)
        x=x_ref[...]
        cs=scatter_heads(dot_nn(sel,mg_ref[...]).astype(BF),own,count)
        qs=scatter_heads(q_ref[...],own,count)
        for c in cps[2]: c.wait()
        v=dot_nt(wts[2],cs).astype(BF)
        shift=dot_nt(jnp.broadcast_to(vec_ref[3:4,:],(16,width)).astype(BF),cs)[0:1,:]
        dp=dot_nn(x,v)+shift
        p=p_ref[...]
        low=p.astype(BF)
        ds=(p*(dp-jnp.sum(p*dp,axis=0,keepdims=True))).astype(BF)
        a=dot_tn(ds,x).astype(BF)
        for c in cps[1]: c.wait()
        pre=(gather_heads(dot_nn(a,wts[1]),own,count).astype(BF).astype(F32)*(HEAD_DIM**-0.5)).astype(BF)
        for c in cps[0]: c.wait()
        rows_grad=dot_nt(pre,wts[0])
        mass=dot_tn(low,jnp.ones((length,128),BF))[:,0:1]
        vg_ref[...]=jnp.zeros_like(vg_ref)
        vg_ref[2:3,:]=jnp.sum(pre.astype(F32),axis=0,keepdims=True)
        vg_ref[3:4,:]=jnp.sum(mass*cs.astype(F32),axis=0,keepdims=True)
        out_ref[...]=gs_ref[...]+dot_nt(ds,u_ref[...])+dot_nt(low,v)+lax.dot_general(hot,rows_grad,(((0,),(0,)),((),())),preferred_element_type=F32,precision=lax.Precision.HIGHEST)
        for j,(l,r) in enumerate(((r_ref[...],pre),(a,qs),(y_ref[...],cs),(merged_ref[...],ag_ref[...]))):
            res[...]=dot_tn(l,r)
            for slot in range(n):
                for h in range(2):
                    part=res[pl.ds(pl.multiple_of((m^slot)*shard,shard),shard),h*cols:(h+1)*cols]
                    (send_v if slot%2 else keep_v)[slot//2,(2*j+h)*shard:(2*j+h+1)*shard,:]=part.astype(BF)
        cps=[]
        for here,first,there in ((keep_v,0,keep),(keep_v,6*shard,keep2),(send_v,0,send),(send_v,6*shard,send2)):
            if n==1 and here is send_v: continue
            rows_out=6*shard if first==0 else 2*shard
            cps.append(pltpu.make_async_copy(here.at[:,pl.ds(first,rows_out)],there.at[:,pl.ds(0,rows_out)],sems.at[3*n+len(cps)]))
        for c in cps: c.start()
        for c in cps: c.wait()
    vm=pl.BlockSpec(memory_space=pltpu.VMEM)
    o1=S((half,6*shard,cols),BF)
    o2=S((half,2*shard+extra,cols),BF)
    return pl.pallas_call(body,in_specs=[SMEM]+[vm]*12+[ANY]*w,out_specs=[vm,ANY,ANY,ANY,ANY,vm],
        out_shape=[S((length,width),F32),o1,o1,o2,o2,S((16,width),F32)],
        scratch_shapes=[pltpu.VMEM((3,width,width),BF),pltpu.VMEM((width,width),F32),pltpu.VMEM((half,8*shard,cols),BF),pltpu.VMEM((half,8*shard,cols),BF),pltpu.SemaphoreType.DMA((3*n+4,))],
        compiler_params=params(),cost_estimate=cost(COST,1<<20),name="globals_back")(me,pos,x,mg,gs,p,u,y,q,rows,merged,ag,vecs,*ffw)


def inputs_back(me,mez,gs,groups,pieces):
    length,width=gs.shape; n=len(pieces); shard=width//n; g=len(groups); cols=width//g
    steps=length//RB
    def body(me_ref,mez_ref,gs_ref,*refs):
        parts=refs[:3*g]; ins=refs[3*g:3*g+n]; chunks=refs[3*g+n:3*g+n+steps]; vg_ref,wts,sems=refs[3*g+n+steps:]
        m=me_ref[0]
        @pl.when(pl.program_id(0)==0)
        def _():
            cps=sum([fetches(ins,wts.at[j],sems,m,j*shard,shard,j*n) for j in range(3)],[])
            for c in cps: c.start()
            vg_ref[...]=jnp.zeros_like(vg_ref)
            for c in cps: c.wait()
        acc=gs_ref[...]
        for j in range(g):
            a=j*cols
            for w in range(3): acc=acc+dot_nt(parts[3*j+w][...],wts[w,:,a:a+cols])
            vg_ref[0:1,a:a+cols]+=jnp.sum(parts[3*j][...].astype(F32),axis=0,keepdims=True)
            vg_ref[1:2,a:a+cols]+=jnp.sum(parts[3*j+2][...].astype(F32),axis=0,keepdims=True)
        chunk_store(chunks,mez_ref[0],acc.astype(BF))
    blk=pl.BlockSpec((RB,width),lambda i:(i,0))
    part=pl.BlockSpec((RB,cols),lambda i:(i,0))
    return pl.pallas_call(body,grid=(length//RB,),in_specs=[SMEM,SMEM,blk]+[part]*(3*g)+[ANY]*n,
        out_specs=[pl.BlockSpec((RB,width),lambda i:(0,0))]*steps+[pl.BlockSpec((16,width),lambda i:(0,0))],out_shape=[S((RB,width),BF)]*steps+[S((16,width),F32)],
        scratch_shapes=[pltpu.VMEM((3,width,width),BF),pltpu.SemaphoreType.DMA((3*n,))],
        compiler_params=params(),cost_estimate=cost(COST,1<<20),name="inputs_back")(me,mez,gs,*[p for t in groups for p in t],*pieces)


def flip(value, axis, bit):
    count = lax.axis_size(axis)
    return lax.ppermute(value, axis, [(index, index ^ bit) for index in range(count)])


def tie(value, *others):
    return lax.optimization_barrier((value,) + others)[0]


def spread_slots(unit, order):
    slots = {0: unit}
    for bit in order:
        for slot in list(slots):
            slots[slot | bit] = flip(slots[slot], "fsdp", bit)
    return [slots[slot] for slot in range(len(slots))]


def add(one, two):
    return one.astype(F32) + two.astype(F32)


def meet(values, parts, *others):
    flat = [list(part.got) if isinstance(part.got, list) else [part.got] for part in parts]
    joined = tuple(values) + tuple(got for gots in flat for got in gots) + others
    joined = list(lax.optimization_barrier(joined))
    values = [joined.pop(0) for _ in values]
    for part, gots in zip(parts, flat):
        new = [joined.pop(0) for _ in gots]
        part.got = new if isinstance(part.got, list) else new[0]
    return values


class Exchange:
    def __init__(self, chunks):
        self.got = [chunks[0]] + [flip(chunks[k], "sp", k) for k in range(1, len(chunks))]


class Reduction:
    def __init__(self, keep, send, x_first):
        self.keep, self.first, self.step = keep, send, 0
        self.got = flip(send, "fsdp", 1)
        self.x_first = x_first

    def advance(self, *gates):
        got = tie(self.got, *gates)
        x_now = self.x_first == (self.step == 0)
        if self.step == 0:
            keep = self.keep.reshape((2, 2) + self.keep.shape[1:])
            got = got.reshape(keep.shape)
            if self.x_first:
                away, here = (keep[:, 1], got[:, 1]), (keep[:, 0], got[:, 0])
            else:
                away, here = (keep[1], got[1]), (keep[0], got[0])
        else:
            away, here = (self.mine[1], got[1]), (self.mine[0], got[0])
        self.send, self.mine = add(*away).astype(BF), add(*here)
        self.got = flip(self.send, "fsdp", 2 if x_now else 4)
        self.step += 1
        return self.send

    def total(self):
        return add(self.mine, self.got)


class SpSum:
    def __init__(self, value, start=True):
        self.low, self.high = lax.axis_index("sp") & 1, lax.axis_index("sp") >> 1
        rows = value.shape[0] // 4
        self.shape = value.shape
        self.value = value.reshape(2, 2, rows, value.shape[1])
        self.got = self.value
        self.step = 0
        if start:
            self.start()

    def start(self):
        self.value = self.got
        self.exchange(self.low, 1)

    def exchange(self, mine, bit):
        send = lax.dynamic_index_in_dim(self.value, 1 - mine, 0, keepdims=False).astype(BF)
        self.value = lax.dynamic_index_in_dim(self.value, mine, 0, keepdims=False)
        self.send, self.got = send, flip(send, "sp", bit)

    def join(self, mine):
        return jnp.stack(
            [jnp.where(mine == 0, self.value, self.got), jnp.where(mine == 0, self.got, self.value)]
        )

    def advance(self):
        if self.step == 0:
            self.value = add(self.value, self.got)
            self.exchange(self.high, 2)
        elif self.step == 1:
            self.value = add(self.value, self.got).astype(BF)
            self.got = flip(self.value, "sp", 2)
        else:
            self.value = self.join(self.high)
            self.got = flip(self.value, "sp", 1)
        self.step += 1

    def total(self):
        return self.join(self.low).reshape(self.shape).astype(F32)


def per_device(
    inputs,
    global_pos,
    w_local,
    w_global,
    w_out,
    b_proj,
    gains,
    shifts,
    w_in,
    c_in,
    w_back,
    cotangent,
):
    sp_count = lax.axis_size("sp")
    fsdp_count = lax.axis_size("fsdp")
    sp_index = lax.axis_index("sp")
    fsdp_index = lax.axis_index("fsdp")
    own_seqs = inputs.shape[0] // sp_count
    glob_count = global_pos.shape[1]
    shard, width = w_out.shape
    ff_shard = w_back.shape[0]
    ff_width = w_in.shape[1]
    tree = fsdp_count == 8 and sp_count == 4 and own_seqs == 1 and shard % 32 == 0
    tree = tree and inputs.shape[1] == RB

    def to_sequence(value):
        if own_seqs == 1:
            moved = lax.all_to_all(value, "sp", split_axis=0, concat_axis=0)
            return moved.reshape(1, -1, width)
        return lax.all_to_all(value, "sp", split_axis=0, concat_axis=1, tiled=True)

    def to_tokens(values):
        if own_seqs == 1:
            return lax.all_to_all(
                values[0].reshape(sp_count, -1, width), "sp", split_axis=0, concat_axis=0
            )
        return lax.all_to_all(jnp.stack(values), "sp", split_axis=1, concat_axis=0, tiled=True)

    own_pos = lax.dynamic_slice_in_dim(global_pos, sp_index * own_seqs, own_seqs, 0)
    blocks = ff_width // width
    x_all = to_sequence(inputs)
    vec_rows = [b_proj, gains, shifts, c_in.reshape(-1, shard)]
    small = jnp.concatenate(vec_rows, axis=0)
    small = jnp.pad(small, ((0, 16 - small.shape[0]), (0, 0)))
    if tree:
        me = fsdp_index.reshape(1).astype(jnp.int32)
        mez = sp_index.reshape(1).astype(jnp.int32)
        first = jnp.concatenate(
            [w_local.reshape(-1, width), jnp.pad(small, ((0, 0), (0, width - shard)))], axis=0
        )
        local_w = spread_slots(first, (2, 4, 1))
        pack = jnp.concatenate(
            [
                w_in.reshape(shard, blocks, width).transpose(1, 0, 2).reshape(-1, width),
                w_back,
                w_global.reshape(-1, width),
                w_out,
            ],
            axis=0,
        )
        ffw = [lax.all_gather(pack, "fsdp")]
        small_all = jnp.stack([piece[3 * shard :, :shard] for piece in local_w])
        small_all = small_all[me[0] ^ jnp.arange(fsdp_count, dtype=jnp.int32)]
    else:
        me = mez = jnp.zeros((1,), jnp.int32)
        local_w = [lax.all_gather(w_local, "fsdp", axis=1, tiled=True).reshape(-1, width)]
        full_global = lax.all_gather(w_global, "fsdp", axis=1, tiled=True).reshape(-1, width)
        full_out = lax.all_gather(w_out, "fsdp", axis=0, tiled=True)
        ffw = [lax.all_gather(value, "fsdp", axis=0, tiled=True) for value in (w_in, w_back)]
        ffw.append(jnp.concatenate([full_global, full_out], axis=0))
        small_all = lax.all_gather(small, "fsdp")
    count = len(local_w)
    up_all = to_sequence(tie(cotangent, x_all))
    vecs = small_all.transpose(1, 0, 2).reshape(16, width).astype(F32)
    c_rows = small_all[:, 10 : 10 + ff_shard // shard].astype(F32)
    c_row = c_rows.reshape(1, ff_width)

    outs, input_grads, totals = [], [], None
    for index in range(own_seqs):
        x = x_all[index]
        pos = jnp.full((16, 1), -1, jnp.int32).at[:glob_count, 0].set(own_pos[index])
        q, k, v = project(me, x, local_w, vecs)
        ctx, lse = attn_fwd(pos, q, k, v)
        ctx_glob, probs, keys, mixed, query, rows = globals_fwd(
            pos, x, ffw, vecs, glob_count, count
        )
        *out, grad_sum, attn_grad, merged_grad, merged, vec_one, c_grad, ff_pack = layer(
            mez, pos, ctx, ctx_glob, x, up_all[index], ffw, vecs, c_row, count
        )
        if tree:
            out_moved = Exchange(out)
        else:
            outs.append(jnp.concatenate(out, axis=0))
        if tree:
            ff_mine = lax.psum_scatter(ff_pack, "fsdp", scatter_dimension=0, tiled=False)
            merged_grad = tie(merged_grad, ff_pack)
        grad_sum, keep_one, send_one, keep_two, send_two, vec_two = globals_bwd(
            me,
            pos,
            x,
            merged_grad,
            grad_sum,
            probs,
            keys,
            mixed,
            query,
            rows,
            merged,
            attn_grad,
            ffw,
            vecs,
            glob_count,
            count,
            3 * shard if tree else 0,
        )
        group_pairs = width // 128 // GROUPS
        groups = []
        if tree:
            one = Reduction(keep_one, send_one, True)
            merged_grad = tie(merged_grad, send_one)
        for group in range(GROUPS):
            parts = attn_bwd(
                pos, q, k, v, merged_grad, ctx, lse, group * group_pairs, group_pairs
            )
            groups.append(parts)
            if tree and group == 0:
                two = Reduction(*local_grads(me, x, parts, unit=(keep_two, send_two)), False)
                (merged_grad,) = meet([merged_grad], [out_moved], two.first)
        if tree:
            (grad_sum,) = meet([grad_sum], [one, two], parts[0])
            grad_sum = tie(grad_sum, one.advance(), two.advance())
        *input_grad, vec_three = inputs_back(me, mez, grad_sum, groups, local_w)
        if tree:
            grads_moved = Exchange(input_grad)
        else:
            input_grads.append(jnp.concatenate(input_grad, axis=0))
        c_grad = c_grad.reshape(fsdp_count, -1, shard).transpose(1, 0, 2).reshape(-1, width)
        vec = vec_one + vec_two + vec_three + jnp.pad(c_grad, ((10, 6 - c_grad.shape[0]), (0, 0)))
        if not tree:
            g_in = ff_pack[0, :ff_width].reshape(blocks, width, width).transpose(1, 0, 2)
            g_in = g_in.reshape(width, ff_width).astype(F32)
            g_back = ff_pack[0, ff_width:].astype(F32)
            g_mixed = jnp.concatenate([keep_one[0], keep_two[0]], axis=0)
            g_mixed = g_mixed.reshape(4, 2, width, width // 2).transpose(0, 2, 1, 3)
            grads = (
                g_back,
                g_in,
                g_mixed.reshape(4, width, width).astype(F32),
                jnp.stack(
                    [
                        jnp.concatenate([dot_tn(x, part[w]) for part in groups], axis=1)
                        for w in range(3)
                    ]
                ),
                vec,
            )
            totals = grads if totals is None else tuple(a + b for a, b in zip(totals, grads))
    if tree:
        x_late, ff_mine = meet([x, ff_mine], [], *input_grad)
        ff_sum = SpSum(ff_mine.astype(F32))
        x_late = tie(x_late, ff_sum.send)
        late = Reduction(*local_grads(me, x_late, groups[-1], vec=vec), False)
        meet([], [one, two, ff_sum, grads_moved], late.first)
        one.advance()
        two.advance()
        ff_sum.advance()
        meet([], [late], one.send, two.send, ff_sum.send)
        late.advance()
        meet([], [one, two, late, ff_sum])
        early_sum = SpSum(jnp.concatenate([one.total(), two.total()], axis=0))
        late.advance()
        ff_sum.advance()
        out = collect(mez, out_moved.got)
        meet([], [late, ff_sum, early_sum])
        late_sum = SpSum(late.total())
        early_sum.advance()
        ff_sum.advance()
        grad_inputs = collect(mez, grads_moved.got)
        meet([], [early_sum, late_sum, ff_sum])
        early_sum.advance()
        late_sum.advance()
        s_ff = ff_sum.total()
        meet([], [early_sum, late_sum])
        early_sum.advance()
        late_sum.advance()
        meet([], [early_sum, late_sum])
        late_sum.advance()
        s_early, s_late = early_sum.total(), late_sum.total()
        half_mixed = s_early[: 8 * shard].reshape(4, 2, shard, -1).transpose(0, 2, 1, 3)
        s_mixed = half_mixed.reshape(4, shard, width)
        s_local = jnp.concatenate(
            [
                s_early[8 * shard :].reshape(3, shard, -1),
                s_late[: 3 * shard].reshape(3, shard, -1),
            ],
            axis=2,
        )
        mine = s_late[3 * shard :, :shard]
        s_in = s_ff[: blocks * shard].reshape(blocks, shard, width).transpose(1, 0, 2)
        s_in = s_in.reshape(shard, ff_width)
        s_back = s_ff[blocks * shard :]
    else:
        out, grad_inputs = to_tokens(outs), to_tokens(input_grads)
        g_back, g_in, g_mixed, g_local, vec = totals

        def reduce(value, dim):
            mine = lax.psum_scatter(value.astype(BF), "fsdp", scatter_dimension=dim, tiled=True)
            return lax.psum(mine, "sp").astype(F32)

        s_back, s_in = reduce(g_back, 0), reduce(g_in, 0)
        s_mixed = reduce(g_mixed, 1)
        s_local = reduce(g_local, 1)
        vec = lax.psum(vec, ("fsdp", "sp"))
        mine = lax.dynamic_slice_in_dim(vec, fsdp_index * shard, shard, 1)
    c_mine = mine[10 : 10 + ff_shard // shard].reshape(-1)
    return (
        out,
        grad_inputs,
        s_local,
        s_mixed[:3],
        s_mixed[3],
        mine[:6],
        mine[6:8],
        mine[8:10],
        s_in,
        c_mine,
        s_back,
    )


def solution(mesh):
    rows = P("fsdp", None)
    tokens = P("fsdp", "sp", None)
    columns = P(None, "fsdp")
    stacked = P(None, "fsdp", None)
    return jax.shard_map(
        per_device,
        mesh=mesh,
        in_specs=(
            tokens,
            rows,
            stacked,
            stacked,
            rows,
            columns,
            columns,
            columns,
            rows,
            P("fsdp"),
            rows,
            tokens,
        ),
        out_specs=(
            tokens,
            tokens,
            stacked,
            stacked,
            rows,
            columns,
            columns,
            columns,
            rows,
            P("fsdp"),
            rows,
        ),
        check_vma=False,
    )
```

```python
import jax
import jax.numpy as jnp
from jax import lax
from jax.experimental import pallas as pl
from jax.experimental.pallas import tpu as pltpu
from jax.sharding import PartitionSpec as P

HEADS = 12
HEAD_DIM = 64
WIN = 256
QB = 128
NEG = -1e9
GROUPS = 2
COST = 2 * 10**10
NORM_EPS = 1e-05
BF = jnp.bfloat16
F32 = jnp.float32
S = jax.ShapeDtypeStruct


def dot_nn(a,b): return jnp.dot(a,b,preferred_element_type=F32)
def dot_nt(a,b): return lax.dot_general(a,b,(((1,),(1,)),((),())),preferred_element_type=F32)
def dot_tn(a,b): return lax.dot_general(a,b,(((0,),(0,)),((),())),preferred_element_type=F32)

def split_pair(block):
    lane=lax.broadcasted_iota(jnp.int32,block.shape,1)
    zero=jnp.zeros_like(block)
    return jnp.concatenate([jnp.where(lane<HEAD_DIM,block,zero),jnp.where(lane<HEAD_DIM,zero,block)],axis=0)

def far_mask(pos, start):
    place=start+lax.broadcasted_iota(jnp.int32,(16,2*QB),1)%QB
    return (pos>=0)&(jnp.abs(place-pos)>WIN)

def edge_masks():
    row=lax.broadcasted_iota(jnp.int32,(QB,2*QB),0)
    col=lax.broadcasted_iota(jnp.int32,(QB,2*QB),1)%QB
    return row>=col, row<=col

def key_range(start,length):
    return max(0,start-WIN), min(length,start+QB+WIN)

def pick_head(both):
    row=lax.broadcasted_iota(jnp.int32,(2*HEAD_DIM,QB),0)
    return jnp.where(row<HEAD_DIM,both[:,:QB],both[:,QB:])

def masked_scores(raw,start,length,low_ok,high_ok):
    lo,hi=key_range(start,length)
    parts=[]
    for first in range(lo,hi,QB):
        chunk=raw[first-lo:first-lo+QB]
        if first==start-WIN: chunk=jnp.where(low_ok,chunk,NEG)
        elif first==start+WIN: chunk=jnp.where(high_ok,chunk,NEG)
        parts.append(chunk)
    return parts

def fwd_kernel(pos_ref,q_ref,k_ref,v_ref,ctx_ref,lse_ref):
    length=q_ref.shape[0]
    pos=pos_ref[...]
    token=lax.broadcasted_iota(jnp.int32,(16,length),1)
    sel=jnp.where(token==pos,1.0,0.0).astype(BF)
    key_far=dot_nn(sel,k_ref[...]).astype(BF)
    val_far_t=dot_nn(sel,v_ref[...]).astype(BF).T
    val_t=v_ref[...].T
    low_ok,high_ok=edge_masks()
    def products(start):
        lo,hi=key_range(start,length)
        qq=split_pair(q_ref[start:start+QB,:])
        return dot_nt(k_ref[lo:hi,:],qq),dot_nt(key_far,qq)
    ahead=products(0)
    for start in range(0,length,QB):
        lo,hi=key_range(start,length)
        raw,raw_far=ahead
        if start+QB<length: ahead=products(start+QB)
        parts=masked_scores(raw,start,length,low_ok,high_ok)
        far=jnp.where(far_mask(pos,start),raw_far,NEG)
        top=jnp.max(far,axis=0,keepdims=True)
        for part in parts: top=jnp.maximum(top,jnp.max(part,axis=0,keepdims=True))
        far_p=jnp.exp(far-top)
        total=jnp.sum(far_p,axis=0,keepdims=True)
        probs=[]
        for part in parts:
            p=jnp.exp(part-top)
            total=total+jnp.sum(p,axis=0,keepdims=True)
            probs.append(p.astype(BF))
        both=dot_nn(val_t[:,lo:hi],jnp.concatenate(probs,axis=0))+dot_nn(val_far_t,far_p.astype(BF))
        both=both*(1.0/total)
        ctx_ref[start:start+QB,:]=pick_head(both).T.astype(BF)
        lse=top+jnp.log(total)
        lse_ref[0,0:1,start:start+QB]=lse[:,:QB]
        lse_ref[0,1:2,start:start+QB]=lse[:,QB:]

def attn_fwd(pos,q,k,v):
    length,width=q.shape
    pairs=width//128
    col=pl.BlockSpec((length,128),lambda i:(0,i))
    return pl.pallas_call(fwd_kernel,grid=(pairs,),
        in_specs=[pl.BlockSpec((16,1),lambda i:(0,0)),col,col,col],
        out_specs=[col,pl.BlockSpec((1,8,length),lambda i:(i,0,0))],
        out_shape=[jax.ShapeDtypeStruct((length,width),BF),jax.ShapeDtypeStruct((pairs,8,length),F32)],
        compiler_params=params(),
        cost_estimate=cost(COST,1<<20),
        name="attend")(pos,q,k,v)

def bwd_kernel(pos_ref,q_ref,k_ref,v_ref,g_ref,ctx_ref,lse_ref,dq_ref,dk_ref,dv_ref,dk_acc,dv_acc,grad_scr):
    length=q_ref.shape[0]
    pos=pos_ref[...]
    token=lax.broadcasted_iota(jnp.int32,(16,length),1)
    sel_bool=token==pos
    sel=jnp.where(sel_bool,1.0,0.0).astype(BF)
    sel_full=jnp.where(sel_bool,1.0,0.0)
    key_far=dot_nn(sel,k_ref[...]).astype(BF)
    val_far=dot_nn(sel,v_ref[...]).astype(BF)
    key_far_t=key_far.T
    key_t=k_ref[...].T
    ones=jnp.ones((16,128),F32)
    is_glob=lax.dot_general(sel_full,ones,(((0,),(0,)),((),())),preferred_element_type=F32)
    grad_scr[...]=jnp.where(is_glob>0.5,0.0,g_ref[...].astype(F32)).astype(BF)
    prod=grad_scr[...].astype(F32)*ctx_ref[...].astype(F32)
    hrow=lax.broadcasted_iota(jnp.int32,(16,128),0)
    hlane=lax.broadcasted_iota(jnp.int32,(16,128),1)//HEAD_DIM
    hsel=jnp.where(hrow==hlane,1.0,0.0)
    delta_all=lax.dot_general(hsel,prod,(((1,),(1,)),((),())),preferred_element_type=F32,precision=lax.Precision.HIGHEST)
    dk_acc[...]=jnp.zeros_like(dk_acc)
    dv_acc[...]=jnp.zeros_like(dv_acc)
    dk_far=jnp.zeros((16,128),F32); dv_far=jnp.zeros((16,128),F32)
    low_ok,high_ok=edge_masks()
    def products(start):
        lo,hi=key_range(start,length)
        qq=split_pair(q_ref[start:start+QB,:])
        gg=split_pair(grad_scr[start:start+QB,:])
        raw=dot_nt(jnp.concatenate([k_ref[lo:hi,:],key_far],axis=0),qq)
        dp=dot_nt(jnp.concatenate([v_ref[lo:hi,:],val_far],axis=0),gg)
        return qq,gg,raw[:hi-lo],dp[:hi-lo],raw[hi-lo:],dp[hi-lo:]
    ahead=products(0)
    for start in range(0,length,QB):
        lo,hi=key_range(start,length)
        qq,gg,raw,dp_all,raw_far,dp_far=ahead
        if start+QB<length: ahead=products(start+QB)
        lse=jnp.concatenate([lse_ref[0,0:1,start:start+QB],lse_ref[0,1:2,start:start+QB]],axis=1)
        delta=jnp.concatenate([delta_all[0:1,start:start+QB],delta_all[1:2,start:start+QB]],axis=1)
        def one(scores,dp):
            p=jnp.exp(scores-lse)
            return p.astype(BF),(p*(dp-delta)).astype(BF)
        far=jnp.where(far_mask(pos,start),raw_far,NEG)
        p_far,ds_far=one(far,dp_far)
        parts=masked_scores(raw,start,length,low_ok,high_ok)
        both=[one(part,dp_all[n*QB:(n+1)*QB]) for n,part in enumerate(parts)]
        p=jnp.concatenate([pair[0] for pair in both]+[p_far],axis=0)
        ds=jnp.concatenate([pair[1] for pair in both]+[ds_far],axis=0)
        dv_all,dk_all=dot_nn(p,gg),dot_nn(ds,qq)
        dv_acc[lo:hi,:]+=dv_all[:hi-lo]
        dk_acc[lo:hi,:]+=dk_all[:hi-lo]
        dv_far=dv_far+dv_all[hi-lo:]; dk_far=dk_far+dk_all[hi-lo:]
        dq_t=dot_nn(jnp.concatenate([key_t[:,lo:hi],key_far_t],axis=1),ds)
        dq_ref[start:start+QB,:]=(pick_head(dq_t).T.astype(BF).astype(F32)*(HEAD_DIM**-0.5)).astype(BF)
    dk_ref[...]=(dk_acc[...]+lax.dot_general(sel_full,dk_far,(((0,),(0,)),((),())),preferred_element_type=F32,precision=lax.Precision.HIGHEST)).astype(BF)
    dv_ref[...]=(dv_acc[...]+lax.dot_general(sel_full,dv_far,(((0,),(0,)),((),())),preferred_element_type=F32,precision=lax.Precision.HIGHEST)).astype(BF)

def attn_bwd(pos,q,k,v,grad,ctx,lse,first,pairs):
    length,width=q.shape
    col=pl.BlockSpec((length,128),lambda i:(0,first+i))
    out_col=pl.BlockSpec((length,128),lambda i:(0,i))
    out=jax.ShapeDtypeStruct((length,128*pairs),BF)
    return pl.pallas_call(bwd_kernel,grid=(pairs,),
        in_specs=[pl.BlockSpec((16,1),lambda i:(0,0)),col,col,col,col,col,pl.BlockSpec((1,8,length),lambda i:(first+i,0,0))],
        out_specs=[out_col,out_col,out_col],
        out_shape=[out,out,out],
        scratch_shapes=[pltpu.VMEM((length,128),F32),pltpu.VMEM((length,128),F32),pltpu.VMEM((length,128),BF)],
        compiler_params=params(),
        cost_estimate=cost(COST,1<<20),
        name="attend_back")(pos,q,k,v,grad,ctx,lse)


ANY=pl.BlockSpec(memory_space=pl.ANY)
SMEM=pl.BlockSpec(memory_space=pltpu.SMEM)
RB=256

def cost(flops,nbytes,trans=0):
    return pl.CostEstimate(flops=int(flops),bytes_accessed=int(nbytes),transcendentals=int(trans))

def params(mib=60):
    return pltpu.CompilerParams(vmem_limit_bytes=mib<<20)

def fetches(pieces,place,sems,me,first,rows,sem0):
    out=[]
    for slot,piece in enumerate(pieces):
        owner=me^slot
        out.append(pltpu.make_async_copy(piece.at[pl.ds(first,rows)],place.at[pl.ds(pl.multiple_of(owner*rows,rows),rows)],sems.at[sem0+slot]))
    return out

def ffn_in_copies(refs,place,sems,sem0):
    if len(refs)>1: return [pltpu.make_async_copy(refs[0],place,sems.at[sem0])]
    pack=refs[0]; n,_,width=pack.shape; shard=place.shape[0]//n
    return [pltpu.make_async_copy(pack.at[s,pl.ds(j*shard,shard)],place.at[pl.ds(s*shard,shard),pl.ds(j*width,width)],sems.at[sem0+s*(place.shape[1]//width)+j])
            for s in range(n) for j in range(place.shape[1]//width)]


def ffn_back_copies(refs,place,sems,sem0):
    if len(refs)>1: return [pltpu.make_async_copy(refs[1],place,sems.at[sem0])]
    pack=refs[0]; n,rows,width=pack.shape; shard=place.shape[0]//n; first=rows-4*(width//n)-shard
    return [pltpu.make_async_copy(pack.at[s,pl.ds(first,shard)],place.at[pl.ds(s*shard,shard)],sems.at[sem0+s]) for s in range(n)]


def plane_copies(refs,plane,place,sems,sem0):
    width=place.shape[0]
    if len(refs)>1: return [pltpu.make_async_copy(refs[2].at[pl.ds(plane*width,width)],place,sems.at[sem0])]
    pack=refs[0]; n,rows,_=pack.shape; shard=width//n; first=rows-(4-plane)*shard
    return [pltpu.make_async_copy(pack.at[s,pl.ds(first,shard)],place.at[pl.ds(s*shard,shard)],sems.at[sem0+s]) for s in range(n)]


def stats(value):
    center=value-jnp.mean(value,axis=-1,keepdims=True)
    inverse=lax.rsqrt(jnp.mean(center*center,axis=-1,keepdims=True)+NORM_EPS)
    return center*inverse,inverse

def norm_back(scaled,normed,inverse):
    return inverse*(scaled-jnp.mean(scaled,axis=-1,keepdims=True)-normed*jnp.mean(scaled*normed,axis=-1,keepdims=True))

def gelu_pair(inner):
    cdf=0.5*(1.0+lax.erf(inner*0.7071067811865476))
    return inner*cdf, cdf+inner*(0.3989422804014327*jnp.exp(-0.5*inner*inner))

def chunk_store(chunks,me,value):
    for slot,chunk in enumerate(chunks):
        @pl.when(pl.program_id(0)^me==slot)
        def _(chunk=chunk): chunk[...]=value


def layer(me,mez,pos,ctx,ctxg,x,upstream,ffw,vecs,c_row,n,extra):
    half=max(n//2,1); cols=x.shape[1]//2
    length,width=x.shape; ff=c_row.shape[1]; w=len(ffw); steps=length//RB; blocks=ff//width; shard=width//n; fs=ff//n
    def body(me_ref,mez_ref,pos_ref,ctx_ref,glob_ref,x_ref,up_ref,vec_ref,c_ref,*refs):
        ff_w=refs[:w]; chunks=refs[w:w+steps]
        gs_ref,mg_ref,vg_ref,cg_ref,pack,keep,send,wout,win,wback,acc_in,acc_back,acc_out,act,slope,stage,keep_v,send_v,sems,out_sems=refs[w+steps:]
        step=pl.program_id(0)
        first=step==0
        co=plane_copies(ff_w,3,wout,sems,0)
        ci=ffn_in_copies(ff_w,win,sems,n)
        cb=ffn_back_copies(ff_w,wback,sems,n+n*blocks)
        @pl.when(first)
        def _():
            for c in co+ci+cb: c.start()
            vg_ref[...]=jnp.zeros_like(vg_ref); cg_ref[...]=jnp.zeros_like(cg_ref)
            acc_in[...]=jnp.zeros_like(acc_in); acc_back[...]=jnp.zeros_like(acc_back)
            acc_out[...]=jnp.zeros_like(acc_out)
            for c in co: c.wait()
        token=step*RB+lax.broadcasted_iota(jnp.int32,(16,RB),1)
        hot=jnp.where(token==pos_ref[...],1.0,0.0).astype(BF)
        is_glob=dot_tn(hot,jnp.ones((16,128),BF))[:,0:1]>0.5
        merged=jnp.where(is_glob,dot_tn(hot,glob_ref[...]),ctx_ref[...].astype(F32)).astype(BF)
        hat1,inv1=stats(x_ref[...].astype(F32)+(dot_nn(merged,wout[...])+vec_ref[4:5,:]))
        norm1=hat1*vec_ref[6:7,:]+vec_ref[8:9,:]
        low=norm1.astype(BF)
        @pl.when(first)
        def _():
            for c in ci: c.wait()
        for a in range(0,ff,width):
            one,two=gelu_pair(dot_nn(low,win[:,a:a+width])+c_ref[:,a:a+width])
            act[:,a:a+width]=one.astype(BF); slope[:,a:a+width]=two.astype(BF)
        @pl.when(first)
        def _():
            for c in cb: c.wait()
        hat2,inv2=stats(norm1+(dot_nn(act[...],wback[...])+vec_ref[5:6,:]))
        chunk_store(chunks,mez_ref[0],(hat2*vec_ref[7:8,:]+vec_ref[9:10,:]).astype(BF))
        up=up_ref[...].astype(F32)
        col=lambda v:jnp.sum(v,axis=0,keepdims=True)
        vg_ref[7:8,:]+=col(up*hat2); vg_ref[9:10,:]+=col(up)
        second=norm_back(up*vec_ref[7:8,:],hat2,inv2)
        bg=second.astype(BF)
        vg_ref[5:6,:]+=col(bg.astype(F32))
        acc=second
        for a in range(0,ff,width):
            ig=(dot_nt(bg,wback[a:a+width,:])*slope[:,a:a+width].astype(F32)).astype(BF)
            cg_ref[:,a:a+width]+=col(ig.astype(F32))
            acc=acc+dot_nt(ig,win[:,a:a+width])
            acc_in[:,a:a+width]+=dot_tn(low,ig)
            acc_back[a:a+width,:]+=dot_tn(act[:,a:a+width],bg)
        vg_ref[6:7,:]+=col(acc*hat1); vg_ref[8:9,:]+=col(acc)
        gs=norm_back(acc*vec_ref[6:7,:],hat1,inv1)
        gs_ref[...]=gs
        ag=gs.astype(BF)
        acc_out[...]+=dot_tn(merged,ag)
        vg_ref[4:5,:]+=col(ag.astype(F32))
        mg_ref[...]=dot_nt(ag,wout[...]).astype(BF)
        @pl.when(step==steps-1)
        def _():
            m=me_ref[0]
            for slot in range(n):
                for h in range(2):
                    part=acc_out[pl.ds(pl.multiple_of((m^slot)*shard,shard),shard),h*cols:(h+1)*cols]
                    (send_v if slot%2 else keep_v)[slot//2,h*shard:(h+1)*shard,:]=part.astype(BF)
            sides=[pltpu.make_async_copy(keep_v,keep.at[:,pl.ds(0,2*shard)],out_sems.at[2*blocks])]
            if n>1: sides.append(pltpu.make_async_copy(send_v,send.at[:,pl.ds(0,2*shard)],out_sems.at[2*blocks+1]))
            for c in sides: c.start()
            copies=[]
            for b in range(2*blocks):
                slot=b%2
                if b>=2: copies[b-2].wait()
                if b<blocks:
                    stage[slot]=acc_in[:,b*width:(b+1)*width].astype(BF)
                    here=stage.at[slot].reshape(n,shard,width)
                    there=pack.at[:,pl.ds(b*shard,shard)]
                else:
                    at=(b-blocks)*width
                    stage[slot]=acc_back[at:at+width,:].astype(BF)
                    if n==1:
                        here,there=stage.at[slot],pack.at[0,pl.ds(blocks*shard+at,width)]
                    else:
                        here=stage.at[slot].reshape(width//fs,fs,width)
                        there=pack.at[pl.ds(at//fs,width//fs),pl.ds(blocks*shard,fs)]
                copies.append(pltpu.make_async_copy(here,there,out_sems.at[b]))
                copies[b].start()
            for c in copies[-2:]+sides: c.wait()
    blk=lambda w:pl.BlockSpec((RB,w),lambda i:(i,0))
    full=lambda s:pl.BlockSpec(s,lambda i:(0,0))
    return pl.pallas_call(body,grid=(steps,),
        in_specs=[SMEM,SMEM,full(pos.shape),blk(width),full(ctxg.shape),blk(width),blk(width),full(vecs.shape),full(c_row.shape)]+[ANY]*w,
        out_specs=[full((RB,width))]*steps+[blk(width)]*2+[full((16,width)),full((1,ff)),ANY,ANY,ANY],
        out_shape=[S((RB,width),BF)]*steps+[S((length,width),F32),S((length,width),BF),S((16,width),F32),S((1,ff),F32),S((n,blocks*shard+fs,width),BF)]+[S((half,2*shard+extra,cols),BF)]*2,
        scratch_shapes=[pltpu.VMEM((width,width),BF),pltpu.VMEM((width,ff),BF),pltpu.VMEM((ff,width),BF),pltpu.VMEM((width,ff),F32),pltpu.VMEM((ff,width),F32),pltpu.VMEM((width,width),F32),
            pltpu.VMEM((RB,ff),BF),pltpu.VMEM((RB,ff),BF),pltpu.VMEM((2,width,width),BF),pltpu.VMEM((half,2*shard,cols),BF),pltpu.VMEM((half,2*shard,cols),BF),pltpu.SemaphoreType.DMA((2*n+n*blocks,)),pltpu.SemaphoreType.DMA((2*blocks+2,))],
        compiler_params=params(),cost_estimate=cost(COST,1<<20),name="layer")(me,mez,pos,ctx,ctxg,x,upstream,vecs,c_row,*ffw)


def local_grads(me,x,grads,unit=None,vec=None,count=8):
    length,width=x.shape; cols=grads[0].shape[1]; shard=width//count; half=count//2; k=len(grads)
    tail=0 if vec is None else 16
    rows=k*shard+tail
    base=0 if unit is None else unit[0].shape[1]-rows
    extra=([] if vec is None else [vec])+([] if unit is None else list(unit))
    def body(me_ref,x_ref,*refs):
        outs=refs[k+len(extra):]
        keep,send,res,keep_v,send_v,vec_v,sems=outs
        m=me_ref[0]
        xt=x_ref[...].T
        for r in range(k):
            res[...]=dot_nn(xt,refs[r][...])
            for slot in range(count):
                part=res[pl.ds(pl.multiple_of((m^slot)*shard,shard),shard),:]
                (send_v if slot%2 else keep_v)[slot//2,r*shard:(r+1)*shard,:]=part.astype(BF)
        if vec is not None:
            vec_v[...]=jnp.zeros_like(vec_v)
            for s in range(count):
                vec_v[s,:,0:shard]=refs[k][:,s*shard:(s+1)*shard]
            for slot in range(count):
                (send_v if slot%2 else keep_v)[slot//2,k*shard:rows,:]=vec_v[m^slot].astype(BF)
        cps=[pltpu.make_async_copy(v,o.at[:,pl.ds(base,rows)],sems.at[i]) for i,(v,o) in enumerate(((keep_v,keep),(send_v,send)))]
        for c in cps: c.start()
        for c in cps: c.wait()
    o=S((half,base+rows,cols),BF)
    vm=pl.BlockSpec(memory_space=pltpu.VMEM)
    first=1+1+k+(0 if vec is None else 1)
    return pl.pallas_call(body,in_specs=[SMEM]+[vm]*(first-1)+[ANY]*(0 if unit is None else 2),out_specs=[ANY]*2,out_shape=[o,o],
        input_output_aliases={} if unit is None else {first:0,first+1:1},
        scratch_shapes=[pltpu.VMEM((width,cols),F32),pltpu.VMEM((half,rows,cols),BF),pltpu.VMEM((half,rows,cols),BF),pltpu.VMEM((count,16,cols),F32),pltpu.SemaphoreType.DMA((2,))],
        compiler_params=params(),cost_estimate=cost(COST,1<<20),name="local_grads")(me,x,*grads,*extra)


def collect(mez,pieces):
    def body(mez_ref,*refs):
        for slot in range(len(pieces)):
            @pl.when(pl.program_id(0)^mez_ref[0]==slot)
            def _(slot=slot): refs[-1][0]=refs[slot][...]
    rows,width=pieces[0].shape; n=len(pieces)
    return pl.pallas_call(body,grid=(n,),in_specs=[SMEM]+[pl.BlockSpec((rows,width),lambda i:(0,0))]*n,
        out_specs=pl.BlockSpec((1,rows,width),lambda i:(i,0,0)),out_shape=S((n,rows,width),BF),
        compiler_params=params(),cost_estimate=cost(COST,1<<20),name="collect")(mez,*pieces)


def project(me,x,pieces,vecs):
    length,width=x.shape; n=len(pieces); shard=width//n
    def body(me_ref,x_ref,vec_ref,*refs):
        ins=refs[:n]; q_ref,k_ref,v_ref,wts,sems=refs[n:]
        m=me_ref[0]
        cps=[fetches(ins,wts.at[j],sems,m,j*shard,shard,j*n) for j in range(3)]
        for j in range(3):
            for c in cps[j]: c.start()
        for c in cps[0]: c.wait()
        scale=HEAD_DIM**-0.5
        for a in range(0,length,RB):
            q_ref[a:a+RB,:]=((dot_nn(x_ref[a:a+RB,:],wts[0])+vec_ref[0:1,:])*scale).astype(BF)
        for c in cps[1]: c.wait()
        for a in range(0,length,RB):
            k_ref[a:a+RB,:]=dot_nn(x_ref[a:a+RB,:],wts[1]).astype(BF)
        for c in cps[2]: c.wait()
        for a in range(0,length,RB):
            v_ref[a:a+RB,:]=(dot_nn(x_ref[a:a+RB,:],wts[2])+vec_ref[1:2,:]).astype(BF)
    vm=pl.BlockSpec(memory_space=pltpu.VMEM)
    return pl.pallas_call(body,in_specs=[SMEM,vm,vm]+[ANY]*n,out_specs=[vm]*3,out_shape=[S((length,width),BF)]*3,
        scratch_shapes=[pltpu.VMEM((3,width,width),BF),pltpu.SemaphoreType.DMA((3*n,))],
        compiler_params=params(),cost_estimate=cost(COST,1<<20),name="project")(me,x,vecs,*pieces)

def own_mask(width):
    return lax.broadcasted_iota(jnp.int32,(16,width),0)==lax.broadcasted_iota(jnp.int32,(16,width),1)//HEAD_DIM

def one_hot(pos,length):
    return jnp.where(lax.broadcasted_iota(jnp.int32,(16,length),1)==pos,1.0,0.0)

def scatter_heads(rows,own,count):
    zero=jnp.zeros((16,rows.shape[1]),F32)
    return jnp.concatenate([jnp.where(own,jnp.broadcast_to(rows[g:g+1,:].astype(F32),zero.shape),zero) for g in range(count)],axis=0).astype(BF)

def gather_heads(value,own,count):
    rows=[jnp.sum(jnp.where(own,value[16*g:16*g+16],0.0),axis=0,keepdims=True) for g in range(count)]
    rows.append(jnp.zeros((16-count,value.shape[1]),F32))
    return jnp.concatenate(rows,axis=0)

def globals_fwd(pos,x,ffw,vecs,count,n):
    length,width=x.shape; wide=16*count; w=len(ffw)
    def body(pos_ref,x_ref,vec_ref,*refs):
        ins=refs[:w]; ctx_ref,p_ref,u_ref,y_ref,q_ref,r_ref,wts,sems=refs[w:]
        cps=[plane_copies(ins,j,wts.at[j],sems,j*n) for j in range(3)]
        for j in range(3):
            for c in cps[j]: c.start()
        own=own_mask(width)
        sel=one_hot(pos_ref[...],length).astype(BF)
        rows=dot_nn(sel,x_ref[...]).astype(BF)
        r_ref[...]=rows
        for c in cps[0]: c.wait()
        q=((dot_nn(rows,wts[0])+vec_ref[2:3,:])*(HEAD_DIM**-0.5)).astype(BF)
        q_ref[...]=q
        for c in cps[1]: c.wait()
        u=dot_nt(scatter_heads(q,own,count),wts[1]).astype(BF)
        u_ref[...]=u
        s=dot_nt(x_ref[...],u)
        p=jnp.exp(s-jnp.max(s,axis=0,keepdims=True))
        p=p/jnp.sum(p,axis=0,keepdims=True)
        p_ref[...]=p
        low=p.astype(BF)
        y=dot_tn(low,x_ref[...]).astype(BF)
        y_ref[...]=y
        mass=dot_tn(low,jnp.ones((length,128),BF))[:,0:1]
        for c in cps[2]: c.wait()
        ctx_ref[...]=gather_heads(dot_nn(y,wts[2])+mass*vec_ref[3:4,:],own,count).astype(BF)
    vm=pl.BlockSpec(memory_space=pltpu.VMEM)
    return pl.pallas_call(body,in_specs=[vm,vm,vm]+[ANY]*w,out_specs=[vm]*6,
        out_shape=[S((16,width),BF),S((length,wide),F32),S((wide,width),BF),S((wide,width),BF),S((16,width),BF),S((16,width),BF)],
        scratch_shapes=[pltpu.VMEM((3,width,width),BF),pltpu.SemaphoreType.DMA((3*n,))],
        compiler_params=params(),cost_estimate=cost(COST,1<<20),name="globals")(pos,x,vecs,*ffw)

def globals_bwd(me,pos,x,mg,p,u,y,q,rows,ffw,vecs,count,n):
    length,width=x.shape; shard=width//n; half=max(n//2,1); w=len(ffw); cols=width//2
    def body(me_ref,pos_ref,x_ref,mg_ref,p_ref,u_ref,y_ref,q_ref,r_ref,vec_ref,*refs):
        ins=refs[:w]; f_ref,g_ref,keep,send,vg_ref,wts,res,keep_v,send_v,sems=refs[w:]
        m=me_ref[0]
        cps=[plane_copies(ins,j,wts.at[j],sems,j*n) for j in range(3)]
        for j in (2,1,0):
            for c in cps[j]: c.start()
        own=own_mask(width)
        hot=one_hot(pos_ref[...],length)
        sel=hot.astype(BF)
        x=x_ref[...]
        cs=scatter_heads(dot_nn(sel,mg_ref[...]).astype(BF),own,count)
        qs=scatter_heads(q_ref[...],own,count)
        for c in cps[2]: c.wait()
        v=dot_nt(cs,wts[2]).astype(BF)
        shift=dot_nt(jnp.broadcast_to(vec_ref[3:4,:],(16,width)).astype(BF),cs)[0:1,:]
        dp=dot_nt(x,v)+shift
        p=p_ref[...]
        low=p.astype(BF)
        ds=(p*(dp-jnp.sum(p*dp,axis=0,keepdims=True))).astype(BF)
        a=dot_tn(ds,x).astype(BF)
        for c in cps[1]: c.wait()
        pre=(gather_heads(dot_nn(a,wts[1]),own,count).astype(BF).astype(F32)*(HEAD_DIM**-0.5)).astype(BF)
        for c in cps[0]: c.wait()
        rows_grad=dot_nt(pre,wts[0])
        mass=dot_tn(low,jnp.ones((length,128),BF))[:,0:1]
        vg_ref[...]=jnp.zeros_like(vg_ref)
        vg_ref[2:3,:]=jnp.sum(pre.astype(F32),axis=0,keepdims=True)
        vg_ref[3:4,:]=jnp.sum(mass*cs.astype(F32),axis=0,keepdims=True)
        wide=16*count
        twice=jnp.concatenate([pos_ref[...],pos_ref[...],jnp.full((96,1),-1,jnp.int32)],axis=0)
        hots=jnp.where(lax.broadcasted_iota(jnp.int32,(128,length),1)==twice,1.0,0.0)
        high=rows_grad.astype(BF)
        f_ref[:,0:wide]=ds; f_ref[:,wide:2*wide]=low; f_ref[:,2*wide:2*wide+128]=hots.T.astype(BF)
        g_ref[...]=jnp.zeros_like(g_ref)
        g_ref[0:wide,:]=u_ref[...]; g_ref[wide:2*wide,:]=v
        g_ref[2*wide:2*wide+16,:]=high; g_ref[2*wide+16:2*wide+32,:]=(rows_grad-high.astype(F32)).astype(BF)
        for j,(l,r) in enumerate(((r_ref[...],pre),(a,qs),(y_ref[...],cs))):
            res[...]=dot_tn(l,r)
            for slot in range(n):
                for h in range(2):
                    part=res[pl.ds(pl.multiple_of((m^slot)*shard,shard),shard),h*cols:(h+1)*cols]
                    (send_v if slot%2 else keep_v)[slot//2,(2*j+h)*shard:(2*j+h+1)*shard,:]=part.astype(BF)
        cps=[pltpu.make_async_copy(keep_v,keep,sems.at[3*n])]
        if n>1: cps.append(pltpu.make_async_copy(send_v,send,sems.at[3*n+1]))
        for c in cps: c.start()
        for c in cps: c.wait()
    vm=pl.BlockSpec(memory_space=pltpu.VMEM)
    o=S((half,6*shard,cols),BF)
    return pl.pallas_call(body,in_specs=[SMEM]+[vm]*9+[ANY]*w,out_specs=[vm,vm,ANY,ANY,vm],
        out_shape=[S((length,32*count+128),BF),S((32*count+128,width),BF),o,o,S((16,width),F32)],
        scratch_shapes=[pltpu.VMEM((3,width,width),BF),pltpu.VMEM((width,width),F32),pltpu.VMEM((half,6*shard,cols),BF),pltpu.VMEM((half,6*shard,cols),BF),pltpu.SemaphoreType.DMA((3*n+2,))],
        compiler_params=params(),cost_estimate=cost(COST,1<<20),name="globals_back")(me,pos,x,mg,p,u,y,q,rows,vecs,*ffw)


def inputs_back(me,mez,gs,glob,groups,pieces):
    length,width=gs.shape; n=len(pieces); shard=width//n; g=len(groups); cols=width//g
    steps=length//RB
    def body(me_ref,mez_ref,gs_ref,f_ref,g_ref,*refs):
        parts=refs[:3*g]; ins=refs[3*g:3*g+n]; chunks=refs[3*g+n:3*g+n+steps]; vg_ref,wts,sems=refs[3*g+n+steps:]
        m=me_ref[0]
        @pl.when(pl.program_id(0)==0)
        def _():
            cps=sum([fetches(ins,wts.at[j],sems,m,j*shard,shard,j*n) for j in range(3)],[])
            for c in cps: c.start()
            vg_ref[...]=jnp.zeros_like(vg_ref)
            for c in cps: c.wait()
        acc=gs_ref[...]+dot_nn(f_ref[...],g_ref[...])
        for j in range(g):
            a=j*cols
            for w in range(3): acc=acc+dot_nt(parts[3*j+w][...],wts[w,:,a:a+cols])
            vg_ref[0:1,a:a+cols]+=jnp.sum(parts[3*j][...].astype(F32),axis=0,keepdims=True)
            vg_ref[1:2,a:a+cols]+=jnp.sum(parts[3*j+2][...].astype(F32),axis=0,keepdims=True)
        chunk_store(chunks,mez_ref[0],acc.astype(BF))
    blk=pl.BlockSpec((RB,width),lambda i:(i,0))
    part=pl.BlockSpec((RB,cols),lambda i:(i,0))
    return pl.pallas_call(body,grid=(length//RB,),in_specs=[SMEM,SMEM,blk,pl.BlockSpec((RB,glob[0].shape[1]),lambda i:(i,0)),pl.BlockSpec(glob[1].shape,lambda i:(0,0))]+[part]*(3*g)+[ANY]*n,
        out_specs=[pl.BlockSpec((RB,width),lambda i:(0,0))]*steps+[pl.BlockSpec((16,width),lambda i:(0,0))],out_shape=[S((RB,width),BF)]*steps+[S((16,width),F32)],
        scratch_shapes=[pltpu.VMEM((3,width,width),BF),pltpu.SemaphoreType.DMA((3*n,))],
        compiler_params=params(),cost_estimate=cost(COST,1<<20),name="inputs_back")(me,mez,gs,*glob,*[p for t in groups for p in t],*pieces)


def flip(value, axis, bit):
    count = lax.axis_size(axis)
    return lax.ppermute(value, axis, [(index, index ^ bit) for index in range(count)])


def tie(value, *others):
    return lax.optimization_barrier((value,) + others)[0]


def spread_slots(unit, order):
    slots = {0: unit}
    for bit in order:
        for slot in list(slots):
            slots[slot | bit] = flip(slots[slot], "fsdp", bit)
    return [slots[slot] for slot in range(len(slots))]


def add(one, two):
    return one.astype(F32) + two.astype(F32)


def meet(values, parts, *others):
    flat = [list(part.got) if isinstance(part.got, list) else [part.got] for part in parts]
    joined = tuple(values) + tuple(got for gots in flat for got in gots) + others
    joined = list(lax.optimization_barrier(joined))
    values = [joined.pop(0) for _ in values]
    for part, gots in zip(parts, flat):
        new = [joined.pop(0) for _ in gots]
        part.got = new if isinstance(part.got, list) else new[0]
    return values


class Exchange:
    def __init__(self, chunks):
        self.got = [chunks[0]] + [flip(chunks[k], "sp", k) for k in range(1, len(chunks))]


class Reduction:
    def __init__(self, keep, send, x_first):
        self.keep, self.first, self.step = keep, send, 0
        self.got = flip(send, "fsdp", 1)
        self.x_first = x_first

    def advance(self, *gates):
        got = tie(self.got, *gates)
        x_now = self.x_first == (self.step == 0)
        if self.step == 0:
            keep = self.keep.reshape((2, 2) + self.keep.shape[1:])
            got = got.reshape(keep.shape)
            if self.x_first:
                away, here = (keep[:, 1], got[:, 1]), (keep[:, 0], got[:, 0])
            else:
                away, here = (keep[1], got[1]), (keep[0], got[0])
        else:
            away, here = (self.mine[1], got[1]), (self.mine[0], got[0])
        self.send, self.mine = add(*away).astype(BF), add(*here)
        self.got = flip(self.send, "fsdp", 2 if x_now else 4)
        self.step += 1
        return self.send

    def total(self):
        return add(self.mine, self.got)


class SpSum:
    def __init__(self, value, start=True):
        self.low, self.high = lax.axis_index("sp") & 1, lax.axis_index("sp") >> 1
        rows = value.shape[0] // 4
        self.shape = value.shape
        self.value = value.reshape(2, 2, rows, value.shape[1])
        self.got = self.value
        self.step = 0
        if start:
            self.start()

    def start(self):
        self.value = self.got
        self.exchange(self.low, 1)

    def exchange(self, mine, bit):
        send = lax.dynamic_index_in_dim(self.value, 1 - mine, 0, keepdims=False).astype(BF)
        self.value = lax.dynamic_index_in_dim(self.value, mine, 0, keepdims=False)
        self.send, self.got = send, flip(send, "sp", bit)

    def join(self, mine):
        return jnp.stack(
            [jnp.where(mine == 0, self.value, self.got), jnp.where(mine == 0, self.got, self.value)]
        )

    def advance(self):
        if self.step == 0:
            self.value = add(self.value, self.got)
            self.exchange(self.high, 2)
        elif self.step == 1:
            self.value = add(self.value, self.got).astype(BF)
            self.got = flip(self.value, "sp", 2)
        else:
            self.value = self.join(self.high)
            self.got = flip(self.value, "sp", 1)
        self.step += 1

    def total(self):
        return self.join(self.low).reshape(self.shape).astype(F32)


def per_device(
    inputs,
    global_pos,
    w_local,
    w_global,
    w_out,
    b_proj,
    gains,
    shifts,
    w_in,
    c_in,
    w_back,
    cotangent,
):
    sp_count = lax.axis_size("sp")
    fsdp_count = lax.axis_size("fsdp")
    sp_index = lax.axis_index("sp")
    fsdp_index = lax.axis_index("fsdp")
    own_seqs = inputs.shape[0] // sp_count
    glob_count = global_pos.shape[1]
    shard, width = w_out.shape
    ff_shard = w_back.shape[0]
    ff_width = w_in.shape[1]
    tree = fsdp_count == 8 and sp_count == 4 and own_seqs == 1 and shard % 32 == 0
    tree = tree and inputs.shape[1] == RB

    def to_sequence(value):
        if own_seqs == 1:
            moved = lax.all_to_all(value, "sp", split_axis=0, concat_axis=0)
            return moved.reshape(1, -1, width)
        return lax.all_to_all(value, "sp", split_axis=0, concat_axis=1, tiled=True)

    def to_tokens(values):
        if own_seqs == 1:
            return lax.all_to_all(
                values[0].reshape(sp_count, -1, width), "sp", split_axis=0, concat_axis=0
            )
        return lax.all_to_all(jnp.stack(values), "sp", split_axis=1, concat_axis=0, tiled=True)

    own_pos = lax.dynamic_slice_in_dim(global_pos, sp_index * own_seqs, own_seqs, 0)
    blocks = ff_width // width
    x_all = to_sequence(inputs)
    vec_rows = [b_proj, gains, shifts, c_in.reshape(-1, shard)]
    small = jnp.concatenate(vec_rows, axis=0)
    small = jnp.pad(small, ((0, 16 - small.shape[0]), (0, 0)))
    if tree:
        me = fsdp_index.reshape(1).astype(jnp.int32)
        mez = sp_index.reshape(1).astype(jnp.int32)
        first = jnp.concatenate(
            [w_local.reshape(-1, width), jnp.pad(small, ((0, 0), (0, width - shard)))], axis=0
        )
        local_w = spread_slots(first, (2, 4, 1))
        pack = jnp.concatenate(
            [
                w_in.reshape(shard, blocks, width).transpose(1, 0, 2).reshape(-1, width),
                w_back,
                w_global.reshape(-1, width),
                w_out,
            ],
            axis=0,
        )
        ffw = [lax.all_gather(pack, "fsdp")]
        small_all = jnp.stack([piece[3 * shard :, :shard] for piece in local_w])
        small_all = small_all[me[0] ^ jnp.arange(fsdp_count, dtype=jnp.int32)]
    else:
        me = mez = jnp.zeros((1,), jnp.int32)
        local_w = [lax.all_gather(w_local, "fsdp", axis=1, tiled=True).reshape(-1, width)]
        full_global = lax.all_gather(w_global, "fsdp", axis=1, tiled=True).reshape(-1, width)
        full_out = lax.all_gather(w_out, "fsdp", axis=0, tiled=True)
        ffw = [lax.all_gather(value, "fsdp", axis=0, tiled=True) for value in (w_in, w_back)]
        ffw.append(jnp.concatenate([full_global, full_out], axis=0))
        small_all = lax.all_gather(small, "fsdp")
    count = len(local_w)
    up_all = to_sequence(tie(cotangent, x_all))
    vecs = small_all.transpose(1, 0, 2).reshape(16, width).astype(F32)
    c_rows = small_all[:, 10 : 10 + ff_shard // shard].astype(F32)
    c_row = c_rows.reshape(1, ff_width)

    outs, input_grads, totals = [], [], None
    for index in range(own_seqs):
        x = x_all[index]
        pos = jnp.full((16, 1), -1, jnp.int32).at[:glob_count, 0].set(own_pos[index])
        q, k, v = project(me, x, local_w, vecs)
        ctx, lse = attn_fwd(pos, q, k, v)
        ctx_glob, probs, keys, mixed, query, rows = globals_fwd(
            pos, x, ffw, vecs, glob_count, count
        )
        *out, grad_sum, merged_grad, vec_one, c_grad, ff_pack, keep_two, send_two = layer(
            me, mez, pos, ctx, ctx_glob, x, up_all[index], ffw, vecs, c_row, count,
            3 * shard if tree else 0,
        )
        if tree:
            out_moved = Exchange(out)
        else:
            outs.append(jnp.concatenate(out, axis=0))
        if tree:
            ff_mine = lax.psum_scatter(ff_pack, "fsdp", scatter_dimension=0, tiled=False)
            merged_grad = tie(merged_grad, ff_pack)
        *glob, keep_one, send_one, vec_two = globals_bwd(
            me, pos, x, merged_grad, probs, keys, mixed, query, rows, ffw, vecs, glob_count, count
        )
        group_pairs = width // 128 // GROUPS
        groups = []
        if tree:
            one = Reduction(keep_one, send_one, True)
            merged_grad = tie(merged_grad, send_one)
        for group in range(GROUPS):
            parts = attn_bwd(
                pos, q, k, v, merged_grad, ctx, lse, group * group_pairs, group_pairs
            )
            groups.append(parts)
            if tree and group == 0:
                two = Reduction(*local_grads(me, x, parts, unit=(keep_two, send_two)), False)
                (merged_grad,) = meet([merged_grad], [out_moved], two.first)
        if tree:
            (grad_sum,) = meet([grad_sum], [one, two], parts[0])
            grad_sum = tie(grad_sum, one.advance(), two.advance())
        *input_grad, vec_three = inputs_back(me, mez, grad_sum, glob, groups, local_w)
        if tree:
            grads_moved = Exchange(input_grad)
        else:
            input_grads.append(jnp.concatenate(input_grad, axis=0))
        c_grad = c_grad.reshape(fsdp_count, -1, shard).transpose(1, 0, 2).reshape(-1, width)
        vec = vec_one + vec_two + vec_three + jnp.pad(c_grad, ((10, 6 - c_grad.shape[0]), (0, 0)))
        if not tree:
            g_in = ff_pack[0, :ff_width].reshape(blocks, width, width).transpose(1, 0, 2)
            g_in = g_in.reshape(width, ff_width).astype(F32)
            g_back = ff_pack[0, ff_width:].astype(F32)
            g_mixed = jnp.concatenate([keep_one[0], keep_two[0]], axis=0)
            g_mixed = g_mixed.reshape(4, 2, width, width // 2).transpose(0, 2, 1, 3)
            grads = (
                g_back,
                g_in,
                g_mixed.reshape(4, width, width).astype(F32),
                jnp.stack(
                    [
                        jnp.concatenate([dot_tn(x, part[w]) for part in groups], axis=1)
                        for w in range(3)
                    ]
                ),
                vec,
            )
            totals = grads if totals is None else tuple(a + b for a, b in zip(totals, grads))
    if tree:
        x_late, ff_mine = meet([x, ff_mine], [], *input_grad)
        ff_sum = SpSum(ff_mine.astype(F32))
        x_late = tie(x_late, ff_sum.send)
        late = Reduction(*local_grads(me, x_late, groups[-1], vec=vec), False)
        meet([], [one, two, ff_sum, grads_moved], late.first)
        one.advance()
        two.advance()
        ff_sum.advance()
        meet([], [late], one.send, two.send, ff_sum.send)
        late.advance()
        meet([], [one, two, late, ff_sum])
        early_sum = SpSum(jnp.concatenate([one.total(), two.total()], axis=0))
        late.advance()
        ff_sum.advance()
        out = collect(mez, out_moved.got)
        meet([], [late, ff_sum, early_sum])
        late_sum = SpSum(late.total())
        early_sum.advance()
        ff_sum.advance()
        grad_inputs = collect(mez, grads_moved.got)
        meet([], [early_sum, late_sum, ff_sum])
        early_sum.advance()
        late_sum.advance()
        s_ff = ff_sum.total()
        meet([], [early_sum, late_sum])
        early_sum.advance()
        late_sum.advance()
        meet([], [early_sum, late_sum])
        late_sum.advance()
        s_early, s_late = early_sum.total(), late_sum.total()
        half_mixed = s_early[: 8 * shard].reshape(4, 2, shard, -1).transpose(0, 2, 1, 3)
        s_mixed = half_mixed.reshape(4, shard, width)
        s_local = jnp.concatenate(
            [
                s_early[8 * shard :].reshape(3, shard, -1),
                s_late[: 3 * shard].reshape(3, shard, -1),
            ],
            axis=2,
        )
        mine = s_late[3 * shard :, :shard]
        s_in = s_ff[: blocks * shard].reshape(blocks, shard, width).transpose(1, 0, 2)
        s_in = s_in.reshape(shard, ff_width)
        s_back = s_ff[blocks * shard :]
    else:
        out, grad_inputs = to_tokens(outs), to_tokens(input_grads)
        g_back, g_in, g_mixed, g_local, vec = totals

        def reduce(value, dim):
            mine = lax.psum_scatter(value.astype(BF), "fsdp", scatter_dimension=dim, tiled=True)
            return lax.psum(mine, "sp").astype(F32)

        s_back, s_in = reduce(g_back, 0), reduce(g_in, 0)
        s_mixed = reduce(g_mixed, 1)
        s_local = reduce(g_local, 1)
        vec = lax.psum(vec, ("fsdp", "sp"))
        mine = lax.dynamic_slice_in_dim(vec, fsdp_index * shard, shard, 1)
    c_mine = mine[10 : 10 + ff_shard // shard].reshape(-1)
    return (
        out,
        grad_inputs,
        s_local,
        s_mixed[:3],
        s_mixed[3],
        mine[:6],
        mine[6:8],
        mine[8:10],
        s_in,
        c_mine,
        s_back,
    )


def solution(mesh):
    rows = P("fsdp", None)
    tokens = P("fsdp", "sp", None)
    columns = P(None, "fsdp")
    stacked = P(None, "fsdp", None)
    return jax.shard_map(
        per_device,
        mesh=mesh,
        in_specs=(
            tokens,
            rows,
            stacked,
            stacked,
            rows,
            columns,
            columns,
            columns,
            rows,
            P("fsdp"),
            rows,
            tokens,
        ),
        out_specs=(
            tokens,
            tokens,
            stacked,
            stacked,
            rows,
            columns,
            columns,
            columns,
            rows,
            P("fsdp"),
            rows,
        ),
        check_vma=False,
    )
```

```python
import jax
import jax.numpy as jnp
from jax import lax
from jax.experimental import pallas as pl
from jax.experimental.pallas import tpu as pltpu
from jax.sharding import PartitionSpec as P

HEADS = 12
HEAD_DIM = 64
WIN = 256
QB = 128
NEG = -1e9
GROUPS = 2
COST = 2 * 10**10
NORM_EPS = 1e-05
BF = jnp.bfloat16
F32 = jnp.float32
S = jax.ShapeDtypeStruct


def dot_nn(a,b): return jnp.dot(a,b,preferred_element_type=F32)
def dot_nt(a,b): return lax.dot_general(a,b,(((1,),(1,)),((),())),preferred_element_type=F32)
def dot_tn(a,b): return lax.dot_general(a,b,(((0,),(0,)),((),())),preferred_element_type=F32)

def split_pair(block):
    lane=lax.broadcasted_iota(jnp.int32,block.shape,1)
    zero=jnp.zeros_like(block)
    return jnp.concatenate([jnp.where(lane<HEAD_DIM,block,zero),jnp.where(lane<HEAD_DIM,zero,block)],axis=0)

def far_mask(pos, start):
    place=start+lax.broadcasted_iota(jnp.int32,(16,2*QB),1)%QB
    return (pos>=0)&(jnp.abs(place-pos)>WIN)

def edge_masks():
    row=lax.broadcasted_iota(jnp.int32,(QB,2*QB),0)
    col=lax.broadcasted_iota(jnp.int32,(QB,2*QB),1)%QB
    return row>=col, row<=col

def key_range(start,length):
    return max(0,start-WIN), min(length,start+QB+WIN)

def pick_head(both):
    row=lax.broadcasted_iota(jnp.int32,(2*HEAD_DIM,QB),0)
    return jnp.where(row<HEAD_DIM,both[:,:QB],both[:,QB:])

def masked_scores(raw,start,length,low_ok,high_ok):
    lo,hi=key_range(start,length)
    parts=[]
    for first in range(lo,hi,QB):
        chunk=raw[first-lo:first-lo+QB]
        if first==start-WIN: chunk=jnp.where(low_ok,chunk,NEG)
        elif first==start+WIN: chunk=jnp.where(high_ok,chunk,NEG)
        parts.append(chunk)
    return parts

def fwd_kernel(pos_ref,q_ref,k_ref,v_ref,ctx_ref,lse_ref):
    length=q_ref.shape[0]
    pos=pos_ref[...]
    token=lax.broadcasted_iota(jnp.int32,(16,length),1)
    sel=jnp.where(token==pos,1.0,0.0).astype(BF)
    key_far=dot_nn(sel,k_ref[...]).astype(BF)
    val_far_t=dot_nn(sel,v_ref[...]).astype(BF).T
    val_t=v_ref[...].T
    low_ok,high_ok=edge_masks()
    def products(start):
        lo,hi=key_range(start,length)
        qq=split_pair(q_ref[start:start+QB,:])
        return dot_nt(k_ref[lo:hi,:],qq),dot_nt(key_far,qq)
    ahead=products(0)
    for start in range(0,length,QB):
        lo,hi=key_range(start,length)
        raw,raw_far=ahead
        if start+QB<length: ahead=products(start+QB)
        parts=masked_scores(raw,start,length,low_ok,high_ok)
        far=jnp.where(far_mask(pos,start),raw_far,NEG)
        top=jnp.max(far,axis=0,keepdims=True)
        for part in parts: top=jnp.maximum(top,jnp.max(part,axis=0,keepdims=True))
        far_p=jnp.exp(far-top)
        total=jnp.sum(far_p,axis=0,keepdims=True)
        probs=[]
        for part in parts:
            p=jnp.exp(part-top)
            total=total+jnp.sum(p,axis=0,keepdims=True)
            probs.append(p.astype(BF))
        both=dot_nn(val_t[:,lo:hi],jnp.concatenate(probs,axis=0))+dot_nn(val_far_t,far_p.astype(BF))
        both=both*(1.0/total)
        ctx_ref[start:start+QB,:]=pick_head(both).T.astype(BF)
        lse=top+jnp.log(total)
        lse_ref[0,0:1,start:start+QB]=lse[:,:QB]
        lse_ref[0,1:2,start:start+QB]=lse[:,QB:]

def attn_fwd(pos,q,k,v):
    length,width=q.shape
    pairs=width//128
    col=pl.BlockSpec((length,128),lambda i:(0,i))
    return pl.pallas_call(fwd_kernel,grid=(pairs,),
        in_specs=[pl.BlockSpec((16,1),lambda i:(0,0)),col,col,col],
        out_specs=[col,pl.BlockSpec((1,8,length),lambda i:(i,0,0))],
        out_shape=[jax.ShapeDtypeStruct((length,width),BF),jax.ShapeDtypeStruct((pairs,8,length),F32)],
        compiler_params=params(),
        cost_estimate=cost(COST,1<<20),
        name="attend")(pos,q,k,v)

def bwd_kernel(pos_ref,q_ref,k_ref,v_ref,g_ref,ctx_ref,lse_ref,dq_ref,dk_ref,dv_ref,dk_acc,dv_acc,grad_scr):
    length=q_ref.shape[0]
    pos=pos_ref[...]
    token=lax.broadcasted_iota(jnp.int32,(16,length),1)
    sel_bool=token==pos
    sel=jnp.where(sel_bool,1.0,0.0).astype(BF)
    sel_full=jnp.where(sel_bool,1.0,0.0)
    key_far=dot_nn(sel,k_ref[...]).astype(BF)
    val_far=dot_nn(sel,v_ref[...]).astype(BF)
    key_far_t=key_far.T
    key_t=k_ref[...].T
    ones=jnp.ones((16,128),F32)
    is_glob=lax.dot_general(sel_full,ones,(((0,),(0,)),((),())),preferred_element_type=F32)
    grad_scr[...]=jnp.where(is_glob>0.5,0.0,g_ref[...].astype(F32)).astype(BF)
    prod=grad_scr[...].astype(F32)*ctx_ref[...].astype(F32)
    hrow=lax.broadcasted_iota(jnp.int32,(16,128),0)
    hlane=lax.broadcasted_iota(jnp.int32,(16,128),1)//HEAD_DIM
    hsel=jnp.where(hrow==hlane,1.0,0.0)
    delta_all=lax.dot_general(hsel,prod,(((1,),(1,)),((),())),preferred_element_type=F32,precision=lax.Precision.HIGHEST)
    dk_acc[...]=jnp.zeros_like(dk_acc)
    dv_acc[...]=jnp.zeros_like(dv_acc)
    dk_far=jnp.zeros((16,128),F32); dv_far=jnp.zeros((16,128),F32)
    low_ok,high_ok=edge_masks()
    def products(start):
        lo,hi=key_range(start,length)
        qq=split_pair(q_ref[start:start+QB,:])
        gg=split_pair(grad_scr[start:start+QB,:])
        raw=dot_nt(jnp.concatenate([k_ref[lo:hi,:],key_far],axis=0),qq)
        dp=dot_nt(jnp.concatenate([v_ref[lo:hi,:],val_far],axis=0),gg)
        return qq,gg,raw[:hi-lo],dp[:hi-lo],raw[hi-lo:],dp[hi-lo:]
    ahead=products(0)
    for start in range(0,length,QB):
        lo,hi=key_range(start,length)
        qq,gg,raw,dp_all,raw_far,dp_far=ahead
        if start+QB<length: ahead=products(start+QB)
        lse=jnp.concatenate([lse_ref[0,0:1,start:start+QB],lse_ref[0,1:2,start:start+QB]],axis=1)
        delta=jnp.concatenate([delta_all[0:1,start:start+QB],delta_all[1:2,start:start+QB]],axis=1)
        def one(scores,dp):
            p=jnp.exp(scores-lse)
            return p.astype(BF),(p*(dp-delta)).astype(BF)
        far=jnp.where(far_mask(pos,start),raw_far,NEG)
        p_far,ds_far=one(far,dp_far)
        parts=masked_scores(raw,start,length,low_ok,high_ok)
        both=[one(part,dp_all[n*QB:(n+1)*QB]) for n,part in enumerate(parts)]
        p=jnp.concatenate([pair[0] for pair in both]+[p_far],axis=0)
        ds=jnp.concatenate([pair[1] for pair in both]+[ds_far],axis=0)
        dv_all,dk_all=dot_nn(p,gg),dot_nn(ds,qq)
        dv_acc[lo:hi,:]+=dv_all[:hi-lo]
        dk_acc[lo:hi,:]+=dk_all[:hi-lo]
        dv_far=dv_far+dv_all[hi-lo:]; dk_far=dk_far+dk_all[hi-lo:]
        dq_t=dot_nn(jnp.concatenate([key_t[:,lo:hi],key_far_t],axis=1),ds)
        dq_ref[start:start+QB,:]=(pick_head(dq_t).T.astype(BF).astype(F32)*(HEAD_DIM**-0.5)).astype(BF)
    dk_ref[...]=(dk_acc[...]+lax.dot_general(sel_full,dk_far,(((0,),(0,)),((),())),preferred_element_type=F32,precision=lax.Precision.HIGHEST)).astype(BF)
    dv_ref[...]=(dv_acc[...]+lax.dot_general(sel_full,dv_far,(((0,),(0,)),((),())),preferred_element_type=F32,precision=lax.Precision.HIGHEST)).astype(BF)

def attn_bwd(pos,q,k,v,grad,ctx,lse,first,pairs):
    length,width=q.shape
    col=pl.BlockSpec((length,128),lambda i:(0,first+i))
    out_col=pl.BlockSpec((length,128),lambda i:(0,i))
    out=jax.ShapeDtypeStruct((length,128*pairs),BF)
    return pl.pallas_call(bwd_kernel,grid=(pairs,),
        in_specs=[pl.BlockSpec((16,1),lambda i:(0,0)),col,col,col,col,col,pl.BlockSpec((1,8,length),lambda i:(first+i,0,0))],
        out_specs=[out_col,out_col,out_col],
        out_shape=[out,out,out],
        scratch_shapes=[pltpu.VMEM((length,128),F32),pltpu.VMEM((length,128),F32),pltpu.VMEM((length,128),BF)],
        compiler_params=params(),
        cost_estimate=cost(COST,1<<20),
        name="attend_back")(pos,q,k,v,grad,ctx,lse)


ANY=pl.BlockSpec(memory_space=pl.ANY)
SMEM=pl.BlockSpec(memory_space=pltpu.SMEM)
RB=256

def cost(flops,nbytes,trans=0):
    return pl.CostEstimate(flops=int(flops),bytes_accessed=int(nbytes),transcendentals=int(trans))

def params(mib=60):
    return pltpu.CompilerParams(vmem_limit_bytes=mib<<20)

def fetches(pieces,place,sems,me,first,rows,sem0):
    out=[]
    for slot,piece in enumerate(pieces):
        owner=me^slot
        out.append(pltpu.make_async_copy(piece.at[pl.ds(first,rows)],place.at[pl.ds(pl.multiple_of(owner*rows,rows),rows)],sems.at[sem0+slot]))
    return out

def ffn_in_copies(refs,place,sems,sem0):
    if len(refs)>1: return [pltpu.make_async_copy(refs[0],place,sems.at[sem0])]
    pack=refs[0]; n,_,width=pack.shape; shard=place.shape[0]//n
    return [pltpu.make_async_copy(pack.at[s,pl.ds(j*shard,shard)],place.at[pl.ds(s*shard,shard),pl.ds(j*width,width)],sems.at[sem0+s*(place.shape[1]//width)+j])
            for s in range(n) for j in range(place.shape[1]//width)]


def ffn_back_copies(refs,place,sems,sem0):
    if len(refs)>1: return [pltpu.make_async_copy(refs[1],place,sems.at[sem0])]
    pack=refs[0]; n,rows,width=pack.shape; shard=place.shape[0]//n; first=rows-4*(width//n)-shard
    return [pltpu.make_async_copy(pack.at[s,pl.ds(first,shard)],place.at[pl.ds(s*shard,shard)],sems.at[sem0+s]) for s in range(n)]


def plane_copies(refs,plane,place,sems,sem0):
    width=place.shape[0]
    if len(refs)>1: return [pltpu.make_async_copy(refs[2].at[pl.ds(plane*width,width)],place,sems.at[sem0])]
    pack=refs[0]; n,rows,_=pack.shape; shard=width//n; first=rows-(4-plane)*shard
    return [pltpu.make_async_copy(pack.at[s,pl.ds(first,shard)],place.at[pl.ds(s*shard,shard)],sems.at[sem0+s]) for s in range(n)]


def stats(value):
    center=value-jnp.mean(value,axis=-1,keepdims=True)
    inverse=lax.rsqrt(jnp.mean(center*center,axis=-1,keepdims=True)+NORM_EPS)
    return center*inverse,inverse

def norm_back(scaled,normed,inverse):
    return inverse*(scaled-jnp.mean(scaled,axis=-1,keepdims=True)-normed*jnp.mean(scaled*normed,axis=-1,keepdims=True))

def gelu_pair(inner):
    cdf=0.5*(1.0+lax.erf(inner*0.7071067811865476))
    return inner*cdf, cdf+inner*(0.3989422804014327*jnp.exp(-0.5*inner*inner))

def chunk_store(chunks,me,value):
    for slot,chunk in enumerate(chunks):
        @pl.when(pl.program_id(0)^me==slot)
        def _(chunk=chunk): chunk[...]=value


def layer(me,mez,pos,ctx,ctxg,x,upstream,ffw,vecs,c_row,n,extra):
    half=max(n//2,1); cols=x.shape[1]//2
    length,width=x.shape; ff=c_row.shape[1]; w=len(ffw); steps=length//RB; blocks=ff//width; shard=width//n; fs=ff//n
    def body(me_ref,mez_ref,pos_ref,ctx_ref,glob_ref,x_ref,up_ref,vec_ref,c_ref,*refs):
        ff_w=refs[:w]; chunks=refs[w:w+steps]
        gs_ref,mg_ref,vg_ref,cg_ref,pack,keep,send,wout,win,wback,acc_in,acc_back,acc_out,act,slope,stage,keep_v,send_v,sems,out_sems=refs[w+steps:]
        step=pl.program_id(0)
        first=step==0
        co=plane_copies(ff_w,3,wout,sems,0)
        ci=ffn_in_copies(ff_w,win,sems,n)
        cb=ffn_back_copies(ff_w,wback,sems,n+n*blocks)
        @pl.when(first)
        def _():
            for c in co+ci+cb: c.start()
            vg_ref[...]=jnp.zeros_like(vg_ref); cg_ref[...]=jnp.zeros_like(cg_ref)
            acc_in[...]=jnp.zeros_like(acc_in); acc_back[...]=jnp.zeros_like(acc_back)
            acc_out[...]=jnp.zeros_like(acc_out)
            for c in co: c.wait()
        token=step*RB+lax.broadcasted_iota(jnp.int32,(16,RB),1)
        hot=jnp.where(token==pos_ref[...],1.0,0.0).astype(BF)
        is_glob=dot_tn(hot,jnp.ones((16,128),BF))[:,0:1]>0.5
        merged=jnp.where(is_glob,dot_tn(hot,glob_ref[...]),ctx_ref[...].astype(F32)).astype(BF)
        hat1,inv1=stats(x_ref[...].astype(F32)+(dot_nn(merged,wout[...])+vec_ref[4:5,:]))
        norm1=hat1*vec_ref[6:7,:]+vec_ref[8:9,:]
        low=norm1.astype(BF)
        @pl.when(first)
        def _():
            for c in ci: c.wait()
        for a in range(0,ff,width):
            one,two=gelu_pair(dot_nn(low,win[:,a:a+width])+c_ref[:,a:a+width])
            act[:,a:a+width]=one.astype(BF); slope[:,a:a+width]=two.astype(BF)
        @pl.when(first)
        def _():
            for c in cb: c.wait()
        hat2,inv2=stats(norm1+(dot_nn(act[...],wback[...])+vec_ref[5:6,:]))
        chunk_store(chunks,mez_ref[0],(hat2*vec_ref[7:8,:]+vec_ref[9:10,:]).astype(BF))
        up=up_ref[...].astype(F32)
        col=lambda v:jnp.sum(v,axis=0,keepdims=True)
        vg_ref[7:8,:]+=col(up*hat2); vg_ref[9:10,:]+=col(up)
        second=norm_back(up*vec_ref[7:8,:],hat2,inv2)
        bg=second.astype(BF)
        vg_ref[5:6,:]+=col(bg.astype(F32))
        acc=second
        low_t=low.T
        for a in range(0,ff,width):
            ig=(dot_nt(bg,wback[a:a+width,:])*slope[:,a:a+width].astype(F32)).astype(BF)
            cg_ref[:,a:a+width]+=col(ig.astype(F32))
            acc=acc+dot_nt(ig,win[:,a:a+width])
            acc_in[:,a:a+width]+=dot_nn(low_t,ig)
            acc_back[a:a+width,:]+=dot_tn(act[:,a:a+width],bg)
        vg_ref[6:7,:]+=col(acc*hat1); vg_ref[8:9,:]+=col(acc)
        gs=norm_back(acc*vec_ref[6:7,:],hat1,inv1)
        gs_ref[...]=gs
        ag=gs.astype(BF)
        acc_out[...]+=dot_tn(merged,ag)
        vg_ref[4:5,:]+=col(ag.astype(F32))
        mg_ref[...]=dot_nt(ag,wout[...]).astype(BF)
        @pl.when(step==steps-1)
        def _():
            m=me_ref[0]
            for slot in range(n):
                for h in range(2):
                    part=acc_out[pl.ds(pl.multiple_of((m^slot)*shard,shard),shard),h*cols:(h+1)*cols]
                    (send_v if slot%2 else keep_v)[slot//2,h*shard:(h+1)*shard,:]=part.astype(BF)
            sides=[pltpu.make_async_copy(keep_v,keep.at[:,pl.ds(0,2*shard)],out_sems.at[2*blocks])]
            if n>1: sides.append(pltpu.make_async_copy(send_v,send.at[:,pl.ds(0,2*shard)],out_sems.at[2*blocks+1]))
            for c in sides: c.start()
            copies=[]
            for b in range(2*blocks):
                slot=b%2
                if b>=2: copies[b-2].wait()
                if b<blocks:
                    stage[slot]=acc_in[:,b*width:(b+1)*width].astype(BF)
                    here=stage.at[slot].reshape(n,shard,width)
                    there=pack.at[:,pl.ds(b*shard,shard)]
                else:
                    at=(b-blocks)*width
                    stage[slot]=acc_back[at:at+width,:].astype(BF)
                    if n==1:
                        here,there=stage.at[slot],pack.at[0,pl.ds(blocks*shard+at,width)]
                    else:
                        here=stage.at[slot].reshape(width//fs,fs,width)
                        there=pack.at[pl.ds(at//fs,width//fs),pl.ds(blocks*shard,fs)]
                copies.append(pltpu.make_async_copy(here,there,out_sems.at[b]))
                copies[b].start()
            for c in copies[-2:]+sides: c.wait()
    blk=lambda w:pl.BlockSpec((RB,w),lambda i:(i,0))
    full=lambda s:pl.BlockSpec(s,lambda i:(0,0))
    return pl.pallas_call(body,grid=(steps,),
        in_specs=[SMEM,SMEM,full(pos.shape),blk(width),full(ctxg.shape),blk(width),blk(width),full(vecs.shape),full(c_row.shape)]+[ANY]*w,
        out_specs=[full((RB,width))]*steps+[blk(width)]*2+[full((16,width)),full((1,ff)),ANY,ANY,ANY],
        out_shape=[S((RB,width),BF)]*steps+[S((length,width),F32),S((length,width),BF),S((16,width),F32),S((1,ff),F32),S((n,blocks*shard+fs,width),BF)]+[S((half,2*shard+extra,cols),BF)]*2,
        scratch_shapes=[pltpu.VMEM((width,width),BF),pltpu.VMEM((width,ff),BF),pltpu.VMEM((ff,width),BF),pltpu.VMEM((width,ff),F32),pltpu.VMEM((ff,width),F32),pltpu.VMEM((width,width),F32),
            pltpu.VMEM((RB,ff),BF),pltpu.VMEM((RB,ff),BF),pltpu.VMEM((2,width,width),BF),pltpu.VMEM((half,2*shard,cols),BF),pltpu.VMEM((half,2*shard,cols),BF),pltpu.SemaphoreType.DMA((2*n+n*blocks,)),pltpu.SemaphoreType.DMA((2*blocks+2,))],
        compiler_params=params(),cost_estimate=cost(COST,1<<20),name="layer")(me,mez,pos,ctx,ctxg,x,upstream,vecs,c_row,*ffw)


def local_grads(me,x,grads,unit=None,vec=None,count=8):
    length,width=x.shape; cols=grads[0].shape[1]; shard=width//count; half=count//2; k=len(grads)
    tail=0 if vec is None else 16
    rows=k*shard+tail
    base=0 if unit is None else unit[0].shape[1]-rows
    extra=([] if vec is None else [vec])+([] if unit is None else list(unit))
    def body(me_ref,x_ref,*refs):
        outs=refs[k+len(extra):]
        keep,send,res,keep_v,send_v,vec_v,sems=outs
        m=me_ref[0]
        xt=x_ref[...].T
        for r in range(k):
            res[...]=dot_nn(xt,refs[r][...])
            for slot in range(count):
                part=res[pl.ds(pl.multiple_of((m^slot)*shard,shard),shard),:]
                (send_v if slot%2 else keep_v)[slot//2,r*shard:(r+1)*shard,:]=part.astype(BF)
        if vec is not None:
            vec_v[...]=jnp.zeros_like(vec_v)
            for s in range(count):
                vec_v[s,:,0:shard]=refs[k][:,s*shard:(s+1)*shard]
            for slot in range(count):
                (send_v if slot%2 else keep_v)[slot//2,k*shard:rows,:]=vec_v[m^slot].astype(BF)
        cps=[pltpu.make_async_copy(v,o.at[:,pl.ds(base,rows)],sems.at[i]) for i,(v,o) in enumerate(((keep_v,keep),(send_v,send)))]
        for c in cps: c.start()
        for c in cps: c.wait()
    o=S((half,base+rows,cols),BF)
    vm=pl.BlockSpec(memory_space=pltpu.VMEM)
    first=1+1+k+(0 if vec is None else 1)
    return pl.pallas_call(body,in_specs=[SMEM]+[vm]*(first-1)+[ANY]*(0 if unit is None else 2),out_specs=[ANY]*2,out_shape=[o,o],
        input_output_aliases={} if unit is None else {first:0,first+1:1},
        scratch_shapes=[pltpu.VMEM((width,cols),F32),pltpu.VMEM((half,rows,cols),BF),pltpu.VMEM((half,rows,cols),BF),pltpu.VMEM((count,16,cols),F32),pltpu.SemaphoreType.DMA((2,))],
        compiler_params=params(),cost_estimate=cost(COST,1<<20),name="local_grads")(me,x,*grads,*extra)


def collect(mez,pieces):
    def body(mez_ref,*refs):
        for slot in range(len(pieces)):
            @pl.when(pl.program_id(0)^mez_ref[0]==slot)
            def _(slot=slot): refs[-1][0]=refs[slot][...]
    rows,width=pieces[0].shape; n=len(pieces)
    return pl.pallas_call(body,grid=(n,),in_specs=[SMEM]+[pl.BlockSpec((rows,width),lambda i:(0,0))]*n,
        out_specs=pl.BlockSpec((1,rows,width),lambda i:(i,0,0)),out_shape=S((n,rows,width),BF),
        compiler_params=params(),cost_estimate=cost(COST,1<<20),name="collect")(mez,*pieces)


def project(me,x,pieces,vecs):
    length,width=x.shape; n=len(pieces); shard=width//n
    def body(me_ref,x_ref,vec_ref,*refs):
        ins=refs[:n]; q_ref,k_ref,v_ref,wts,sems=refs[n:]
        m=me_ref[0]
        cps=[fetches(ins,wts.at[j],sems,m,j*shard,shard,j*n) for j in range(3)]
        for j in range(3):
            for c in cps[j]: c.start()
        for c in cps[0]: c.wait()
        scale=HEAD_DIM**-0.5
        for a in range(0,length,RB):
            q_ref[a:a+RB,:]=((dot_nn(x_ref[a:a+RB,:],wts[0])+vec_ref[0:1,:])*scale).astype(BF)
        for c in cps[1]: c.wait()
        for a in range(0,length,RB):
            k_ref[a:a+RB,:]=dot_nn(x_ref[a:a+RB,:],wts[1]).astype(BF)
        for c in cps[2]: c.wait()
        for a in range(0,length,RB):
            v_ref[a:a+RB,:]=(dot_nn(x_ref[a:a+RB,:],wts[2])+vec_ref[1:2,:]).astype(BF)
    vm=pl.BlockSpec(memory_space=pltpu.VMEM)
    return pl.pallas_call(body,in_specs=[SMEM,vm,vm]+[ANY]*n,out_specs=[vm]*3,out_shape=[S((length,width),BF)]*3,
        scratch_shapes=[pltpu.VMEM((3,width,width),BF),pltpu.SemaphoreType.DMA((3*n,))],
        compiler_params=params(),cost_estimate=cost(COST,1<<20),name="project")(me,x,vecs,*pieces)

def own_mask(width):
    return lax.broadcasted_iota(jnp.int32,(16,width),0)==lax.broadcasted_iota(jnp.int32,(16,width),1)//HEAD_DIM

def one_hot(pos,length):
    return jnp.where(lax.broadcasted_iota(jnp.int32,(16,length),1)==pos,1.0,0.0)

def scatter_heads(rows,own,count):
    zero=jnp.zeros((16,rows.shape[1]),F32)
    return jnp.concatenate([jnp.where(own,jnp.broadcast_to(rows[g:g+1,:].astype(F32),zero.shape),zero) for g in range(count)],axis=0).astype(BF)

def gather_heads(value,own,count):
    rows=[jnp.sum(jnp.where(own,value[16*g:16*g+16],0.0),axis=0,keepdims=True) for g in range(count)]
    rows.append(jnp.zeros((16-count,value.shape[1]),F32))
    return jnp.concatenate(rows,axis=0)

def globals_fwd(pos,x,ffw,vecs,count,n):
    length,width=x.shape; wide=16*count; w=len(ffw)
    def body(pos_ref,x_ref,vec_ref,*refs):
        ins=refs[:w]; ctx_ref,p_ref,u_ref,y_ref,q_ref,r_ref,wts,sems=refs[w:]
        cps=[plane_copies(ins,j,wts.at[j],sems,j*n) for j in range(3)]
        for j in range(3):
            for c in cps[j]: c.start()
        own=own_mask(width)
        sel=one_hot(pos_ref[...],length).astype(BF)
        rows=dot_nn(sel,x_ref[...]).astype(BF)
        r_ref[...]=rows
        for c in cps[0]: c.wait()
        q=((dot_nn(rows,wts[0])+vec_ref[2:3,:])*(HEAD_DIM**-0.5)).astype(BF)
        q_ref[...]=q
        for c in cps[1]: c.wait()
        u=dot_nt(scatter_heads(q,own,count),wts[1]).astype(BF)
        u_ref[...]=u
        s=dot_nt(x_ref[...],u)
        p=jnp.exp(s-jnp.max(s,axis=0,keepdims=True))
        p=p/jnp.sum(p,axis=0,keepdims=True)
        p_ref[...]=p
        low=p.astype(BF)
        y=dot_tn(low,x_ref[...]).astype(BF)
        y_ref[...]=y
        mass=dot_tn(low,jnp.ones((length,128),BF))[:,0:1]
        for c in cps[2]: c.wait()
        ctx_ref[...]=gather_heads(dot_nn(y,wts[2])+mass*vec_ref[3:4,:],own,count).astype(BF)
    vm=pl.BlockSpec(memory_space=pltpu.VMEM)
    return pl.pallas_call(body,in_specs=[vm,vm,vm]+[ANY]*w,out_specs=[vm]*6,
        out_shape=[S((16,width),BF),S((length,wide),F32),S((wide,width),BF),S((wide,width),BF),S((16,width),BF),S((16,width),BF)],
        scratch_shapes=[pltpu.VMEM((3,width,width),BF),pltpu.SemaphoreType.DMA((3*n,))],
        compiler_params=params(),cost_estimate=cost(COST,1<<20),name="globals")(pos,x,vecs,*ffw)

def globals_bwd(me,pos,x,mg,p,u,y,q,rows,ffw,vecs,count,n):
    length,width=x.shape; shard=width//n; half=max(n//2,1); w=len(ffw); cols=width//2
    def body(me_ref,pos_ref,x_ref,mg_ref,p_ref,u_ref,y_ref,q_ref,r_ref,vec_ref,*refs):
        ins=refs[:w]; f_ref,g_ref,keep,send,vg_ref,wts,res,keep_v,send_v,sems=refs[w:]
        m=me_ref[0]
        cps=[plane_copies(ins,j,wts.at[j],sems,j*n) for j in range(3)]
        for j in (2,1,0):
            for c in cps[j]: c.start()
        own=own_mask(width)
        hot=one_hot(pos_ref[...],length)
        sel=hot.astype(BF)
        x=x_ref[...]
        cs=scatter_heads(dot_nn(sel,mg_ref[...]).astype(BF),own,count)
        qs=scatter_heads(q_ref[...],own,count)
        for c in cps[2]: c.wait()
        v=dot_nt(cs,wts[2]).astype(BF)
        shift=dot_nt(jnp.broadcast_to(vec_ref[3:4,:],(16,width)).astype(BF),cs)[0:1,:]
        dp=dot_nt(x,v)+shift
        p=p_ref[...]
        low=p.astype(BF)
        ds=(p*(dp-jnp.sum(p*dp,axis=0,keepdims=True))).astype(BF)
        a=dot_tn(ds,x).astype(BF)
        for c in cps[1]: c.wait()
        pre=(gather_heads(dot_nn(a,wts[1]),own,count).astype(BF).astype(F32)*(HEAD_DIM**-0.5)).astype(BF)
        for c in cps[0]: c.wait()
        rows_grad=dot_nt(pre,wts[0])
        mass=dot_tn(low,jnp.ones((length,128),BF))[:,0:1]
        vg_ref[...]=jnp.zeros_like(vg_ref)
        vg_ref[2:3,:]=jnp.sum(pre.astype(F32),axis=0,keepdims=True)
        vg_ref[3:4,:]=jnp.sum(mass*cs.astype(F32),axis=0,keepdims=True)
        wide=16*count
        twice=jnp.concatenate([pos_ref[...],pos_ref[...],jnp.full((96,1),-1,jnp.int32)],axis=0)
        hots=jnp.where(lax.broadcasted_iota(jnp.int32,(128,length),1)==twice,1.0,0.0)
        high=rows_grad.astype(BF)
        f_ref[:,0:wide]=ds; f_ref[:,wide:2*wide]=low; f_ref[:,2*wide:2*wide+128]=hots.T.astype(BF)
        g_ref[...]=jnp.zeros_like(g_ref)
        g_ref[0:wide,:]=u_ref[...]; g_ref[wide:2*wide,:]=v
        g_ref[2*wide:2*wide+16,:]=high; g_ref[2*wide+16:2*wide+32,:]=(rows_grad-high.astype(F32)).astype(BF)
        for j,(l,r) in enumerate(((r_ref[...],pre),(a,qs),(y_ref[...],cs))):
            res[...]=dot_tn(l,r)
            for slot in range(n):
                for h in range(2):
                    part=res[pl.ds(pl.multiple_of((m^slot)*shard,shard),shard),h*cols:(h+1)*cols]
                    (send_v if slot%2 else keep_v)[slot//2,(2*j+h)*shard:(2*j+h+1)*shard,:]=part.astype(BF)
        cps=[pltpu.make_async_copy(keep_v,keep,sems.at[3*n])]
        if n>1: cps.append(pltpu.make_async_copy(send_v,send,sems.at[3*n+1]))
        for c in cps: c.start()
        for c in cps: c.wait()
    vm=pl.BlockSpec(memory_space=pltpu.VMEM)
    o=S((half,6*shard,cols),BF)
    return pl.pallas_call(body,in_specs=[SMEM]+[vm]*9+[ANY]*w,out_specs=[vm,vm,ANY,ANY,vm],
        out_shape=[S((length,32*count+128),BF),S((32*count+128,width),BF),o,o,S((16,width),F32)],
        scratch_shapes=[pltpu.VMEM((3,width,width),BF),pltpu.VMEM((width,width),F32),pltpu.VMEM((half,6*shard,cols),BF),pltpu.VMEM((half,6*shard,cols),BF),pltpu.SemaphoreType.DMA((3*n+2,))],
        compiler_params=params(),cost_estimate=cost(COST,1<<20),name="globals_back")(me,pos,x,mg,p,u,y,q,rows,vecs,*ffw)


def inputs_back(me,mez,gs,glob,groups,pieces):
    length,width=gs.shape; n=len(pieces); shard=width//n; g=len(groups); cols=width//g
    steps=length//RB
    def body(me_ref,mez_ref,gs_ref,f_ref,g_ref,*refs):
        parts=refs[:3*g]; ins=refs[3*g:3*g+n]; chunks=refs[3*g+n:3*g+n+steps]; vg_ref,wts,sems=refs[3*g+n+steps:]
        m=me_ref[0]
        @pl.when(pl.program_id(0)==0)
        def _():
            cps=sum([fetches(ins,wts.at[j],sems,m,j*shard,shard,j*n) for j in range(3)],[])
            for c in cps: c.start()
            vg_ref[...]=jnp.zeros_like(vg_ref)
            for c in cps: c.wait()
        acc=gs_ref[...]+dot_nn(f_ref[...],g_ref[...])
        for j in range(g):
            a=j*cols
            for w in range(3): acc=acc+dot_nt(parts[3*j+w][...],wts[w,:,a:a+cols])
            vg_ref[0:1,a:a+cols]+=jnp.sum(parts[3*j][...].astype(F32),axis=0,keepdims=True)
            vg_ref[1:2,a:a+cols]+=jnp.sum(parts[3*j+2][...].astype(F32),axis=0,keepdims=True)
        chunk_store(chunks,mez_ref[0],acc.astype(BF))
    blk=pl.BlockSpec((RB,width),lambda i:(i,0))
    part=pl.BlockSpec((RB,cols),lambda i:(i,0))
    return pl.pallas_call(body,grid=(length//RB,),in_specs=[SMEM,SMEM,blk,pl.BlockSpec((RB,glob[0].shape[1]),lambda i:(i,0)),pl.BlockSpec(glob[1].shape,lambda i:(0,0))]+[part]*(3*g)+[ANY]*n,
        out_specs=[pl.BlockSpec((RB,width),lambda i:(0,0))]*steps+[pl.BlockSpec((16,width),lambda i:(0,0))],out_shape=[S((RB,width),BF)]*steps+[S((16,width),F32)],
        scratch_shapes=[pltpu.VMEM((3,width,width),BF),pltpu.SemaphoreType.DMA((3*n,))],
        compiler_params=params(),cost_estimate=cost(COST,1<<20),name="inputs_back")(me,mez,gs,*glob,*[p for t in groups for p in t],*pieces)


def flip(value, axis, bit):
    count = lax.axis_size(axis)
    return lax.ppermute(value, axis, [(index, index ^ bit) for index in range(count)])


def tie(value, *others):
    return lax.optimization_barrier((value,) + others)[0]


def spread_slots(unit, order):
    slots = {0: unit}
    for bit in order:
        for slot in list(slots):
            slots[slot | bit] = flip(slots[slot], "fsdp", bit)
    return [slots[slot] for slot in range(len(slots))]


def add(one, two):
    return one.astype(F32) + two.astype(F32)


def meet(values, parts, *others):
    flat = [list(part.got) if isinstance(part.got, list) else [part.got] for part in parts]
    joined = tuple(values) + tuple(got for gots in flat for got in gots) + others
    joined = list(lax.optimization_barrier(joined))
    values = [joined.pop(0) for _ in values]
    for part, gots in zip(parts, flat):
        new = [joined.pop(0) for _ in gots]
        part.got = new if isinstance(part.got, list) else new[0]
    return values


class Held:
    def __init__(self, got):
        self.got = got


class Exchange:
    def __init__(self, chunks):
        self.got = [chunks[0]] + [flip(chunks[k], "sp", k) for k in range(1, len(chunks))]


class Reduction:
    def __init__(self, keep, send, x_first):
        self.keep, self.first, self.step = keep, send, 0
        self.got = flip(send, "fsdp", 1)
        self.x_first = x_first

    def advance(self, *gates):
        got = tie(self.got, *gates)
        x_now = self.x_first == (self.step == 0)
        if self.step == 0:
            keep = self.keep.reshape((2, 2) + self.keep.shape[1:])
            got = got.reshape(keep.shape)
            if self.x_first:
                away, here = (keep[:, 1], got[:, 1]), (keep[:, 0], got[:, 0])
            else:
                away, here = (keep[1], got[1]), (keep[0], got[0])
        else:
            away, here = (self.mine[1], got[1]), (self.mine[0], got[0])
        self.send, self.mine = add(*away).astype(BF), add(*here)
        self.got = flip(self.send, "fsdp", 2 if x_now else 4)
        self.step += 1
        return self.send

    def total(self):
        return add(self.mine, self.got)


class SpSum:
    def __init__(self, value, start=True):
        self.low, self.high = lax.axis_index("sp") & 1, lax.axis_index("sp") >> 1
        rows = value.shape[0] // 4
        self.shape = value.shape
        self.value = value.reshape(2, 2, rows, value.shape[1])
        self.got = self.value
        self.step = 0
        if start:
            self.start()

    def start(self):
        self.value = self.got
        self.exchange(self.low, 1)

    def exchange(self, mine, bit):
        send = lax.dynamic_index_in_dim(self.value, 1 - mine, 0, keepdims=False).astype(BF)
        self.value = lax.dynamic_index_in_dim(self.value, mine, 0, keepdims=False)
        self.send, self.got = send, flip(send, "sp", bit)

    def join(self, mine):
        return jnp.stack(
            [jnp.where(mine == 0, self.value, self.got), jnp.where(mine == 0, self.got, self.value)]
        )

    def advance(self):
        if self.step == 0:
            self.value = add(self.value, self.got)
            self.exchange(self.high, 2)
        elif self.step == 1:
            self.value = add(self.value, self.got).astype(BF)
            self.got = flip(self.value, "sp", 2)
        else:
            self.value = self.join(self.high)
            self.got = flip(self.value, "sp", 1)
        self.step += 1

    def total(self):
        return self.join(self.low).reshape(self.shape).astype(F32)


def per_device(
    inputs,
    global_pos,
    w_local,
    w_global,
    w_out,
    b_proj,
    gains,
    shifts,
    w_in,
    c_in,
    w_back,
    cotangent,
):
    sp_count = lax.axis_size("sp")
    fsdp_count = lax.axis_size("fsdp")
    sp_index = lax.axis_index("sp")
    fsdp_index = lax.axis_index("fsdp")
    own_seqs = inputs.shape[0] // sp_count
    glob_count = global_pos.shape[1]
    shard, width = w_out.shape
    ff_shard = w_back.shape[0]
    ff_width = w_in.shape[1]
    tree = fsdp_count == 8 and sp_count == 4 and own_seqs == 1 and shard % 32 == 0
    tree = tree and inputs.shape[1] == RB

    def to_sequence(value):
        if own_seqs == 1:
            moved = lax.all_to_all(value, "sp", split_axis=0, concat_axis=0)
            return moved.reshape(1, -1, width)
        return lax.all_to_all(value, "sp", split_axis=0, concat_axis=1, tiled=True)

    def to_tokens(values):
        if own_seqs == 1:
            return lax.all_to_all(
                values[0].reshape(sp_count, -1, width), "sp", split_axis=0, concat_axis=0
            )
        return lax.all_to_all(jnp.stack(values), "sp", split_axis=1, concat_axis=0, tiled=True)

    own_pos = lax.dynamic_slice_in_dim(global_pos, sp_index * own_seqs, own_seqs, 0)
    blocks = ff_width // width
    x_all = to_sequence(inputs)
    vec_rows = [b_proj, gains, shifts, c_in.reshape(-1, shard)]
    small = jnp.concatenate(vec_rows, axis=0)
    small = jnp.pad(small, ((0, 16 - small.shape[0]), (0, 0)))
    if tree:
        me = fsdp_index.reshape(1).astype(jnp.int32)
        mez = sp_index.reshape(1).astype(jnp.int32)
        first = jnp.concatenate(
            [w_local.reshape(-1, width), jnp.pad(small, ((0, 0), (0, width - shard)))], axis=0
        )
        local_w = spread_slots(first, (2, 4, 1))
        pack = jnp.concatenate(
            [
                w_in.reshape(shard, blocks, width).transpose(1, 0, 2).reshape(-1, width),
                w_back,
                w_global.reshape(-1, width),
                w_out,
            ],
            axis=0,
        )
        ffw = [lax.all_gather(pack, "fsdp")]
        small_all = jnp.stack([piece[3 * shard :, :shard] for piece in local_w])
        small_all = small_all[me[0] ^ jnp.arange(fsdp_count, dtype=jnp.int32)]
    else:
        me = mez = jnp.zeros((1,), jnp.int32)
        local_w = [lax.all_gather(w_local, "fsdp", axis=1, tiled=True).reshape(-1, width)]
        full_global = lax.all_gather(w_global, "fsdp", axis=1, tiled=True).reshape(-1, width)
        full_out = lax.all_gather(w_out, "fsdp", axis=0, tiled=True)
        ffw = [lax.all_gather(value, "fsdp", axis=0, tiled=True) for value in (w_in, w_back)]
        ffw.append(jnp.concatenate([full_global, full_out], axis=0))
        small_all = lax.all_gather(small, "fsdp")
    count = len(local_w)
    up_all = to_sequence(tie(cotangent, x_all))
    vecs = small_all.transpose(1, 0, 2).reshape(16, width).astype(F32)
    c_rows = small_all[:, 10 : 10 + ff_shard // shard].astype(F32)
    c_row = c_rows.reshape(1, ff_width)

    outs, input_grads, totals = [], [], None
    for index in range(own_seqs):
        x = x_all[index]
        pos = jnp.full((16, 1), -1, jnp.int32).at[:glob_count, 0].set(own_pos[index])
        q, k, v = project(me, x, local_w, vecs)
        ctx, lse = attn_fwd(pos, q, k, v)
        ctx_glob, probs, keys, mixed, query, rows = globals_fwd(
            pos, x, ffw, vecs, glob_count, count
        )
        *out, grad_sum, merged_grad, vec_one, c_grad, ff_pack, keep_two, send_two = layer(
            me, mez, pos, ctx, ctx_glob, x, up_all[index], ffw, vecs, c_row, count,
            3 * shard if tree else 0,
        )
        if tree:
            out_moved = Exchange(out)
            out_two, out_rest = Held(out_moved.got[2]), Held(out_moved.got[1::2])
        else:
            outs.append(jnp.concatenate(out, axis=0))
        if tree:
            ff_mine = lax.psum_scatter(ff_pack, "fsdp", scatter_dimension=0, tiled=False)
            merged_grad = tie(merged_grad, ff_pack)
        *glob, keep_one, send_one, vec_two = globals_bwd(
            me, pos, x, merged_grad, probs, keys, mixed, query, rows, ffw, vecs, glob_count, count
        )
        group_pairs = width // 128 // GROUPS
        groups = []
        if tree:
            one = Reduction(keep_one, send_one, True)
            merged_grad = tie(merged_grad, send_one)
        for group in range(GROUPS):
            parts = attn_bwd(
                pos, q, k, v, merged_grad, ctx, lse, group * group_pairs, group_pairs
            )
            groups.append(parts)
            if tree and group == 0:
                two = Reduction(*local_grads(me, x, parts, unit=(keep_two, send_two)), False)
                (merged_grad,) = meet([merged_grad], [out_two], two.first)
        if tree:
            (grad_sum,) = meet([grad_sum], [one, two, out_rest], parts[0])
            grad_sum = tie(grad_sum, one.advance(), two.advance())
        *input_grad, vec_three = inputs_back(me, mez, grad_sum, glob, groups, local_w)
        if tree:
            grads_moved = Exchange(input_grad)
        else:
            input_grads.append(jnp.concatenate(input_grad, axis=0))
        c_grad = c_grad.reshape(fsdp_count, -1, shard).transpose(1, 0, 2).reshape(-1, width)
        vec = vec_one + vec_two + vec_three + jnp.pad(c_grad, ((10, 6 - c_grad.shape[0]), (0, 0)))
        if not tree:
            g_in = ff_pack[0, :ff_width].reshape(blocks, width, width).transpose(1, 0, 2)
            g_in = g_in.reshape(width, ff_width).astype(F32)
            g_back = ff_pack[0, ff_width:].astype(F32)
            g_mixed = jnp.concatenate([keep_one[0], keep_two[0]], axis=0)
            g_mixed = g_mixed.reshape(4, 2, width, width // 2).transpose(0, 2, 1, 3)
            grads = (
                g_back,
                g_in,
                g_mixed.reshape(4, width, width).astype(F32),
                jnp.stack(
                    [
                        jnp.concatenate([dot_tn(x, part[w]) for part in groups], axis=1)
                        for w in range(3)
                    ]
                ),
                vec,
            )
            totals = grads if totals is None else tuple(a + b for a, b in zip(totals, grads))
    if tree:
        x_late, ff_mine = meet([x, ff_mine], [], *input_grad)
        ff_sum = SpSum(ff_mine.astype(F32))
        x_late = tie(x_late, ff_sum.send)
        late = Reduction(*local_grads(me, x_late, groups[-1], vec=vec), False)
        meet([], [one, two, ff_sum, grads_moved], late.first)
        one.advance()
        two.advance()
        ff_sum.advance()
        meet([], [late], one.send, two.send, ff_sum.send)
        late.advance()
        meet([], [one, two, late, ff_sum])
        early_sum = SpSum(jnp.concatenate([one.total(), two.total()], axis=0))
        late.advance()
        ff_sum.advance()
        near, far = out_rest.got
        out = collect(mez, [out_moved.got[0], near, out_two.got, far])
        meet([], [late, ff_sum, early_sum])
        late_sum = SpSum(late.total())
        early_sum.advance()
        ff_sum.advance()
        grad_inputs = collect(mez, grads_moved.got)
        meet([], [early_sum, late_sum, ff_sum])
        early_sum.advance()
        late_sum.advance()
        s_ff = ff_sum.total()
        meet([], [early_sum, late_sum])
        early_sum.advance()
        late_sum.advance()
        meet([], [early_sum, late_sum])
        late_sum.advance()
        s_early, s_late = early_sum.total(), late_sum.total()
        half_mixed = s_early[: 8 * shard].reshape(4, 2, shard, -1).transpose(0, 2, 1, 3)
        s_mixed = half_mixed.reshape(4, shard, width)
        s_local = jnp.concatenate(
            [
                s_early[8 * shard :].reshape(3, shard, -1),
                s_late[: 3 * shard].reshape(3, shard, -1),
            ],
            axis=2,
        )
        mine = s_late[3 * shard :, :shard]
        s_in = s_ff[: blocks * shard].reshape(blocks, shard, width).transpose(1, 0, 2)
        s_in = s_in.reshape(shard, ff_width)
        s_back = s_ff[blocks * shard :]
    else:
        out, grad_inputs = to_tokens(outs), to_tokens(input_grads)
        g_back, g_in, g_mixed, g_local, vec = totals

        def reduce(value, dim):
            mine = lax.psum_scatter(value.astype(BF), "fsdp", scatter_dimension=dim, tiled=True)
            return lax.psum(mine, "sp").astype(F32)

        s_back, s_in = reduce(g_back, 0), reduce(g_in, 0)
        s_mixed = reduce(g_mixed, 1)
        s_local = reduce(g_local, 1)
        vec = lax.psum(vec, ("fsdp", "sp"))
        mine = lax.dynamic_slice_in_dim(vec, fsdp_index * shard, shard, 1)
    c_mine = mine[10 : 10 + ff_shard // shard].reshape(-1)
    return (
        out,
        grad_inputs,
        s_local,
        s_mixed[:3],
        s_mixed[3],
        mine[:6],
        mine[6:8],
        mine[8:10],
        s_in,
        c_mine,
        s_back,
    )


def solution(mesh):
    rows = P("fsdp", None)
    tokens = P("fsdp", "sp", None)
    columns = P(None, "fsdp")
    stacked = P(None, "fsdp", None)
    return jax.shard_map(
        per_device,
        mesh=mesh,
        in_specs=(
            tokens,
            rows,
            stacked,
            stacked,
            rows,
            columns,
            columns,
            columns,
            rows,
            P("fsdp"),
            rows,
            tokens,
        ),
        out_specs=(
            tokens,
            tokens,
            stacked,
            stacked,
            rows,
            columns,
            columns,
            columns,
            rows,
            P("fsdp"),
            rows,
        ),
        check_vma=False,
    )
```
